256 devices in a mesh: space: 64 (over x, z, core), mode: 4 (over y).
Axes of the slice: x: 4, y: 4, z: 8, core: 2. Of those that a mesh axis runs over, the one named last changes fastest.
Arguments:
- modes_in: bfloat16 [120, 131072], P('mode', 'space'), may hold values from -6 to 6
- blocks: bfloat16 [5, 4608, 128, 128], P(None, 'space'), may hold values from -0.25 to 0.25
- block_cols: int32 [1152, 4], P('space'), may hold values from 0 to 15
- send_slot: int32 [16384], P('space'), may hold values from 0 to 511, as said below
- recv_row: int32 [32768], P('space'), may hold values from 0 to 2048, as said below
- mix_cols: int32 [5, 120, 8], replicated, may hold values from 0 to 120, as said below
- mix_coef: float32 [5, 120, 8], replicated, as said below
Outputs:
- first_apply: bfloat16 [120, 131072], P('mode', 'space')
- second_apply: bfloat16 [120, 131072], P('mode', 'space')
The draws below stay inside these ranges and needn't reach their ends.
Inputs may be any that keep to these rules, and one draw needn't show every extreme that they name: Interface row e of subdomain d goes to subdomain send_slot[d * 256 + e] // 8 at position send_slot[d * 256 + e] % 8. A subdomain's entries are distinct, and for each destination they fill positions from 0 upward, at most 8; one destination, the same for all subdomains, gets 8 rows from every subdomain. `recv_row`: entry o * 64 * 8 + d * 8 + p is the own degree of freedom of subdomain o at which position p from subdomain d is added; it is 2048 exactly where subdomain d sends fewer than p + 1 rows to o. Live entries may repeat. `mix_cols`: column 120 marks a padded slot. Each row of each term has from 4 to 8 live slots, both reached; live columns may repeat. `mix_coef`: zero exactly on padded slots.
All inputs are finite; a program needn't handle non-finite values.
Results may differ from the reference program's by a relative error of at most 0.022.
Values may be sent and summed in bfloat16 or wider, within the bound.
No kernel may reach another device: no remote copies, remote signals or barrier semaphores. Data moves between devices by JAX's collectives and lax.ppermute only.
A program may use at most 64 MiB of HBM per device.

```python
import jax
import jax.numpy as jnp
from jax import lax

P_SIZE = 120
TERMS = 5
BLK = 128
NZ_ROW = 4
NNZ_C = 8
B_DEV = 16
OUT_BLOCKS = 18
D_OWN = 2048
IF_DEV = 256
CAP = 8
N_DOF = 131072
N_SPACE = 64


def pair_counts(key):
    count_key = jax.random.fold_in(key, 11)
    half_cap = CAP // 2
    offsets = jax.random.randint(jax.random.fold_in(count_key, 1), (N_SPACE, N_SPACE // 2), -half_cap, half_cap + 1)
    chosen = jax.random.randint(jax.random.fold_in(count_key, 2), (), 0, N_SPACE // 2)
    side_bit = jax.random.randint(jax.random.fold_in(count_key, 3), (), 0, 2)
    pair_ids = jnp.arange(N_SPACE // 2)
    forced = half_cap - 2 * half_cap * side_bit
    offsets = jnp.where(pair_ids[None, :] == chosen, forced, offsets)
    return jnp.stack([half_cap + offsets, half_cap - offsets], axis=-1).reshape(N_SPACE, N_SPACE)


def draw_send_slot(key, part):
    counts = pair_counts(key)
    slot_ids = jnp.arange(N_SPACE * CAP)
    position = slot_ids % CAP
    target_dev = slot_ids // CAP
    valid_slot = position[None, :] < counts[:, target_dev]
    order_keys = jnp.where(valid_slot, slot_ids[None, :], slot_ids[None, :] + N_SPACE * CAP)
    ordered = jnp.sort(order_keys, axis=1)[:, :IF_DEV]
    perm_keys = jax.random.split(jax.random.fold_in(key, 12), N_SPACE)
    shuffled = jax.vmap(lambda one_key, slot_row: jax.random.permutation(one_key, slot_row))(perm_keys, ordered)
    return shuffled.reshape(-1).astype(jnp.int32)


def draw_recv_row(key, part):
    counts = pair_counts(key)
    targets = jax.random.randint(jax.random.fold_in(key, 13), (N_SPACE, N_SPACE, CAP), 0, D_OWN)
    live_slot = jnp.arange(CAP)[None, None, :] < counts.T[:, :, None]
    return jnp.where(live_slot, targets, D_OWN).reshape(-1).astype(jnp.int32)


def chaos_live(key):
    live_key = jax.random.fold_in(key, 21)
    live_counts = jax.random.randint(live_key, (TERMS, P_SIZE), NNZ_C // 2, NNZ_C + 1)
    row_ids = jnp.arange(P_SIZE)
    live_counts = jnp.where(row_ids[None, :] % 3 == 0, NNZ_C, live_counts)
    live_counts = jnp.where(row_ids[None, :] % 3 == 1, NNZ_C // 2, live_counts)
    return jnp.arange(NNZ_C)[None, None, :] < live_counts[:, :, None]


def draw_mix_cols(key, part):
    live_slot = chaos_live(key)
    picks = jax.random.randint(jax.random.fold_in(key, 22), (TERMS, P_SIZE, NNZ_C), 0, P_SIZE)
    picks = picks.at[0, :, 0].set(jnp.arange(P_SIZE))
    return jnp.where(live_slot, picks, P_SIZE).astype(jnp.int32)


def draw_mix_coef(key, part):
    live_slot = chaos_live(key)
    sign_key = jax.random.fold_in(key, 23)
    size_key = jax.random.fold_in(key, 24)
    signs = jnp.where(jax.random.bernoulli(sign_key, 0.5, (TERMS, P_SIZE, NNZ_C)), 1.0, -1.0)
    magnitude = jax.random.uniform(size_key, (TERMS, P_SIZE, NNZ_C), jnp.float32, 0.5, 1.5)
    scaled = signs * magnitude / jnp.sqrt(0.75 * TERMS * NNZ_C)
    return jnp.where(live_slot, scaled, 0.0).astype(jnp.float32)


def place_ends(result, stream_key, least, largest):
    index_at = [jax.random.randint(jax.random.fold_in(stream_key, axis), (), 0, length) for axis, length in enumerate(result.shape)]
    widest = result.shape.index(max(result.shape))
    beside = index_at[:widest] + [(index_at[widest] + 1) % result.shape[widest]] + index_at[widest + 1:]
    return result.at[tuple(index_at)].set(least).at[tuple(beside)].set(largest)


def level_of(stream_key, shape, pieces, smallest, top_value):
    loudness = 1.0
    for axis_at, shards_of in pieces:
        steps = jax.random.uniform(jax.random.fold_in(jax.random.fold_in(stream_key, 6), axis_at), (shards_of,), jnp.float32, smallest / len(pieces), top_value / len(pieces))
        loudness = loudness * jnp.repeat(jnp.exp(steps), shape[axis_at] // shards_of).reshape((-1,) + (1,) * (len(shape) - 1 - axis_at))
    return loudness


def centred(own_key, shape, width, most, shards=(), kind=jnp.bfloat16):
    values = width * jax.random.normal(own_key, shape, jnp.float32)
    if shards:
        values = values * level_of(own_key, shape, shards, -0.22, 0.18)
    return jnp.clip(values, -most, most).astype(kind)


def setup_inputs(seed: int = 0) -> dict:
    key_list = jax.random.split(jax.random.key(seed), 8)
    modes_in = centred(key_list[0], (P_SIZE, N_DOF), 1.0, 6.0, ((0, 4), (1, 64)))
    blocks = centred(key_list[1], (TERMS, N_SPACE * OUT_BLOCKS * NZ_ROW, BLK, BLK), (NZ_ROW * BLK) ** -0.5, 0.25, ((1, 64),))
    block_cols = place_ends(jax.random.randint(key_list[2], (N_SPACE * OUT_BLOCKS, NZ_ROW), 0, B_DEV), jax.random.fold_in(key_list[2], 1), 0, B_DEV - 1).astype(jnp.int32)
    send_slot = draw_send_slot(jax.random.fold_in(key_list[7], 71), 0)
    recv_row = draw_recv_row(jax.random.fold_in(key_list[7], 71), 0)
    mix_cols = draw_mix_cols(jax.random.fold_in(key_list[7], 71), 0)
    mix_coef = draw_mix_coef(jax.random.fold_in(key_list[7], 71), 0)
    return {"modes_in": modes_in, "blocks": blocks, "block_cols": block_cols, "send_slot": send_slot, "recv_row": recv_row, "mix_cols": mix_cols, "mix_coef": mix_coef}


def dense_mixer(mix_cols, mix_coef):
    columns = jnp.arange(P_SIZE, dtype=jnp.int32)
    onehot_table = (mix_cols[..., None] == columns).astype(jnp.float32)
    return jnp.sum(mix_coef[..., None] * onehot_table, axis=2).astype(jnp.bfloat16)


def device_products(operands):
    field_dev, stiff_dev, cols_dev = operands
    picked = field_dev[:, :, cols_dev, :].astype(jnp.float32)
    return jnp.einsum('kmcnd,kcnde->mce', picked, stiff_dev.astype(jnp.float32))


def reference(modes_in, blocks, block_cols, send_slot, recv_row, mix_cols, mix_coef):
    chaos_mixer = dense_mixer(mix_cols, mix_coef)
    stiffness = blocks.reshape(TERMS, N_SPACE, OUT_BLOCKS, NZ_ROW, BLK, BLK).transpose(1, 0, 2, 3, 4, 5)
    col_lists = block_cols.reshape(N_SPACE, OUT_BLOCKS, NZ_ROW)
    slot_lists = send_slot.reshape(N_SPACE, IF_DEV)
    recv_lists = recv_row.reshape(N_SPACE, N_SPACE * CAP)
    dest_dev = (slot_lists // CAP).astype(jnp.int32)
    slot_pos = (slot_lists % CAP).astype(jnp.int32)
    source_dev = jnp.arange(N_SPACE, dtype=jnp.int32)[:, None]
    target_row = recv_lists[dest_dev, source_dev * CAP + slot_pos]
    global_row = jnp.where(target_row < D_OWN, dest_dev * D_OWN + target_row, N_DOF).reshape(-1).astype(jnp.int32)

    def one_apply(field_now):
        mixed_field = jnp.einsum('kij,jn->kin', chaos_mixer.astype(jnp.float32), field_now.astype(jnp.float32)).astype(jnp.bfloat16)
        per_device = mixed_field.reshape(TERMS, P_SIZE, N_SPACE, B_DEV, BLK).transpose(2, 0, 1, 3, 4)
        products = lax.map(device_products, (per_device, stiffness, col_lists))
        flat_rows = products.reshape(N_SPACE, P_SIZE, OUT_BLOCKS * BLK)
        owned_part = flat_rows[:, :, :D_OWN].transpose(1, 0, 2).reshape(P_SIZE, N_DOF)
        interface = flat_rows[:, :, D_OWN:].transpose(1, 0, 2).reshape(P_SIZE, N_SPACE * IF_DEV)
        assembled = owned_part.at[:, global_row].add(interface, mode='drop')
        return assembled.astype(jnp.bfloat16)

    first_apply = one_apply(modes_in)
    second_apply = one_apply(first_apply)
    return (first_apply, second_apply)
```

```python
import functools

import jax
import jax.numpy as jnp
from jax import lax
from jax.experimental import pallas as pl
from jax.experimental.pallas import tpu as pltpu
from jax.sharding import PartitionSpec as P

LANES = 128
PAD = 32
QUARTERS = 4

VMEM = pl.BlockSpec(memory_space=pltpu.VMEM)
SMEM = pl.BlockSpec(memory_space=pltpu.SMEM)
ANY = pl.BlockSpec(memory_space=pl.ANY)
VMEM_LIMIT = 40 * 1024 * 1024


def call(kernel, outs, ins, in_specs, flops, scratch=(), grid=None, out_specs=None):
    out_bytes = sum(o.size * o.dtype.itemsize for o in outs)
    in_bytes = sum(a.size * a.dtype.itemsize for a in ins)
    extra = {} if grid is None else {"grid": grid}
    return pl.pallas_call(
        kernel,
        out_shape=outs,
        in_specs=in_specs,
        out_specs=out_specs or [VMEM] * len(outs),
        scratch_shapes=scratch,
        compiler_params=pltpu.CompilerParams(vmem_limit_bytes=VMEM_LIMIT),
        cost_estimate=pl.CostEstimate(flops=flops, bytes_accessed=in_bytes + out_bytes, transcendentals=0),
        **extra,
    )(*ins)


def one_hot(hit):
    return jnp.where(hit, 1.0, 0.0).astype(jnp.bfloat16)


def tables_kernel(cols_ref, coef_ref, send_ref, recv_ref, recv2_ref, g_ref, s_ref, s2_ref, r_ref, r2_ref):
    lanes = lax.broadcasted_iota(jnp.int32, g_ref.shape, 1)
    total = jnp.zeros(g_ref.shape, jnp.float32)
    for slot in range(cols_ref.shape[1]):
        total += jnp.where(cols_ref[:, slot:slot + 1] == lanes, coef_ref[:, slot:slot + 1], 0.0)
    g_ref[...] = total.astype(jnp.bfloat16)
    send = send_ref[...]
    s_ref[...] = one_hot(send == lax.broadcasted_iota(jnp.int32, s_ref.shape, 0))
    width = send.shape[1]
    rows = lax.broadcasted_iota(jnp.int32, (s2_ref.shape[0], width), 0)
    for quarter in range(QUARTERS):
        s2_ref[:, quarter * width:(quarter + 1) * width] = one_hot(send == rows * QUARTERS + quarter)
    for table, recv in ((r_ref, recv_ref), (r2_ref, recv2_ref)):
        wanted = recv[...]
        step = 256
        for at in range(0, table.shape[1], step):
            target = lax.broadcasted_iota(jnp.int32, (table.shape[0], step), 1) + at
            table[:, at:at + step] = one_hot(wanted == target)


def block_row(row, rows, cols_ref, mixed_ref, stiff_ref, first):
    terms = stiff_ref.shape[0]
    stored = cols_ref.shape[1]
    total = None
    for term in range(terms):
        picked = jnp.concatenate(
            [mixed_ref[cols_ref[row, c], term * rows:(term + 1) * rows, :] for c in range(stored)], axis=1
        )
        stiff = stiff_ref[term, first:first + stored].reshape(stored * LANES, LANES)
        product = jnp.dot(picked, stiff, preferred_element_type=jnp.float32)
        total = product if total is None else total + product
    return total


def mix(mixer, field, mixed_ref, width=256):
    for at in range(0, field.shape[1], width):
        mixed = jnp.dot(mixer, field[:, at:at + width], preferred_element_type=jnp.float32).astype(jnp.bfloat16)
        for part in range(width // LANES):
            mixed_ref[at // LANES + part] = mixed[:, part * LANES:(part + 1) * LANES]


def interface_rows(rows, cols_ref, mixed_ref, stiff_ref):
    stored = cols_ref.shape[1]
    owned_blocks = mixed_ref.shape[0]
    parts = [
        block_row(row, rows, cols_ref, mixed_ref, stiff_ref, (row - owned_blocks) * stored)
        for row in range(owned_blocks, cols_ref.shape[0])
    ]
    return jnp.concatenate(parts, axis=1).astype(jnp.bfloat16)


def interface_copy(blocks_ref, stiff_ref, sem):
    count = stiff_ref.shape[1]
    return pltpu.make_async_copy(blocks_ref.at[:, pl.ds(blocks_ref.shape[1] - count, count)], stiff_ref, sem)


def first_kernel(v0, v1, v2, v3, g_ref, s_ref, cols_ref, blocks_ref, mixed_ref, packed_ref, field_ref, stiff_ref, sem):
    copy = interface_copy(blocks_ref, stiff_ref, sem)
    copy.start()
    field_ref[...] = jnp.zeros_like(field_ref)
    for slot, source in enumerate((v0, v1, v2, v3)):
        field_ref[slot * PAD:slot * PAD + source.shape[0], :] = source[...]
    mix(g_ref[...], field_ref, mixed_ref)
    copy.wait()
    rows = field_ref.shape[0]
    part = interface_rows(rows, cols_ref, mixed_ref, stiff_ref)
    packed = lax.dot_general(s_ref[...], part, (((1,), (1,)), ((), ())), preferred_element_type=jnp.float32)
    packed_ref[...] = packed.astype(jnp.bfloat16)


def own_kernel(per_step, cols_ref, mixed_ref, stiff_ref, own_ref):
    stored = cols_ref.shape[1]
    rows = own_ref.shape[0]
    step = pl.program_id(0)
    for part in range(per_step):
        own_ref[:, part * LANES:(part + 1) * LANES] = block_row(
            step * per_step + part, rows, cols_ref, mixed_ref, stiff_ref, part * stored
        )


def second_kernel(own_ref, arrived_ref, r_ref, g_ref, s2_ref, cols_ref, blocks_ref,
                  first_ref, mixed_ref, packed_ref, field_ref, spread_ref, stiff_ref, sem):
    copy = interface_copy(blocks_ref, stiff_ref, sem)
    copy.start()
    arrived = arrived_ref[...].astype(jnp.float32).T.astype(jnp.bfloat16)
    width = 256
    for at in range(0, own_ref.shape[1], width):
        added = jnp.dot(arrived, r_ref[:, at:at + width], preferred_element_type=jnp.float32)
        field_ref[:, at:at + width] = (own_ref[:, at:at + width] + added).astype(jnp.bfloat16)
    first_ref[...] = field_ref[:first_ref.shape[0], :]
    rows = own_ref.shape[0]
    terms = stiff_ref.shape[0]
    mixer = jnp.concatenate([g_ref[term * rows:term * rows + PAD, :] for term in range(terms)], axis=0)
    mix(mixer, field_ref, mixed_ref)
    spread_ref[...] = jnp.zeros_like(spread_ref)
    copy.wait()
    part = interface_rows(PAD, cols_ref, mixed_ref, stiff_ref)
    wide = part.shape[1]
    for quarter in range(QUARTERS):
        spread_ref[quarter * PAD:(quarter + 1) * PAD, quarter * wide:(quarter + 1) * wide] = part
    packed = lax.dot_general(s2_ref[...], spread_ref[...], (((1,), (1,)), ((), ())), preferred_element_type=jnp.float32)
    packed_ref[...] = packed.astype(jnp.bfloat16)


def last_kernel(own_ref, arrived_ref, r2_ref, out_ref):
    turned = arrived_ref[...].astype(jnp.float32).T.astype(jnp.bfloat16)
    arrived = jnp.concatenate([turned[quarter * PAD:(quarter + 1) * PAD, :] for quarter in range(QUARTERS)], axis=1)
    width = 256
    for at in range(0, own_ref.shape[1], width):
        added = jnp.dot(arrived, r2_ref[:, at:at + width], preferred_element_type=jnp.float32)
        total = (own_ref[:, at:at + width] + added).astype(jnp.bfloat16)
        out_ref[:, at:at + width] = total[:out_ref.shape[0], :]


def local(groups, peers, modes_in, blocks, block_cols, send_slot, recv_row, mix_cols, mix_coef):
    bf16, f32 = jnp.bfloat16, jnp.float32
    terms, all_stored, blk, _ = blocks.shape
    out_blocks, stored = block_cols.shape
    modes_dev, owned = modes_in.shape
    modes = groups * modes_dev
    owned_blocks = owned // blk
    interface = send_slot.shape[0]
    slots = recv_row.shape[0]
    cap = slots // peers
    rows = groups * PAD
    me = lax.axis_index("mode")
    Shape = jax.ShapeDtypeStruct

    others = [
        lax.ppermute(modes_in, "mode", [((to + s) % groups, to) for to in range(groups)])
        for s in (2, 1, 3)
    ]
    fields = [modes_in, others[1], others[0], others[2]]

    def own_first(table, fill):
        split = table.reshape(terms, groups, modes_dev, table.shape[-1])
        turned = lax.dynamic_slice_in_dim(jnp.concatenate([split, split], axis=1), me, groups, axis=1)
        padded = jnp.pad(turned, ((0, 0), (0, 0), (0, PAD - modes_dev), (0, 0)), constant_values=fill)
        return padded.reshape(terms * rows, table.shape[-1])

    place = (mix_cols // modes_dev - me + groups) % groups * PAD + mix_cols % modes_dev
    place = jnp.where(mix_cols < modes, place, -1)
    halves = cap // QUARTERS
    recv2 = recv_row.reshape(peers, halves, QUARTERS).transpose(2, 0, 1).reshape(slots, 1)
    g, s, s2, r, r2 = call(
        tables_kernel,
        [Shape((terms * rows, rows), bf16), Shape((slots, interface), bf16),
         Shape((slots // QUARTERS, QUARTERS * interface), bf16),
         Shape((slots, owned), bf16), Shape((slots, owned), bf16)],
        [own_first(place, -1), own_first(mix_coef, 0.0), send_slot.reshape(1, interface),
         recv_row.reshape(slots, 1), recv2],
        [VMEM] * 5, flops=10 * slots * owned,
    )
    if_stored = (out_blocks - owned_blocks) * stored
    stiff_scratch = pltpu.VMEM((terms, if_stored, blk, blk), bf16)
    mixed, packed = call(
        first_kernel,
        [Shape((owned_blocks, terms * rows, blk), bf16), Shape((slots, rows), bf16)],
        [*fields, g, s, block_cols, blocks],
        [VMEM] * 6 + [SMEM, ANY], flops=2 * terms * rows * rows * owned,
        scratch=[pltpu.VMEM((rows, owned), bf16), stiff_scratch, pltpu.SemaphoreType.DMA],
    )
    arrived = lax.all_to_all(packed.reshape(peers, cap, rows), "space", split_axis=0, concat_axis=0, tiled=True)

    def own_rows(mixed_field, count):
        per_step = 2
        return call(
            functools.partial(own_kernel, per_step),
            [Shape((count, owned), f32)], [block_cols, mixed_field, blocks],
            [SMEM, VMEM, pl.BlockSpec((terms, per_step * stored, blk, blk), lambda i: (0, i, 0, 0))],
            flops=2 * terms * stored * owned_blocks * count * blk * blk,
            grid=(owned_blocks // per_step,),
            out_specs=[pl.BlockSpec((count, per_step * blk), lambda i: (0, i))],
        )[0]

    own = own_rows(mixed, rows)
    first_apply, mixed2, packed2 = call(
        second_kernel,
        [Shape((modes_dev, owned), bf16), Shape((owned_blocks, terms * PAD, blk), bf16),
         Shape((slots // QUARTERS, QUARTERS * PAD), bf16)],
        [own, arrived.reshape(slots, rows), r, g, s2, block_cols, blocks],
        [VMEM] * 5 + [SMEM, ANY], flops=2 * slots * rows * owned,
        scratch=[pltpu.VMEM((rows, owned), bf16), pltpu.VMEM((QUARTERS * PAD, QUARTERS * interface), bf16),
                 stiff_scratch, pltpu.SemaphoreType.DMA],
    )
    arrived2 = lax.all_to_all(
        packed2.reshape(peers, halves, QUARTERS * PAD), "space", split_axis=0, concat_axis=0, tiled=True
    )
    own2 = own_rows(mixed2, PAD)
    second_apply = call(
        last_kernel, [Shape((modes_dev, owned), bf16)],
        [own2, arrived2.reshape(slots // QUARTERS, QUARTERS * PAD), r2],
        [VMEM] * 3, flops=2 * slots * PAD * owned,
    )[0]
    return (first_apply, second_apply)


def solution(mesh):
    in_specs = (
        P("mode", "space"),
        P(None, "space", None, None),
        P("space", None),
        P("space"),
        P("space"),
        P(),
        P(),
    )
    out_specs = (P("mode", "space"), P("mode", "space"))
    body = functools.partial(local, mesh.shape["mode"], mesh.shape["space"])
    return jax.shard_map(body, mesh=mesh, in_specs=in_specs, out_specs=out_specs, check_vma=False)
```

```python
import functools

import jax
import jax.numpy as jnp
from jax import lax
from jax.experimental import pallas as pl
from jax.experimental.pallas import tpu as pltpu
from jax.sharding import PartitionSpec as P

LANES = 128
PAD = 32
QUARTERS = 4
WIDTH = 256

VMEM = pl.BlockSpec(memory_space=pltpu.VMEM)
SMEM = pl.BlockSpec(memory_space=pltpu.SMEM)
HBM = pl.BlockSpec(memory_space=pltpu.HBM)
VMEM_LIMIT = 48 * 1024 * 1024
bf16, f32, i32 = jnp.bfloat16, jnp.float32, jnp.int32


def call(kernel, outs, ins, in_specs, out_specs, flops, scratch=()):
    moved = sum(a.size * a.dtype.itemsize for a in [*outs, *ins])
    return pl.pallas_call(
        kernel,
        out_shape=outs,
        in_specs=in_specs,
        out_specs=out_specs,
        scratch_shapes=scratch,
        compiler_params=pltpu.CompilerParams(vmem_limit_bytes=VMEM_LIMIT),
        cost_estimate=pl.CostEstimate(flops=flops, bytes_accessed=moved, transcendentals=0),
    )(*ins)


def one_hot(hit):
    return jnp.where(hit, 1.0, 0.0).astype(bf16)


def dot(a, b):
    return jnp.dot(a, b, preferred_element_type=f32)


def dot_t(a, b):
    return lax.dot_general(a, b, (((1,), (1,)), ((), ())), preferred_element_type=f32)


def padded_place(modes, groups, modes_dev):
    place = modes
    for group in range(1, groups):
        place += jnp.where(modes >= group * modes_dev, PAD - modes_dev, 0)
    return place


def mixer_columns(term, groups, cols_ref, coef_ref):
    modes = cols_ref.shape[2]
    cols = cols_ref[term]
    place = jnp.where(cols < modes, padded_place(cols, groups, modes // groups), -1)
    coef = coef_ref[term]
    want = lax.broadcasted_iota(i32, (groups * PAD, modes), 0)
    total = jnp.zeros(want.shape, f32)
    for slot in range(cols.shape[0]):
        total += jnp.where(place[slot:slot + 1, :] == want, coef[slot:slot + 1, :], 0.0)
    return total.astype(bf16)


def mixer_kernel(groups, cols_ref, coef_ref, g_ref):
    modes = cols_ref.shape[2]
    rows = groups * PAD
    out_mode = lax.broadcasted_iota(i32, (rows, modes), 1)
    spread = one_hot(padded_place(out_mode, groups, modes // groups) == lax.broadcasted_iota(i32, (rows, modes), 0))
    for term in range(cols_ref.shape[0]):
        g_ref[term * rows:(term + 1) * rows, :] = dot_t(spread, mixer_columns(term, groups, cols_ref, coef_ref)).astype(bf16)


def receive_table(recv_ref, r_ref):
    slots = recv_ref.shape[1]
    turned = jnp.broadcast_to(recv_ref[...].astype(f32), (LANES, slots)).T
    wanted = turned[:, :1].astype(i32)
    for at in range(0, r_ref.shape[1], WIDTH):
        r_ref[:, at:at + WIDTH] = one_hot(wanted == lax.broadcasted_iota(i32, (slots, WIDTH), 1) + at)


def block_row(row, rows, cols_ref, mixed_ref, stiff):
    terms, stored = stiff.shape[:2]
    picked = jnp.concatenate(
        [
            mixed_ref[cols_ref[c, row], term * rows:(term + 1) * rows, :]
            for term in range(terms)
            for c in range(stored)
        ],
        axis=1,
    )
    return dot(picked, stiff.reshape(terms * stored * LANES, LANES))


def mix(mixer, field_ref, mixed_ref):
    rows = field_ref.shape[0] * field_ref.shape[1]
    for at in range(0, field_ref.shape[2], WIDTH):
        field = field_ref[:, :, at:at + WIDTH].reshape(rows, WIDTH)
        mixed = dot(mixer, field).astype(bf16)
        for part in range(WIDTH // LANES):
            mixed_ref[at // LANES + part] = mixed[:, part * LANES:(part + 1) * LANES]


def first_kernel(groups, v0, v1, v2, v3, g_ref, send_ref, cols_ref, blocks_ref,
                 packed_ref, own_out, token_ref, field_ref, mixed_ref, own_ref, sems):
    me = lax.axis_index("mode")
    rows = groups * PAD
    stored, out_blocks = cols_ref.shape
    owned_blocks = mixed_ref.shape[0]
    field_ref[...] = jnp.zeros_like(field_ref)
    for slot, source in enumerate((v0, v1, v2, v3)):
        field_ref[lax.rem(me + slot, groups), :source.shape[0], :] = source[...]
    mix(g_ref[...], field_ref, mixed_ref)

    def row_of(row):
        return block_row(row, rows, cols_ref, mixed_ref, blocks_ref[:, row * stored:(row + 1) * stored])

    copies = []
    for row in range(owned_blocks):
        own_ref[:, row * LANES:(row + 1) * LANES] = row_of(row)
        if row % 4 == 3:
            at = pl.ds((row - 3) * LANES, 4 * LANES)
            copies.append(pltpu.make_async_copy(own_ref.at[:, at], own_out.at[:, at], sems.at[row // 4]))
            copies[-1].start()
    part = jnp.concatenate([row_of(row) for row in range(owned_blocks, out_blocks)], axis=1).astype(bf16)
    slots = packed_ref.shape[0]
    place = one_hot(send_ref[...] == lax.broadcasted_iota(i32, (slots, send_ref.shape[1]), 0))
    packed_ref[...] = dot_t(place, part).astype(bf16)
    token_ref[...] = jnp.zeros_like(token_ref)
    for copy in copies:
        copy.wait()


def between_kernel(groups, token_ref, cols_ref, coef_ref, recv_ref, r_ref, g2_ref):
    me = lax.axis_index("mode")
    modes = cols_ref.shape[2]
    modes_dev = modes // groups
    row = lax.broadcasted_iota(i32, (PAD, modes), 0)
    mine = one_hot((lax.broadcasted_iota(i32, (PAD, modes), 1) == row + me * modes_dev) & (row < modes_dev))
    for term in range(cols_ref.shape[0]):
        g2_ref[term * PAD:(term + 1) * PAD, :] = dot_t(mine, mixer_columns(term, groups, cols_ref, coef_ref)).astype(bf16)
    receive_table(recv_ref, r_ref)


def second_kernel(groups, own_ref, arrived_ref, r_ref, g2_ref, send_ref, cols_ref, blocks_ref,
                  first_ref, mixed_out, packed_ref, field_ref, mixed_ref, spread_ref, stiff_ref, sem, sems):
    me = lax.axis_index("mode")
    stored, out_blocks = cols_ref.shape
    owned_blocks = mixed_ref.shape[0]
    count = stiff_ref.shape[1]
    fetch = pltpu.make_async_copy(blocks_ref.at[:, pl.ds(owned_blocks * stored, count)], stiff_ref, sem)
    fetch.start()
    arrived = arrived_ref[...].astype(f32).T.astype(bf16)
    for at in range(0, own_ref.shape[1], WIDTH):
        total = own_ref[:, at:at + WIDTH] + dot(arrived, r_ref[:, at:at + WIDTH])
        field_ref[:, :, at:at + WIDTH] = total.astype(bf16).reshape(groups, PAD, WIDTH)
    first_ref[...] = field_ref[me, :first_ref.shape[0], :]
    mix(g2_ref[...], field_ref, mixed_ref)
    keep = pltpu.make_async_copy(mixed_ref, mixed_out, sems)
    keep.start()
    spread_ref[...] = jnp.zeros_like(spread_ref)
    width = send_ref.shape[1]
    send = send_ref[...]
    lines = lax.broadcasted_iota(i32, (packed_ref.shape[0], width), 0) * QUARTERS
    place = jnp.concatenate([one_hot(send == lines + quarter) for quarter in range(QUARTERS)], axis=1)
    fetch.wait()
    part = jnp.concatenate(
        [
            block_row(row, PAD, cols_ref, mixed_ref, stiff_ref[:, (row - owned_blocks) * stored:(row - owned_blocks + 1) * stored])
            for row in range(owned_blocks, out_blocks)
        ],
        axis=1,
    ).astype(bf16)
    for quarter in range(QUARTERS):
        spread_ref[quarter * PAD:(quarter + 1) * PAD, quarter * width:(quarter + 1) * width] = part
    packed_ref[...] = dot_t(place, spread_ref[...]).astype(bf16)
    keep.wait()


def own_kernel(steps, cols_ref, recv_ref, mixed_hbm, blocks_ref, own_ref, r_ref, mixed_ref, stiff_ref, sem, sems):
    stored = cols_ref.shape[0]
    owned_blocks = mixed_ref.shape[0]
    per = owned_blocks // steps
    fetch = pltpu.make_async_copy(mixed_hbm, mixed_ref, sem)
    fetch.start()
    copies = []
    for step in range(steps):
        at = pl.ds(step * per * stored, per * stored)
        copies.append(pltpu.make_async_copy(blocks_ref.at[:, at], stiff_ref.at[:, at], sems.at[step]))
        copies[-1].start()
    receive_table(recv_ref, r_ref)
    fetch.wait()
    for step in range(steps):
        copies[step].wait()
        for row in range(step * per, (step + 1) * per):
            own_ref[:, row * LANES:(row + 1) * LANES] = block_row(
                row, PAD, cols_ref, mixed_ref, stiff_ref[:, row * stored:(row + 1) * stored]
            )


def last_kernel(own_ref, arrived_ref, r_ref, out_ref, slots_ref):
    arrived = arrived_ref[...].astype(f32)
    lines = arrived.shape[0]
    for quarter in range(QUARTERS):
        turned = pltpu.roll(arrived, (QUARTERS - quarter) % QUARTERS * PAD, 1)
        slots_ref[pl.ds(quarter, lines, stride=QUARTERS), :] = turned
    by_slot = slots_ref[...].T[:PAD, :].astype(bf16)
    for at in range(0, own_ref.shape[1], WIDTH):
        total = own_ref[:, at:at + WIDTH] + dot(by_slot, r_ref[:, at:at + WIDTH])
        out_ref[:, at:at + WIDTH] = total.astype(bf16)[:out_ref.shape[0], :]


def local(groups, peers, modes_in, blocks, block_cols, send_slot, recv_row, mix_cols, mix_coef):
    terms, all_stored, blk, _ = blocks.shape
    out_blocks, stored = block_cols.shape
    modes_dev, owned = modes_in.shape
    owned_blocks = owned // blk
    interface = send_slot.shape[0]
    slots = recv_row.shape[0]
    cap = slots // peers
    rows = groups * PAD
    lines = slots // QUARTERS
    Shape = jax.ShapeDtypeStruct
    dma = pltpu.SemaphoreType.DMA

    others = {
        s: lax.ppermute(modes_in, "mode", [((to + s) % groups, to) for to in range(groups)])
        for s in (2, 1, 3)
    }
    fields = [modes_in, others[1], others[2], others[3]]
    cols_t = block_cols.T
    mix_cols_t, mix_coef_t = mix_cols.transpose(0, 2, 1), mix_coef.transpose(0, 2, 1)
    send, recv = send_slot.reshape(1, interface), recv_row.reshape(1, slots)

    g = call(
        functools.partial(mixer_kernel, groups), [Shape((terms * rows, rows), bf16)],
        [mix_cols_t, mix_coef_t], [VMEM] * 2, [VMEM], flops=10**6,
    )[0]
    field_scratch = pltpu.VMEM((groups, PAD, owned), bf16)
    packed, own, token = call(
        functools.partial(first_kernel, groups),
        [Shape((slots, rows), bf16), Shape((rows, owned), f32), Shape((8, LANES), f32)],
        [*fields, g, send, cols_t, blocks],
        [VMEM] * 6 + [SMEM, VMEM], [VMEM, HBM, VMEM],
        flops=2 * terms * stored * out_blocks * rows * blk * blk,
        scratch=[field_scratch, pltpu.VMEM((owned_blocks, terms * rows, blk), bf16),
                 pltpu.VMEM((rows, owned), f32), dma((owned_blocks // 4,))],
    )
    arrived = lax.all_to_all(packed.reshape(peers, cap, rows), "space", split_axis=0, concat_axis=0, tiled=True)
    r, g2 = call(
        functools.partial(between_kernel, groups), [Shape((slots, owned), bf16), Shape((terms * PAD, rows), bf16)],
        [token, mix_cols_t, mix_coef_t, recv], [VMEM] * 4, [VMEM] * 2, flops=10**9,
    )
    first_apply, mixed2, packed2 = call(
        functools.partial(second_kernel, groups),
        [Shape((modes_dev, owned), bf16), Shape((owned_blocks, terms * PAD, blk), bf16), Shape((lines, QUARTERS * PAD), bf16)],
        [own, arrived.reshape(slots, rows), r, g2, send, cols_t, blocks],
        [VMEM] * 5 + [SMEM, HBM], [VMEM, HBM, VMEM], flops=2 * slots * rows * owned,
        scratch=[field_scratch, pltpu.VMEM((owned_blocks, terms * PAD, blk), bf16),
                 pltpu.VMEM((QUARTERS * PAD, QUARTERS * interface), bf16),
                 pltpu.VMEM((terms, (out_blocks - owned_blocks) * stored, blk, blk), bf16), dma, dma],
    )
    arrived2 = lax.all_to_all(
        packed2.reshape(peers, cap // QUARTERS, QUARTERS * PAD), "space", split_axis=0, concat_axis=0, tiled=True
    )
    steps = 8
    own2, r2 = call(
        functools.partial(own_kernel, steps), [Shape((PAD, owned), f32), Shape((slots, owned), bf16)],
        [cols_t, recv, mixed2, blocks], [SMEM, VMEM, HBM, HBM], [VMEM] * 2,
        flops=2 * terms * stored * owned_blocks * PAD * blk * blk,
        scratch=[pltpu.VMEM((owned_blocks, terms * PAD, blk), bf16),
                 pltpu.VMEM((terms, owned_blocks * stored, blk, blk), bf16), dma, dma((steps,))],
    )
    second_apply = call(
        last_kernel, [Shape((modes_dev, owned), bf16)],
        [own2, arrived2.reshape(lines, QUARTERS * PAD), r2], [VMEM] * 3, [VMEM],
        flops=2 * slots * PAD * owned, scratch=[pltpu.VMEM((slots, QUARTERS * PAD), f32)],
    )[0]
    return (first_apply, second_apply)


def solution(mesh):
    in_specs = (
        P("mode", "space"),
        P(None, "space", None, None),
        P("space", None),
        P("space"),
        P("space"),
        P(),
        P(),
    )
    out_specs = (P("mode", "space"), P("mode", "space"))
    body = functools.partial(local, mesh.shape["mode"], mesh.shape["space"])
    return jax.shard_map(body, mesh=mesh, in_specs=in_specs, out_specs=out_specs, check_vma=False)
```

```python
import functools
import math

import jax
import jax.numpy as jnp
from jax import lax
from jax.experimental import pallas as pl
from jax.experimental.pallas import tpu as pltpu
from jax.sharding import PartitionSpec as P

LANES = 128
PAD = 32
QUARTERS = 4
WIDTH = 256

VMEM = pl.BlockSpec(memory_space=pltpu.VMEM)
SMEM = pl.BlockSpec(memory_space=pltpu.SMEM)
HBM = pl.BlockSpec(memory_space=pltpu.HBM)
VMEM_LIMIT = 32 * 1024 * 1024
bf16, f32, i32 = jnp.bfloat16, jnp.float32, jnp.int32


def call(kernel, outs, ins, in_specs, out_specs, flops, scratch=()):
    moved = sum(math.prod(a.shape) * jnp.dtype(a.dtype).itemsize for a in [*outs, *ins])
    return pl.pallas_call(
        kernel,
        out_shape=outs,
        in_specs=in_specs,
        out_specs=out_specs,
        scratch_shapes=scratch,
        compiler_params=pltpu.CompilerParams(vmem_limit_bytes=VMEM_LIMIT),
        cost_estimate=pl.CostEstimate(flops=flops, bytes_accessed=moved, transcendentals=0),
    )(*ins)


def begin(sems, *pairs):
    copies = [pltpu.make_async_copy(source, target, sems.at[at]) for at, (source, target) in enumerate(pairs)]
    for copy in copies:
        copy.start()
    return copies


def finish(copies):
    for copy in copies:
        copy.wait()


def one_hot(hit):
    return jnp.where(hit, 1.0, 0.0).astype(bf16)


def dot(a, b):
    return jnp.dot(a, b, preferred_element_type=f32)


def dot_t(a, b):
    return lax.dot_general(a, b, (((1,), (1,)), ((), ())), preferred_element_type=f32)


def padded_place(modes, groups, modes_dev):
    place = modes
    for group in range(1, groups):
        place += jnp.where(modes >= group * modes_dev, PAD - modes_dev, 0)
    return place


def mixer_columns(term, groups, cols_ref, coef_ref):
    modes = cols_ref.shape[2]
    cols = cols_ref[term]
    place = jnp.where(cols < modes, padded_place(cols, groups, modes // groups), -1)
    coef = coef_ref[term]
    want = lax.broadcasted_iota(i32, (groups * PAD, modes), 0)
    total = jnp.zeros(want.shape, f32)
    for slot in range(cols.shape[0]):
        total += jnp.where(place[slot:slot + 1, :] == want, coef[slot:slot + 1, :], 0.0)
    return total.astype(bf16)


def receive_table(recv_ref, r_ref):
    slots = recv_ref.shape[1]
    turned = jnp.broadcast_to(recv_ref[...].astype(f32), (LANES, slots)).T
    wanted = turned[:, :1].astype(i32)
    for at in range(0, r_ref.shape[1], WIDTH):
        r_ref[:, at:at + WIDTH] = one_hot(wanted == lax.broadcasted_iota(i32, (slots, WIDTH), 1) + at)


def block_row(row, rows, cols_ref, mixed_ref, stiff):
    terms, stored = stiff.shape[:2]
    picked = jnp.concatenate(
        [
            mixed_ref[cols_ref[c, row], term * rows:(term + 1) * rows, :]
            for term in range(terms)
            for c in range(stored)
        ],
        axis=1,
    )
    return dot(picked, stiff.reshape(terms * stored * LANES, LANES))


def mix(mixer, field_ref, mixed_ref, start, stop):
    rows = field_ref.shape[0] * field_ref.shape[1]
    for at in range(start, stop, WIDTH):
        field = field_ref[:, :, at:at + WIDTH].reshape(rows, WIDTH)
        mixed = dot(mixer, field).astype(bf16)
        for part in range(WIDTH // LANES):
            mixed_ref[at // LANES + part] = mixed[:, part * LANES:(part + 1) * LANES]


def interface_part(rows, cols_ref, mixed_ref, stiff_ref):
    stored, out_blocks = cols_ref.shape
    owned_blocks = mixed_ref.shape[0]
    parts = [
        block_row(row, rows, cols_ref, mixed_ref, stiff_ref[:, (row - owned_blocks) * stored:(row - owned_blocks + 1) * stored])
        for row in range(owned_blocks, out_blocks)
    ]
    return jnp.concatenate(parts, axis=1).astype(bf16)


def last_stored(blocks_ref, stiff_ref):
    count = stiff_ref.shape[1]
    return blocks_ref.at[:, pl.ds(blocks_ref.shape[1] - count, count)]


def setup_kernel(groups, cols_hbm, coef_hbm, send_hbm, own_hbm, blocks_ref,
                 g_ref, place_ref, own_ref, stiff_ref, cols_ref, coef_ref, send_ref, sems):
    copies = begin(
        sems, (cols_hbm, cols_ref), (coef_hbm, coef_ref), (send_hbm, send_ref), (own_hbm, own_ref),
        (last_stored(blocks_ref, stiff_ref), stiff_ref),
    )
    modes = cols_ref.shape[2]
    rows = groups * PAD
    out_mode = lax.broadcasted_iota(i32, (rows, modes), 1)
    spread = one_hot(padded_place(out_mode, groups, modes // groups) == lax.broadcasted_iota(i32, (rows, modes), 0))
    finish(copies[:3])
    for term in range(cols_ref.shape[0]):
        g_ref[term * rows:(term + 1) * rows, :] = dot_t(spread, mixer_columns(term, groups, cols_ref, coef_ref)).astype(bf16)
    place_ref[...] = one_hot(send_ref[...] == lax.broadcasted_iota(i32, place_ref.shape, 0))
    finish(copies[3:])


def first_kernel(groups, v0, v1, v2, v3, g_ref, place_ref, cols_hbm, stiff_ref,
                 packed_ref, mixed_hbm, field_ref, mixed_ref, cols_ref, sems):
    cols_copy = begin(sems, (cols_hbm, cols_ref))
    me = lax.axis_index("mode")
    modes_dev, owned = v0.shape
    field_ref[:, modes_dev:, :] = jnp.zeros_like(field_ref[:, modes_dev:, :])
    for slot, source in enumerate((v0, v1, v2, v3)):
        field_ref[lax.rem(me + slot, groups), :modes_dev, :] = source[...]
    mixer = g_ref[...]
    pieces = 2
    width = owned // pieces
    keeps = []
    for piece in range(pieces):
        mix(mixer, field_ref, mixed_ref, piece * width, (piece + 1) * width)
        at = pl.ds(piece * width // LANES, width // LANES)
        keeps += begin(sems.at[pl.ds(1 + piece, 1)], (mixed_ref.at[at], mixed_hbm.at[at]))
    finish(cols_copy)
    part = interface_part(groups * PAD, cols_ref, mixed_ref, stiff_ref)
    packed_ref[...] = dot_t(place_ref[...], part).astype(bf16)
    finish(keeps)


def own_fetch(steps, stored, blocks_ref, stiff_ref, sems):
    count = stiff_ref.shape[1] // steps
    return begin(
        sems, *((blocks_ref.at[:, pl.ds(step * count, count)], stiff_ref.at[:, pl.ds(step * count, count)]) for step in range(steps))
    )


def own_rows(rows, cols_ref, mixed_ref, stiff_ref, copies, own_ref):
    stored = cols_ref.shape[0]
    per = mixed_ref.shape[0] // len(copies)
    for step, copy in enumerate(copies):
        copy.wait()
        for row in range(step * per, (step + 1) * per):
            own_ref[:, row * LANES:(row + 1) * LANES] = block_row(
                row, rows, cols_ref, mixed_ref, stiff_ref[:, row * stored:(row + 1) * stored]
            )


def between_kernel(groups, steps, mixed_hbm, cols_hbm, coef_hbm, recv_hbm, where_hbm, blocks_ref,
                   own_ref, r_ref, g2_ref, mixed_ref, stiff_ref, cols_ref, coef_ref, recv_ref, where_ref, sems):
    small = begin(
        sems, (cols_hbm, cols_ref), (coef_hbm, coef_ref), (recv_hbm, recv_ref), (where_hbm, where_ref), (mixed_hbm, mixed_ref)
    )
    copies = own_fetch(steps, where_ref.shape[0], blocks_ref, stiff_ref, sems.at[pl.ds(len(small), steps)])
    me = lax.axis_index("mode")
    modes = cols_ref.shape[2]
    modes_dev = modes // groups
    row = lax.broadcasted_iota(i32, (PAD, modes), 0)
    mine = one_hot((lax.broadcasted_iota(i32, (PAD, modes), 1) == row + me * modes_dev) & (row < modes_dev))
    finish(small[:3])
    for term in range(cols_ref.shape[0]):
        g2_ref[term * PAD:(term + 1) * PAD, :] = dot_t(mine, mixer_columns(term, groups, cols_ref, coef_ref)).astype(bf16)
    receive_table(recv_ref, r_ref)
    finish(small[3:])
    own_rows(groups * PAD, where_ref, mixed_ref, stiff_ref, copies, own_ref)


def second_kernel(groups, own_ref, arrived_ref, r_ref, g2_ref, send_hbm, where_hbm, blocks_ref,
                  first_ref, mixed_hbm, packed_ref, field_ref, mixed_ref, spread_ref, stiff_ref, send_ref, where_ref, sems):
    small = begin(sems, (send_hbm, send_ref), (where_hbm, where_ref), (last_stored(blocks_ref, stiff_ref), stiff_ref))
    me = lax.axis_index("mode")
    owned = own_ref.shape[1]
    arrived = arrived_ref[...].astype(f32).T.astype(bf16)
    for at in range(0, owned, WIDTH):
        total = own_ref[:, at:at + WIDTH] + dot(arrived, r_ref[:, at:at + WIDTH])
        field_ref[:, :, at:at + WIDTH] = total.astype(bf16).reshape(groups, PAD, WIDTH)
    first_ref[...] = field_ref[me, :first_ref.shape[0], :]
    mix(g2_ref[...], field_ref, mixed_ref, 0, owned)
    keeps = begin(sems.at[pl.ds(len(small), 1)], (mixed_ref, mixed_hbm))
    spread_ref[...] = jnp.zeros_like(spread_ref)
    width = send_ref.shape[1]
    finish(small)
    send = send_ref[...]
    lines = lax.broadcasted_iota(i32, (packed_ref.shape[0], width), 0) * QUARTERS
    place = jnp.concatenate([one_hot(send == lines + quarter) for quarter in range(QUARTERS)], axis=1)
    part = interface_part(PAD, where_ref, mixed_ref, stiff_ref)
    for quarter in range(QUARTERS):
        spread_ref[quarter * PAD:(quarter + 1) * PAD, quarter * width:(quarter + 1) * width] = part
    packed_ref[...] = dot_t(place, spread_ref[...]).astype(bf16)
    finish(keeps)


def own_kernel(steps, where_hbm, recv_hbm, mixed_hbm, blocks_ref, own_ref, r_ref,
               mixed_ref, stiff_ref, recv_ref, where_ref, sems):
    small = begin(sems, (recv_hbm, recv_ref), (where_hbm, where_ref), (mixed_hbm, mixed_ref))
    copies = own_fetch(steps, where_ref.shape[0], blocks_ref, stiff_ref, sems.at[pl.ds(len(small), steps)])
    finish(small[:1])
    receive_table(recv_ref, r_ref)
    finish(small[1:])
    own_rows(PAD, where_ref, mixed_ref, stiff_ref, copies, own_ref)


def last_kernel(own_ref, arrived_ref, r_ref, out_ref, slots_ref):
    arrived = arrived_ref[...].astype(f32)
    lines = arrived.shape[0]
    for quarter in range(QUARTERS):
        turned = pltpu.roll(arrived, (QUARTERS - quarter) % QUARTERS * PAD, 1)
        slots_ref[pl.ds(quarter, lines, stride=QUARTERS), :] = turned
    by_slot = slots_ref[...].T[:PAD, :].astype(bf16)
    for at in range(0, own_ref.shape[1], WIDTH):
        total = own_ref[:, at:at + WIDTH] + dot(by_slot, r_ref[:, at:at + WIDTH])
        out_ref[:, at:at + WIDTH] = total.astype(bf16)[:out_ref.shape[0], :]


def local(groups, peers, modes_in, blocks, block_cols, send_slot, recv_row, mix_cols, mix_coef):
    terms, all_stored, blk, _ = blocks.shape
    out_blocks, stored = block_cols.shape
    modes_dev, owned = modes_in.shape
    owned_blocks = owned // blk
    interface = send_slot.shape[0]
    slots = recv_row.shape[0]
    cap = slots // peers
    rows = groups * PAD
    lines = slots // QUARTERS
    Shape, dma = jax.ShapeDtypeStruct, pltpu.SemaphoreType.DMA

    def pin(x):
        return pltpu.with_memory_space_constraint(x, pltpu.HBM)

    others = {
        s: lax.ppermute(modes_in, "mode", [((to + s) % groups, to) for to in range(groups)])
        for s in (2, 1, 3)
    }
    blocks = pin(blocks)
    where = pin(block_cols.T)
    mix_cols, mix_coef = pin(mix_cols.transpose(0, 2, 1)), pin(mix_coef.transpose(0, 2, 1))
    send, recv = pin(send_slot.reshape(1, interface)), pin(recv_row.reshape(1, slots))
    tables = [pltpu.VMEM(mix_cols.shape, i32), pltpu.VMEM(mix_coef.shape, f32)]
    where_scratch = pltpu.SMEM(where.shape, i32)
    send_scratch, recv_scratch = pltpu.VMEM(send.shape, i32), pltpu.VMEM(recv.shape, i32)
    if_blocks = (terms, (out_blocks - owned_blocks) * stored, blk, blk)
    own_scratch = pltpu.VMEM((terms, owned_blocks * stored, blk, blk), bf16)
    field_scratch = pltpu.VMEM((groups, PAD, owned), bf16)
    block_flops = 2 * terms * stored * blk * blk
    wide, narrow = (owned_blocks, terms * rows, blk), (owned_blocks, terms * PAD, blk)

    g, place, own_field, stiff = call(
        functools.partial(setup_kernel, groups),
        [Shape((terms * rows, rows), bf16), Shape((slots, interface), bf16), Shape((modes_dev, owned), bf16), Shape(if_blocks, bf16)],
        [mix_cols, mix_coef, send, pin(modes_in), blocks], [HBM] * 5, [VMEM] * 4, flops=10**6,
        scratch=[*tables, send_scratch, dma((5,))],
    )
    packed, mixed = call(
        functools.partial(first_kernel, groups),
        [Shape((slots, rows), bf16), pltpu.HBM(wide, bf16)],
        [own_field, others[1], others[2], others[3], g, place, where, stiff],
        [VMEM] * 6 + [HBM, VMEM], [VMEM, HBM],
        flops=block_flops * (out_blocks - owned_blocks) * rows,
        scratch=[field_scratch, pltpu.VMEM(wide, bf16), where_scratch, dma((3,))],
    )
    arrived = lax.all_to_all(packed.reshape(peers, cap, rows), "space", split_axis=0, concat_axis=0, tiled=True)
    steps = 8
    own, r, g2 = call(
        functools.partial(between_kernel, groups, steps),
        [Shape((rows, owned), f32), Shape((slots, owned), bf16), Shape((terms * PAD, rows), bf16)],
        [pin(mixed), mix_cols, mix_coef, recv, where, blocks], [HBM] * 6, [VMEM] * 3,
        flops=block_flops * owned_blocks * rows,
        scratch=[pltpu.VMEM(wide, bf16), own_scratch, *tables, recv_scratch, where_scratch, dma((5 + steps,))],
    )
    first_apply, mixed2, packed2 = call(
        functools.partial(second_kernel, groups),
        [Shape((modes_dev, owned), bf16), pltpu.HBM(narrow, bf16), Shape((lines, QUARTERS * PAD), bf16)],
        [own, arrived.reshape(slots, rows), r, g2, send, where, blocks],
        [VMEM] * 4 + [HBM] * 3, [VMEM, HBM, VMEM], flops=2 * slots * rows * owned,
        scratch=[field_scratch, pltpu.VMEM(narrow, bf16), pltpu.VMEM((QUARTERS * PAD, QUARTERS * interface), bf16),
                 pltpu.VMEM(if_blocks, bf16), send_scratch, where_scratch, dma((4,))],
    )
    arrived2 = lax.all_to_all(
        packed2.reshape(peers, cap // QUARTERS, QUARTERS * PAD), "space", split_axis=0, concat_axis=0, tiled=True
    )
    own2, r2 = call(
        functools.partial(own_kernel, steps), [Shape((PAD, owned), f32), Shape((slots, owned), bf16)],
        [where, recv, pin(mixed2), blocks], [HBM] * 4, [VMEM] * 2, flops=block_flops * owned_blocks * PAD,
        scratch=[pltpu.VMEM(narrow, bf16), own_scratch, recv_scratch, where_scratch, dma((3 + steps,))],
    )
    second_apply = call(
        last_kernel, [Shape((modes_dev, owned), bf16)],
        [own2, arrived2.reshape(lines, QUARTERS * PAD), r2], [VMEM] * 3, [VMEM],
        flops=2 * slots * PAD * owned, scratch=[pltpu.VMEM((slots, QUARTERS * PAD), f32)],
    )[0]
    return (first_apply, second_apply)


def solution(mesh):
    in_specs = (
        P("mode", "space"),
        P(None, "space", None, None),
        P("space", None),
        P("space"),
        P("space"),
        P(),
        P(),
    )
    out_specs = (P("mode", "space"), P("mode", "space"))
    body = functools.partial(local, mesh.shape["mode"], mesh.shape["space"])
    return jax.shard_map(body, mesh=mesh, in_specs=in_specs, out_specs=out_specs, check_vma=False)
```

```python
import functools
import math

import jax
import jax.numpy as jnp
from jax import lax
from jax.experimental import pallas as pl
from jax.experimental.pallas import tpu as pltpu
from jax.sharding import PartitionSpec as P

LANES = 128
PAD = 32
QUARTERS = 4
WIDTH = 256

VMEM = pl.BlockSpec(memory_space=pltpu.VMEM)
SMEM = pl.BlockSpec(memory_space=pltpu.SMEM)
HBM = pl.BlockSpec(memory_space=pltpu.HBM)
VMEM_LIMIT = 32 * 1024 * 1024
bf16, f32, i32 = jnp.bfloat16, jnp.float32, jnp.int32


def call(kernel, outs, ins, in_specs, out_specs, flops, scratch=()):
    moved = sum(math.prod(a.shape) * jnp.dtype(a.dtype).itemsize for a in [*outs, *ins])
    return pl.pallas_call(
        kernel,
        out_shape=outs,
        in_specs=in_specs,
        out_specs=out_specs,
        scratch_shapes=scratch,
        compiler_params=pltpu.CompilerParams(vmem_limit_bytes=VMEM_LIMIT),
        cost_estimate=pl.CostEstimate(flops=flops, bytes_accessed=moved, transcendentals=0),
    )(*ins)


def begin(sems, *pairs):
    copies = [pltpu.make_async_copy(source, target, sems.at[at]) for at, (source, target) in enumerate(pairs)]
    for copy in copies:
        copy.start()
    return copies


def finish(copies):
    for copy in copies:
        copy.wait()


def one_hot(hit):
    return jnp.where(hit, 1.0, 0.0).astype(bf16)


def dot(a, b):
    return jnp.dot(a, b, preferred_element_type=f32)


def dot_t(a, b):
    return lax.dot_general(a, b, (((1,), (1,)), ((), ())), preferred_element_type=f32)


def padded_place(modes, groups, modes_dev):
    place = modes
    for group in range(1, groups):
        place += jnp.where(modes >= group * modes_dev, PAD - modes_dev, 0)
    return place


def mixer_columns(term, groups, cols_ref, coef_ref):
    modes = cols_ref.shape[2]
    cols = cols_ref[term]
    place = jnp.where(cols < modes, padded_place(cols, groups, modes // groups), -1)
    coef = coef_ref[term]
    want = lax.broadcasted_iota(i32, (groups * PAD, modes), 0)
    total = jnp.zeros(want.shape, f32)
    for slot in range(cols.shape[0]):
        total += jnp.where(place[slot:slot + 1, :] == want, coef[slot:slot + 1, :], 0.0)
    return total.astype(bf16)


def block_row(row, rows, cols_ref, mixed_ref, stiff):
    terms, stored = stiff.shape[:2]
    picked = jnp.concatenate(
        [
            mixed_ref[cols_ref[c, row], term * rows:(term + 1) * rows, :]
            for term in range(terms)
            for c in range(stored)
        ],
        axis=1,
    )
    return dot(picked, stiff.reshape(terms * stored * LANES, LANES))


def last_stored(blocks_ref, stiff_ref):
    count = stiff_ref.shape[1]
    return blocks_ref.at[:, pl.ds(blocks_ref.shape[1] - count, count)]


def by_quarter(rows_ref, quarter):
    return rows_ref[pl.ds(quarter, rows_ref.shape[0] // QUARTERS, stride=QUARTERS), :]


def receive_table(recv_ref, r_ref, turned_ref):
    slots = recv_ref.shape[1]
    turned_ref[...] = jnp.broadcast_to(recv_ref[...].astype(f32), (LANES, slots)).T
    lanes = lax.broadcasted_iota(i32, (slots // QUARTERS, LANES), 1)
    for quarter in range(QUARTERS):
        offset = by_quarter(turned_ref, quarter).astype(i32) - lanes
        at = slice(quarter * slots // QUARTERS, (quarter + 1) * slots // QUARTERS)
        for block in range(r_ref.shape[0]):
            r_ref[block, at, :] = one_hot(offset == block * LANES)


def mixed_row(picked, stiff, mixer):
    terms, stored = stiff.shape[:2]
    wide = jnp.concatenate([stiff[term].reshape(stored * LANES, LANES) for term in range(terms)], axis=1)
    product = dot(picked, wide).astype(bf16)
    return dot(mixer, jnp.concatenate([product[:, term * LANES:(term + 1) * LANES] for term in range(terms)], axis=0))


def setup_kernel(groups, cols_hbm, coef_hbm, send_hbm, own_hbm, blocks_ref,
                 g_ref, place_ref, own_ref, stiff_ref, cols_ref, coef_ref, send_ref, sems):
    copies = begin(
        sems, (cols_hbm, cols_ref), (coef_hbm, coef_ref), (send_hbm, send_ref), (own_hbm, own_ref),
        (last_stored(blocks_ref, stiff_ref), stiff_ref),
    )
    modes = cols_ref.shape[2]
    rows = groups * PAD
    out_mode = lax.broadcasted_iota(i32, (rows, modes), 1)
    spread = one_hot(padded_place(out_mode, groups, modes // groups) == lax.broadcasted_iota(i32, (rows, modes), 0))
    finish(copies[:3])
    for term in range(cols_ref.shape[0]):
        g_ref[:, term * rows:(term + 1) * rows] = dot_t(spread, mixer_columns(term, groups, cols_ref, coef_ref)).astype(bf16)
    place_ref[...] = one_hot(send_ref[...] == lax.broadcasted_iota(i32, place_ref.shape, 0))
    finish(copies[3:])


def first_kernel(groups, v0, v1, v2, v3, g_ref, place_ref, where_hbm, stiff_ref,
                 packed_ref, field_hbm, g_hbm, field_ref, where_ref, sems):
    copies = begin(sems, (where_hbm, where_ref), (g_ref, g_hbm))
    me = lax.axis_index("mode")
    owned_blocks, _, _, lanes = field_ref.shape
    modes_dev = v0.shape[0]
    field_ref[:, :, modes_dev:, :] = jnp.zeros_like(field_ref[:, :, modes_dev:, :])
    for slot, source in enumerate((v0, v1, v2, v3)):
        group = lax.rem(me + slot, groups)
        for block in range(owned_blocks):
            field_ref[block, group, :modes_dev, :] = source[:, block * lanes:(block + 1) * lanes]
    copies += begin(sems.at[pl.ds(2, 1)], (field_ref, field_hbm))
    copies[0].wait()
    mixer = g_ref[...]
    stored, out_blocks = where_ref.shape
    parts = []
    for row in range(owned_blocks, out_blocks):
        picked = jnp.concatenate(
            [field_ref[where_ref[c, row]].reshape(groups * PAD, lanes) for c in range(stored)], axis=1
        )
        at = (row - owned_blocks) * stored
        parts.append(mixed_row(picked, stiff_ref[:, at:at + stored], mixer))
    part = jnp.concatenate(parts, axis=1).astype(bf16)
    packed_ref[...] = dot_t(place_ref[...], part).astype(bf16)
    finish(copies[1:])


def own_fetch(steps, stored, blocks_ref, stiff_ref, sems):
    count = stiff_ref.shape[1] // steps
    return begin(
        sems, *((blocks_ref.at[:, pl.ds(step * count, count)], stiff_ref.at[:, pl.ds(step * count, count)]) for step in range(steps))
    )


def between_kernel(groups, steps, field_hbm, g_hbm, cols_hbm, coef_hbm, recv_hbm, where_hbm, blocks_ref,
                   own_ref, own_hbm, r_ref, g2_ref, g2_hbm,
                   field_ref, g_ref, stiff_ref, cols_ref, coef_ref, recv_ref, where_ref, turned_ref, sems):
    small = begin(
        sems, (cols_hbm, cols_ref), (coef_hbm, coef_ref), (recv_hbm, recv_ref), (where_hbm, where_ref),
        (g_hbm, g_ref), (field_hbm, field_ref),
    )
    used = len(small)
    copies = own_fetch(steps, where_ref.shape[0], blocks_ref, stiff_ref, sems.at[pl.ds(used, steps)])
    me = lax.axis_index("mode")
    terms, _, modes = cols_ref.shape
    modes_dev = modes // groups
    rows = groups * PAD
    row = lax.broadcasted_iota(i32, (PAD, modes), 0)
    mine = one_hot((lax.broadcasted_iota(i32, (PAD, modes), 1) == row + me * modes_dev) & (row < modes_dev))
    finish(small[:3])
    for term in range(terms):
        g2_ref[:, term * rows:(term + 1) * rows] = dot_t(mine, mixer_columns(term, groups, cols_ref, coef_ref)).astype(bf16)
    keeps = begin(sems.at[pl.ds(used + steps, 1)], (g2_ref, g2_hbm))
    receive_table(recv_ref, r_ref, turned_ref)
    finish(small[3:])
    mixer = g_ref[...]
    stored = where_ref.shape[0]
    owned_blocks = own_ref.shape[0]
    per = owned_blocks // steps
    for step in range(steps):
        copies[step].wait()
        for block in range(step * per, (step + 1) * per):
            picked = jnp.concatenate(
                [field_ref[where_ref[c, block]].reshape(rows, LANES) for c in range(stored)], axis=1
            )
            own_ref[block] = mixed_row(picked, stiff_ref[:, block * stored:(block + 1) * stored], mixer)
        at = pl.ds(step * per, per)
        keeps += begin(sems.at[pl.ds(used + steps + 1 + step, 1)], (own_ref.at[at], own_hbm.at[at]))
    finish(keeps)


def second_kernel(groups, own_ref, arrived_ref, r_ref, g2_ref, send_hbm, where_hbm, blocks_ref,
                  packed_ref, turned_hbm, turned_ref, lines_ref, spread_ref, stiff_ref, send_ref, where_ref, sems):
    small = begin(sems, (where_hbm, where_ref), (send_hbm, send_ref), (last_stored(blocks_ref, stiff_ref), stiff_ref))
    lines_ref[...] = arrived_ref[...].astype(f32)
    turned_ref[...] = jnp.concatenate(
        [by_quarter(lines_ref, quarter).T.astype(bf16) for quarter in range(QUARTERS)], axis=1
    )
    keeps = begin(sems.at[pl.ds(len(small), 1)], (turned_ref, turned_hbm))
    turned = turned_ref[...]
    width = send_ref.shape[1]
    finish(small[:2])
    lines = lax.broadcasted_iota(i32, (packed_ref.shape[0], width), 0) * QUARTERS
    place = jnp.concatenate([one_hot(send_ref[...] == lines + quarter) for quarter in range(QUARTERS)], axis=1)
    spread_ref[...] = jnp.zeros_like(spread_ref)
    stored, out_blocks = where_ref.shape
    owned_blocks = own_ref.shape[0]
    picks = []
    for row in range(owned_blocks, out_blocks):
        columns = [where_ref[c, row] for c in range(stored)]
        base = jnp.concatenate([own_ref[column] for column in columns], axis=1)
        table = jnp.concatenate([r_ref[column] for column in columns], axis=1)
        picks.append((base + dot(turned, table)).astype(bf16))
    small[2].wait()
    mixer = g2_ref[...]
    part = jnp.concatenate(
        [mixed_row(picked, stiff_ref[:, at * stored:(at + 1) * stored], mixer) for at, picked in enumerate(picks)], axis=1
    ).astype(bf16)
    for quarter in range(QUARTERS):
        spread_ref[quarter * PAD:(quarter + 1) * PAD, quarter * width:(quarter + 1) * width] = part
    packed_ref[...] = dot_t(place, spread_ref[...]).astype(bf16)
    finish(keeps)


def own_kernel(groups, steps, where_hbm, recv_hbm, g2_hbm, turned_hbm, own_hbm, blocks_ref,
               first_ref, own2_ref, r_ref,
               own_ref, field_ref, mixed_ref, stiff_ref, recv_ref, where_ref, g2_ref, turned_ref, rows_ref, sems):
    small = begin(
        sems, (recv_hbm, recv_ref), (where_hbm, where_ref), (g2_hbm, g2_ref), (turned_hbm, turned_ref), (own_hbm, own_ref)
    )
    copies = own_fetch(steps, where_ref.shape[0], blocks_ref, stiff_ref, sems.at[pl.ds(len(small), steps)])
    me = lax.axis_index("mode")
    small[0].wait()
    receive_table(recv_ref, r_ref, rows_ref)
    finish(small[1:])
    owned_blocks, rows, lanes = own_ref.shape
    terms, stored = stiff_ref.shape[0], where_ref.shape[0]
    modes_dev = first_ref.shape[0]
    turned = turned_ref[...]
    mixer = jnp.concatenate([g2_ref[:, term * rows:(term + 1) * rows] for term in range(terms)], axis=0)
    for block in range(0, owned_blocks, 2):
        table = jnp.concatenate([r_ref[block], r_ref[block + 1]], axis=1)
        base = jnp.concatenate([own_ref[block], own_ref[block + 1]], axis=1)
        field = (base + dot(turned, table)).astype(bf16)
        mixed = dot(mixer, field).astype(bf16)
        for part in range(2):
            field_ref[block + part] = field[:, part * lanes:(part + 1) * lanes].reshape(groups, PAD, lanes)
            mixed_ref[block + part] = mixed[:, part * lanes:(part + 1) * lanes]
            first_ref[:, (block + part) * lanes:(block + part + 1) * lanes] = field_ref[block + part, me, :modes_dev, :]
    per = owned_blocks // steps
    for step in range(steps):
        copies[step].wait()
        for block in range(step * per, (step + 1) * per):
            own2_ref[:, block * lanes:(block + 1) * lanes] = block_row(
                block, PAD, where_ref, mixed_ref, stiff_ref[:, block * stored:(block + 1) * stored]
            )


def last_kernel(own_ref, arrived_ref, r_ref, out_ref):
    turned = arrived_ref[...].astype(f32).T.astype(bf16)
    by_slot = jnp.concatenate([turned[quarter * PAD:(quarter + 1) * PAD, :] for quarter in range(QUARTERS)], axis=1)
    for block in range(0, r_ref.shape[0], 2):
        at = slice(block * LANES, (block + 2) * LANES)
        table = jnp.concatenate([r_ref[block], r_ref[block + 1]], axis=1)
        total = own_ref[:, at] + dot(by_slot, table)
        out_ref[:, at] = total.astype(bf16)[:out_ref.shape[0], :]


def local(groups, peers, modes_in, blocks, block_cols, send_slot, recv_row, mix_cols, mix_coef):
    terms, all_stored, blk, _ = blocks.shape
    out_blocks, stored = block_cols.shape
    modes_dev, owned = modes_in.shape
    owned_blocks = owned // blk
    interface = send_slot.shape[0]
    slots = recv_row.shape[0]
    cap = slots // peers
    rows = groups * PAD
    lines = slots // QUARTERS
    Shape, dma = jax.ShapeDtypeStruct, pltpu.SemaphoreType.DMA

    def pin(x):
        return pltpu.with_memory_space_constraint(x, pltpu.HBM)

    others = {
        s: lax.ppermute(modes_in, "mode", [((to + s) % groups, to) for to in range(groups)])
        for s in (2, 1, 3)
    }
    blocks = pin(blocks)
    where = pin(block_cols.T)
    mix_cols, mix_coef = pin(mix_cols.transpose(0, 2, 1)), pin(mix_coef.transpose(0, 2, 1))
    send, recv = pin(send_slot.reshape(1, interface)), pin(recv_row.reshape(1, slots))
    tables = [pltpu.VMEM(mix_cols.shape, i32), pltpu.VMEM(mix_coef.shape, f32)]
    where_scratch = pltpu.SMEM(where.shape, i32)
    send_scratch, recv_scratch = pltpu.VMEM(send.shape, i32), pltpu.VMEM(recv.shape, i32)
    if_blocks = (terms, (out_blocks - owned_blocks) * stored, blk, blk)
    own_scratch = pltpu.VMEM((terms, owned_blocks * stored, blk, blk), bf16)
    field_shape = (owned_blocks, groups, PAD, blk)
    field_scratch = pltpu.VMEM(field_shape, bf16)
    own_shape, table_shape = (owned_blocks, rows, blk), (owned_blocks, slots, blk)
    turned_scratch = pltpu.VMEM((slots, LANES), f32)
    block_flops = 2 * terms * stored * blk * blk

    g, place, own_field, stiff = call(
        functools.partial(setup_kernel, groups),
        [Shape((rows, terms * rows), bf16), Shape((slots, interface), bf16), Shape((modes_dev, owned), bf16), Shape(if_blocks, bf16)],
        [mix_cols, mix_coef, send, pin(modes_in), blocks], [HBM] * 5, [VMEM] * 4, flops=10**6,
        scratch=[*tables, send_scratch, dma((5,))],
    )
    packed, field, g_kept = call(
        functools.partial(first_kernel, groups),
        [Shape((slots, rows), bf16), pltpu.HBM(field_shape, bf16), pltpu.HBM((rows, terms * rows), bf16)],
        [own_field, others[1], others[2], others[3], g, place, where, stiff],
        [VMEM] * 6 + [HBM, VMEM], [VMEM, HBM, HBM],
        flops=block_flops * (out_blocks - owned_blocks) * rows,
        scratch=[field_scratch, where_scratch, dma((3,))],
    )
    arrived = lax.all_to_all(packed.reshape(peers, cap, rows), "space", split_axis=0, concat_axis=0, tiled=True)
    steps = 16
    own, own_kept, r, g2, g2_kept = call(
        functools.partial(between_kernel, groups, steps),
        [Shape(own_shape, f32), pltpu.HBM(own_shape, f32), Shape(table_shape, bf16),
         Shape((PAD, terms * rows), bf16), pltpu.HBM((PAD, terms * rows), bf16)],
        [pin(field), pin(g_kept), mix_cols, mix_coef, recv, where, blocks], [HBM] * 7, [VMEM, HBM, VMEM, VMEM, HBM],
        flops=block_flops * owned_blocks * rows,
        scratch=[field_scratch, pltpu.VMEM((rows, terms * rows), bf16), own_scratch, *tables, recv_scratch, where_scratch,
                 turned_scratch, dma((7 + 2 * steps,))],
    )
    packed2, turned = call(
        functools.partial(second_kernel, groups),
        [Shape((lines, QUARTERS * PAD), bf16), pltpu.HBM((rows, slots), bf16)],
        [own, arrived.reshape(slots, rows), r, g2, send, where, blocks],
        [VMEM] * 4 + [HBM] * 3, [VMEM, HBM], flops=2 * slots * rows * owned,
        scratch=[pltpu.VMEM((rows, slots), bf16), turned_scratch, pltpu.VMEM((QUARTERS * PAD, QUARTERS * interface), bf16),
                 pltpu.VMEM(if_blocks, bf16), send_scratch, where_scratch, dma((4,))],
    )
    arrived2 = lax.all_to_all(
        packed2.reshape(peers, cap // QUARTERS, QUARTERS * PAD), "space", split_axis=0, concat_axis=0, tiled=True
    )
    first_apply, own2, r2 = call(
        functools.partial(own_kernel, groups, steps),
        [Shape((modes_dev, owned), bf16), Shape((PAD, owned), f32), Shape(table_shape, bf16)],
        [where, recv, pin(g2_kept), pin(turned), pin(own_kept), blocks], [HBM] * 6, [VMEM] * 3,
        flops=block_flops * owned_blocks * PAD,
        scratch=[pltpu.VMEM(own_shape, f32), field_scratch, pltpu.VMEM((owned_blocks, terms * PAD, blk), bf16), own_scratch,
                 recv_scratch, where_scratch, pltpu.VMEM((PAD, terms * rows), bf16), pltpu.VMEM((rows, slots), bf16),
                 turned_scratch, dma((5 + steps,))],
    )
    second_apply = call(
        last_kernel, [Shape((modes_dev, owned), bf16)],
        [own2, arrived2.reshape(lines, QUARTERS * PAD), r2], [VMEM] * 3, [VMEM], flops=2 * slots * PAD * owned,
    )[0]
    return (first_apply, second_apply)


def solution(mesh):
    in_specs = (
        P("mode", "space"),
        P(None, "space", None, None),
        P("space", None),
        P("space"),
        P("space"),
        P(),
        P(),
    )
    out_specs = (P("mode", "space"), P("mode", "space"))
    body = functools.partial(local, mesh.shape["mode"], mesh.shape["space"])
    return jax.shard_map(body, mesh=mesh, in_specs=in_specs, out_specs=out_specs, check_vma=False)
```

```python
import functools
import math

import jax
import jax.numpy as jnp
from jax import lax
from jax.experimental import pallas as pl
from jax.experimental.pallas import tpu as pltpu
from jax.sharding import PartitionSpec as P

LANES = 128
PAD = 32
QUARTERS = 4
WIDTH = 256

VMEM = pl.BlockSpec(memory_space=pltpu.VMEM)
SMEM = pl.BlockSpec(memory_space=pltpu.SMEM)
HBM = pl.BlockSpec(memory_space=pltpu.HBM)
VMEM_LIMIT = 32 * 1024 * 1024
bf16, f32, i32 = jnp.bfloat16, jnp.float32, jnp.int32


def call(kernel, outs, ins, in_specs, out_specs, flops, scratch=()):
    moved = sum(math.prod(a.shape) * jnp.dtype(a.dtype).itemsize for a in [*outs, *ins])
    return pl.pallas_call(
        kernel,
        out_shape=outs,
        in_specs=in_specs,
        out_specs=out_specs,
        scratch_shapes=scratch,
        compiler_params=pltpu.CompilerParams(vmem_limit_bytes=VMEM_LIMIT),
        cost_estimate=pl.CostEstimate(flops=flops, bytes_accessed=moved, transcendentals=0),
    )(*ins)


def begin(sems, *pairs):
    copies = [pltpu.make_async_copy(source, target, sems.at[at]) for at, (source, target) in enumerate(pairs)]
    for copy in copies:
        copy.start()
    return copies


def finish(copies):
    for copy in copies:
        copy.wait()


def one_hot(hit):
    return jnp.where(hit, 1.0, 0.0).astype(bf16)


def dot(a, b):
    return jnp.dot(a, b, preferred_element_type=f32)


def dot_t(a, b):
    return lax.dot_general(a, b, (((1,), (1,)), ((), ())), preferred_element_type=f32)


def padded_place(modes, groups, modes_dev):
    place = modes
    for group in range(1, groups):
        place += jnp.where(modes >= group * modes_dev, PAD - modes_dev, 0)
    return place


def mixer_columns(term, groups, cols_ref, coef_ref):
    modes = cols_ref.shape[2]
    cols = cols_ref[term]
    place = jnp.where(cols < modes, padded_place(cols, groups, modes // groups), -1)
    coef = coef_ref[term]
    want = lax.broadcasted_iota(i32, (groups * PAD, modes), 0)
    total = jnp.zeros(want.shape, f32)
    for slot in range(cols.shape[0]):
        total += jnp.where(place[slot:slot + 1, :] == want, coef[slot:slot + 1, :], 0.0)
    return total.astype(bf16)


def receive_table(recv_ref, r_ref):
    slots = recv_ref.shape[1]
    turned = jnp.broadcast_to(recv_ref[...].astype(f32), (LANES, slots)).T
    wanted = turned[:, :1].astype(i32)
    for at in range(0, r_ref.shape[1], WIDTH):
        r_ref[:, at:at + WIDTH] = one_hot(wanted == lax.broadcasted_iota(i32, (slots, WIDTH), 1) + at)


def block_row(row, rows, cols_ref, mixed_ref, stiff):
    terms, stored = stiff.shape[:2]
    picked = jnp.concatenate(
        [
            mixed_ref[cols_ref[c, row], term * rows:(term + 1) * rows, :]
            for term in range(terms)
            for c in range(stored)
        ],
        axis=1,
    )
    return dot(picked, stiff.reshape(terms * stored * LANES, LANES))


def mix(mixer, field_ref, mixed_ref):
    blocks, groups, pad, lanes = field_ref.shape
    for block in range(0, blocks, 2):
        pair = [field_ref[block + part].reshape(groups * pad, lanes) for part in range(2)]
        mixed = dot(mixer, jnp.concatenate(pair, axis=1)).astype(bf16)
        for part in range(2):
            mixed_ref[block + part] = mixed[:, part * lanes:(part + 1) * lanes]


def stacked(wide):
    return jnp.concatenate([wide[:, at:at + LANES] for at in range(0, wide.shape[1], LANES)], axis=0)


def interface_part(rows, cols_ref, mixed_ref, stiff_ref):
    stored, out_blocks = cols_ref.shape
    owned_blocks = mixed_ref.shape[0]
    parts = [
        block_row(row, rows, cols_ref, mixed_ref, stiff_ref[:, (row - owned_blocks) * stored:(row - owned_blocks + 1) * stored])
        for row in range(owned_blocks, out_blocks)
    ]
    return jnp.concatenate(parts, axis=1).astype(bf16)


def last_stored(blocks_ref, stiff_ref):
    count = stiff_ref.shape[1]
    return blocks_ref.at[:, pl.ds(blocks_ref.shape[1] - count, count)]


def mixed_row(picked, stiff, mixer):
    terms, stored = stiff.shape[:2]
    wide = jnp.concatenate([stiff[term].reshape(stored * LANES, LANES) for term in range(terms)], axis=1)
    product = dot(picked, wide).astype(bf16)
    return dot(mixer, jnp.concatenate([product[:, term * LANES:(term + 1) * LANES] for term in range(terms)], axis=0))


def setup_kernel(groups, cols_hbm, coef_hbm, send_hbm, own_hbm, where_hbm, blocks_ref,
                 g_ref, place_ref, own_ref, where_ref, stiff_ref, cols_ref, coef_ref, send_ref, sems):
    copies = begin(
        sems, (cols_hbm, cols_ref), (coef_hbm, coef_ref), (send_hbm, send_ref), (own_hbm, own_ref),
        (where_hbm, where_ref), (last_stored(blocks_ref, stiff_ref), stiff_ref),
    )
    modes = cols_ref.shape[2]
    rows = groups * PAD
    out_mode = lax.broadcasted_iota(i32, (rows, modes), 1)
    spread = one_hot(padded_place(out_mode, groups, modes // groups) == lax.broadcasted_iota(i32, (rows, modes), 0))
    finish(copies[:3])
    for term in range(cols_ref.shape[0]):
        g_ref[:, term * rows:(term + 1) * rows] = dot_t(spread, mixer_columns(term, groups, cols_ref, coef_ref)).astype(bf16)
    place_ref[...] = one_hot(send_ref[...] == lax.broadcasted_iota(i32, place_ref.shape, 0))
    finish(copies[3:])


def first_kernel(groups, v0, v1, v2, v3, g_ref, place_ref, where_ref, stiff_ref,
                 packed_ref, field_hbm, g_hbm, field_ref, sems):
    copies = begin(sems, (g_ref, g_hbm))
    me = lax.axis_index("mode")
    owned_blocks, _, _, lanes = field_ref.shape
    modes_dev = v0.shape[0]
    field_ref[:, :, modes_dev:, :] = jnp.zeros_like(field_ref[:, :, modes_dev:, :])
    for slot, source in enumerate((v0, v1, v2, v3)):
        group = lax.rem(me + slot, groups)
        for block in range(owned_blocks):
            field_ref[block, group, :modes_dev, :] = source[:, block * lanes:(block + 1) * lanes]
    copies += begin(sems.at[pl.ds(1, 1)], (field_ref, field_hbm))
    mixer = g_ref[...]
    stored, out_blocks = where_ref.shape
    parts = []
    for row in range(owned_blocks, out_blocks):
        picked = jnp.concatenate(
            [field_ref[where_ref[c, row]].reshape(groups * PAD, lanes) for c in range(stored)], axis=1
        )
        at = (row - owned_blocks) * stored
        parts.append(mixed_row(picked, stiff_ref[:, at:at + stored], mixer))
    part = jnp.concatenate(parts, axis=1).astype(bf16)
    packed_ref[...] = dot_t(place_ref[...], part).astype(bf16)
    finish(copies)


def own_fetch(steps, stored, blocks_ref, stiff_ref, sems):
    count = stiff_ref.shape[1] // steps
    return begin(
        sems, *((blocks_ref.at[:, pl.ds(step * count, count)], stiff_ref.at[:, pl.ds(step * count, count)]) for step in range(steps))
    )


def own_rows(rows, cols_ref, mixed_ref, stiff_ref, copies, own_ref):
    stored = cols_ref.shape[0]
    per = mixed_ref.shape[0] // len(copies)
    for step, copy in enumerate(copies):
        copy.wait()
        for row in range(step * per, (step + 1) * per):
            own_ref[:, row * LANES:(row + 1) * LANES] = block_row(
                row, rows, cols_ref, mixed_ref, stiff_ref[:, row * stored:(row + 1) * stored]
            )


def between_kernel(groups, steps, field_hbm, g_hbm, cols_hbm, coef_hbm, recv_hbm, send_hbm, where_hbm, blocks_ref,
                   own_ref, r_ref, g2_ref, where_out, send_out, field_ref, g_ref, mixed_ref, stiff_ref,
                   cols_ref, coef_ref, recv_ref, where_ref, sems):
    small = begin(
        sems, (cols_hbm, cols_ref), (coef_hbm, coef_ref), (recv_hbm, recv_ref), (where_hbm, where_ref),
        (g_hbm, g_ref), (field_hbm, field_ref), (where_hbm, where_out), (send_hbm, send_out),
    )
    copies = own_fetch(steps, where_ref.shape[0], blocks_ref, stiff_ref, sems.at[pl.ds(len(small), steps)])
    me = lax.axis_index("mode")
    terms, _, modes = cols_ref.shape
    modes_dev = modes // groups
    row = lax.broadcasted_iota(i32, (PAD, modes), 0)
    mine = one_hot((lax.broadcasted_iota(i32, (PAD, modes), 1) == row + me * modes_dev) & (row < modes_dev))
    finish(small[:3])
    for term in range(terms):
        g2_ref[term * PAD:(term + 1) * PAD, :] = dot_t(mine, mixer_columns(term, groups, cols_ref, coef_ref)).astype(bf16)
    receive_table(recv_ref, r_ref)
    finish(small[3:])
    mix(stacked(g_ref[...]), field_ref, mixed_ref)
    own_rows(groups * PAD, where_ref, mixed_ref, stiff_ref, copies, own_ref)


def second_kernel(groups, own_ref, arrived_ref, r_ref, g2_ref, send_ref, where_ref, blocks_ref,
                  first_ref, mixed_hbm, packed_ref, field_ref, mixed_ref, spread_ref, stiff_ref, sems):
    small = begin(sems, (last_stored(blocks_ref, stiff_ref), stiff_ref))
    me = lax.axis_index("mode")
    owned = own_ref.shape[1]
    arrived = arrived_ref[...].astype(f32).T.astype(bf16)
    for at in range(0, owned, WIDTH):
        total = own_ref[:, at:at + WIDTH] + dot(arrived, r_ref[:, at:at + WIDTH])
        total = total.astype(bf16)
        for part in range(0, WIDTH, LANES):
            field_ref[(at + part) // LANES] = total[:, part:part + LANES].reshape(groups, PAD, LANES)
    mix(g2_ref[...], field_ref, mixed_ref)
    keeps = begin(sems.at[pl.ds(len(small), 1)], (mixed_ref, mixed_hbm))
    spread_ref[...] = jnp.zeros_like(spread_ref)
    width = send_ref.shape[1]
    send = send_ref[...]
    lines = lax.broadcasted_iota(i32, (packed_ref.shape[0], width), 0) * QUARTERS
    place = jnp.concatenate([one_hot(send == lines + quarter) for quarter in range(QUARTERS)], axis=1)
    finish(small)
    part = interface_part(PAD, where_ref, mixed_ref, stiff_ref)
    for quarter in range(QUARTERS):
        spread_ref[quarter * PAD:(quarter + 1) * PAD, quarter * width:(quarter + 1) * width] = part
    packed_ref[...] = dot_t(place, spread_ref[...]).astype(bf16)
    for block in range(field_ref.shape[0]):
        first_ref[:, block * LANES:(block + 1) * LANES] = field_ref[block, me, :first_ref.shape[0], :]
    finish(keeps)


def own_kernel(steps, where_hbm, recv_hbm, mixed_hbm, blocks_ref, own_ref, r_ref,
               mixed_ref, stiff_ref, recv_ref, where_ref, sems):
    small = begin(sems, (recv_hbm, recv_ref), (where_hbm, where_ref), (mixed_hbm, mixed_ref))
    copies = own_fetch(steps, where_ref.shape[0], blocks_ref, stiff_ref, sems.at[pl.ds(len(small), steps)])
    finish(small[:1])
    receive_table(recv_ref, r_ref)
    finish(small[1:])
    own_rows(PAD, where_ref, mixed_ref, stiff_ref, copies, own_ref)


def last_kernel(own_ref, arrived_ref, r_ref, out_ref, slots_ref):
    arrived = arrived_ref[...].astype(f32)
    lines = arrived.shape[0]
    for quarter in range(QUARTERS):
        turned = pltpu.roll(arrived, (QUARTERS - quarter) % QUARTERS * PAD, 1)
        slots_ref[pl.ds(quarter, lines, stride=QUARTERS), :] = turned
    by_slot = slots_ref[...].T[:PAD, :].astype(bf16)
    for at in range(0, own_ref.shape[1], WIDTH):
        total = own_ref[:, at:at + WIDTH] + dot(by_slot, r_ref[:, at:at + WIDTH])
        out_ref[:, at:at + WIDTH] = total.astype(bf16)[:out_ref.shape[0], :]


def local(groups, peers, modes_in, blocks, block_cols, send_slot, recv_row, mix_cols, mix_coef):
    terms, all_stored, blk, _ = blocks.shape
    out_blocks, stored = block_cols.shape
    modes_dev, owned = modes_in.shape
    owned_blocks = owned // blk
    interface = send_slot.shape[0]
    slots = recv_row.shape[0]
    cap = slots // peers
    rows = groups * PAD
    lines = slots // QUARTERS
    Shape, dma = jax.ShapeDtypeStruct, pltpu.SemaphoreType.DMA

    def pin(x):
        return pltpu.with_memory_space_constraint(x, pltpu.HBM)

    others = {
        s: lax.ppermute(modes_in, "mode", [((to + s) % groups, to) for to in range(groups)])
        for s in (2, 1, 3)
    }
    blocks = pin(blocks)
    where = pin(block_cols.T)
    mix_cols, mix_coef = pin(mix_cols.transpose(0, 2, 1)), pin(mix_coef.transpose(0, 2, 1))
    send, recv = pin(send_slot.reshape(1, interface)), pin(recv_row.reshape(1, slots))
    tables = [pltpu.VMEM(mix_cols.shape, i32), pltpu.VMEM(mix_coef.shape, f32)]
    where_scratch = pltpu.SMEM(where.shape, i32)
    send_scratch, recv_scratch = pltpu.VMEM(send.shape, i32), pltpu.VMEM(recv.shape, i32)
    if_blocks = (terms, (out_blocks - owned_blocks) * stored, blk, blk)
    own_scratch = pltpu.VMEM((terms, owned_blocks * stored, blk, blk), bf16)
    field_shape, mixer_shape = (owned_blocks, groups, PAD, blk), (rows, terms * rows)
    field_scratch = pltpu.VMEM(field_shape, bf16)
    block_flops = 2 * terms * stored * blk * blk
    wide, narrow = (owned_blocks, terms * rows, blk), (owned_blocks, terms * PAD, blk)

    g, place, own_field, where_near, stiff = call(
        functools.partial(setup_kernel, groups),
        [Shape(mixer_shape, bf16), Shape((slots, interface), bf16), Shape((modes_dev, owned), bf16),
         Shape(where.shape, i32), Shape(if_blocks, bf16)],
        [mix_cols, mix_coef, send, pin(modes_in), where, blocks], [HBM] * 6, [VMEM] * 5, flops=10**6,
        scratch=[*tables, send_scratch, dma((6,))],
    )
    packed, field, g_kept = call(
        functools.partial(first_kernel, groups),
        [Shape((slots, rows), bf16), pltpu.HBM(field_shape, bf16), pltpu.HBM(mixer_shape, bf16)],
        [own_field, others[1], others[2], others[3], g, place, where_near, stiff],
        [VMEM] * 6 + [SMEM, VMEM], [VMEM, HBM, HBM],
        flops=block_flops * (out_blocks - owned_blocks) * rows,
        scratch=[field_scratch, dma((2,))],
    )
    arrived = lax.all_to_all(packed.reshape(peers, cap, rows), "space", split_axis=0, concat_axis=0, tiled=True)
    steps = 8
    own, r, g2, where_near, send_near = call(
        functools.partial(between_kernel, groups, steps),
        [Shape((rows, owned), f32), Shape((slots, owned), bf16), Shape((terms * PAD, rows), bf16),
         Shape(where.shape, i32), Shape(send.shape, i32)],
        [pin(field), pin(g_kept), mix_cols, mix_coef, recv, send, where, blocks], [HBM] * 8, [VMEM] * 5,
        flops=block_flops * owned_blocks * rows,
        scratch=[field_scratch, pltpu.VMEM(mixer_shape, bf16), pltpu.VMEM(wide, bf16), own_scratch, *tables, recv_scratch,
                 where_scratch, dma((8 + steps,))],
    )
    first_apply, mixed2, packed2 = call(
        functools.partial(second_kernel, groups),
        [Shape((modes_dev, owned), bf16), pltpu.HBM(narrow, bf16), Shape((lines, QUARTERS * PAD), bf16)],
        [own, arrived.reshape(slots, rows), r, g2, send_near, where_near, blocks],
        [VMEM] * 5 + [SMEM, HBM], [VMEM, HBM, VMEM], flops=2 * slots * rows * owned,
        scratch=[field_scratch, pltpu.VMEM(narrow, bf16), pltpu.VMEM((QUARTERS * PAD, QUARTERS * interface), bf16),
                 pltpu.VMEM(if_blocks, bf16), dma((2,))],
    )
    arrived2 = lax.all_to_all(
        packed2.reshape(peers, cap // QUARTERS, QUARTERS * PAD), "space", split_axis=0, concat_axis=0, tiled=True
    )
    own2, r2 = call(
        functools.partial(own_kernel, steps), [Shape((PAD, owned), f32), Shape((slots, owned), bf16)],
        [where, recv, pin(mixed2), blocks], [HBM] * 4, [VMEM] * 2, flops=block_flops * owned_blocks * PAD,
        scratch=[pltpu.VMEM(narrow, bf16), own_scratch, recv_scratch, where_scratch, dma((3 + steps,))],
    )
    second_apply = call(
        last_kernel, [Shape((modes_dev, owned), bf16)],
        [own2, arrived2.reshape(lines, QUARTERS * PAD), r2], [VMEM] * 3, [VMEM],
        flops=2 * slots * PAD * owned, scratch=[pltpu.VMEM((slots, QUARTERS * PAD), f32)],
    )[0]
    return (first_apply, second_apply)


def solution(mesh):
    in_specs = (
        P("mode", "space"),
        P(None, "space", None, None),
        P("space", None),
        P("space"),
        P("space"),
        P(),
        P(),
    )
    out_specs = (P("mode", "space"), P("mode", "space"))
    body = functools.partial(local, mesh.shape["mode"], mesh.shape["space"])
    return jax.shard_map(body, mesh=mesh, in_specs=in_specs, out_specs=out_specs, check_vma=False)
```

```python
import functools
import math

import jax
import jax.numpy as jnp
from jax import lax
from jax.experimental import pallas as pl
from jax.experimental.pallas import tpu as pltpu
from jax.sharding import PartitionSpec as P

LANES = 128
PAD = 32
QUARTERS = 4
WIDTH = 256

VMEM = pl.BlockSpec(memory_space=pltpu.VMEM)
SMEM = pl.BlockSpec(memory_space=pltpu.SMEM)
HBM = pl.BlockSpec(memory_space=pltpu.HBM)
VMEM_LIMIT = 32 * 1024 * 1024
bf16, f32, i32 = jnp.bfloat16, jnp.float32, jnp.int32


def call(kernel, outs, ins, in_specs, out_specs, flops, scratch=()):
    moved = sum(math.prod(a.shape) * jnp.dtype(a.dtype).itemsize for a in [*outs, *ins])
    return pl.pallas_call(
        kernel,
        out_shape=outs,
        in_specs=in_specs,
        out_specs=out_specs,
        scratch_shapes=scratch,
        compiler_params=pltpu.CompilerParams(vmem_limit_bytes=VMEM_LIMIT),
        cost_estimate=pl.CostEstimate(flops=flops, bytes_accessed=moved, transcendentals=0),
    )(*ins)


def begin(sems, *pairs):
    copies = [pltpu.make_async_copy(source, target, sems.at[at]) for at, (source, target) in enumerate(pairs)]
    for copy in copies:
        copy.start()
    return copies


def finish(copies):
    for copy in copies:
        copy.wait()


def one_hot(hit):
    return jnp.where(hit, 1.0, 0.0).astype(bf16)


def dot(a, b):
    return jnp.dot(a, b, preferred_element_type=f32)


def dot_t(a, b):
    return lax.dot_general(a, b, (((1,), (1,)), ((), ())), preferred_element_type=f32)


def padded_place(modes, groups, modes_dev):
    place = modes
    for group in range(1, groups):
        place += jnp.where(modes >= group * modes_dev, PAD - modes_dev, 0)
    return place


def mixer_columns(term, groups, cols_ref, coef_ref):
    modes = cols_ref.shape[2]
    cols = cols_ref[term]
    place = jnp.where(cols < modes, padded_place(cols, groups, modes // groups), -1)
    coef = coef_ref[term]
    want = lax.broadcasted_iota(i32, (groups * PAD, modes), 0)
    total = jnp.zeros(want.shape, f32)
    for slot in range(cols.shape[0]):
        total += jnp.where(place[slot:slot + 1, :] == want, coef[slot:slot + 1, :], 0.0)
    return total.astype(bf16)


def receive_table(recv_ref, r_ref):
    slots = recv_ref.shape[1]
    turned = jnp.broadcast_to(recv_ref[...].astype(f32), (LANES, slots)).T
    wanted = turned[:, :1].astype(i32)
    for at in range(0, r_ref.shape[1], WIDTH):
        r_ref[:, at:at + WIDTH] = one_hot(wanted == lax.broadcasted_iota(i32, (slots, WIDTH), 1) + at)


def block_row(row, rows, cols_ref, mixed_ref, stiff):
    terms, stored = stiff.shape[:2]
    picked = jnp.concatenate(
        [
            mixed_ref[cols_ref[c, row], term * rows:(term + 1) * rows, :]
            for term in range(terms)
            for c in range(stored)
        ],
        axis=1,
    )
    return dot(picked, stiff.reshape(terms * stored * LANES, LANES))


def mix(mixer, field_ref, mixed_ref):
    blocks, groups, pad, lanes = field_ref.shape
    for block in range(0, blocks, 2):
        pair = [field_ref[block + part].reshape(groups * pad, lanes) for part in range(2)]
        mixed = dot(mixer, jnp.concatenate(pair, axis=1)).astype(bf16)
        for part in range(2):
            mixed_ref[block + part] = mixed[:, part * lanes:(part + 1) * lanes]


def stacked(wide):
    return jnp.concatenate([wide[:, at:at + LANES] for at in range(0, wide.shape[1], LANES)], axis=0)


def interface_part(rows, cols_ref, mixed_ref, stiff_ref):
    stored, out_blocks = cols_ref.shape
    owned_blocks = mixed_ref.shape[0]
    parts = [
        block_row(row, rows, cols_ref, mixed_ref, stiff_ref[:, (row - owned_blocks) * stored:(row - owned_blocks + 1) * stored])
        for row in range(owned_blocks, out_blocks)
    ]
    return jnp.concatenate(parts, axis=1).astype(bf16)


def last_stored(blocks_ref, stiff_ref):
    count = stiff_ref.shape[1]
    return blocks_ref.at[:, pl.ds(blocks_ref.shape[1] - count, count)]


def mixed_row(picked, stiff, mixer):
    terms, stored = stiff.shape[:2]
    wide = jnp.concatenate([stiff[term].reshape(stored * LANES, LANES) for term in range(terms)], axis=1)
    product = dot(picked, wide).astype(bf16)
    return dot(mixer, jnp.concatenate([product[:, term * LANES:(term + 1) * LANES] for term in range(terms)], axis=0))


def setup_kernel(groups, cols_hbm, coef_hbm, send_hbm, recv_hbm, own_hbm, where_hbm, blocks_ref,
                 g_ref, g2_ref, place_ref, send_ref, recv_ref, own_ref, where_ref, stiff_ref, cols_ref, coef_ref, sems):
    copies = begin(
        sems, (cols_hbm, cols_ref), (coef_hbm, coef_ref), (send_hbm, send_ref), (own_hbm, own_ref),
        (where_hbm, where_ref), (recv_hbm, recv_ref), (last_stored(blocks_ref, stiff_ref), stiff_ref),
    )
    me = lax.axis_index("mode")
    modes = cols_ref.shape[2]
    rows = groups * PAD
    out_mode = lax.broadcasted_iota(i32, (rows, modes), 1)
    spread = one_hot(padded_place(out_mode, groups, modes // groups) == lax.broadcasted_iota(i32, (rows, modes), 0))
    finish(copies[:3])
    modes_dev = modes // groups
    row = lax.broadcasted_iota(i32, (PAD, modes), 0)
    mine = one_hot((lax.broadcasted_iota(i32, (PAD, modes), 1) == row + me * modes_dev) & (row < modes_dev))
    for term in range(cols_ref.shape[0]):
        columns = mixer_columns(term, groups, cols_ref, coef_ref)
        g_ref[:, term * rows:(term + 1) * rows] = dot_t(spread, columns).astype(bf16)
        g2_ref[term * PAD:(term + 1) * PAD, :] = dot_t(mine, columns).astype(bf16)
    place_ref[...] = one_hot(send_ref[...] == lax.broadcasted_iota(i32, place_ref.shape, 0))
    finish(copies[3:])


def first_kernel(groups, v0, v1, v2, v3, g_ref, place_ref, where_ref, stiff_ref,
                 packed_ref, field_ref):
    me = lax.axis_index("mode")
    owned_blocks, _, _, lanes = field_ref.shape
    modes_dev = v0.shape[0]
    field_ref[:, :, modes_dev:, :] = jnp.zeros_like(field_ref[:, :, modes_dev:, :])
    for slot, source in enumerate((v0, v1, v2, v3)):
        group = lax.rem(me + slot, groups)
        for block in range(owned_blocks):
            field_ref[block, group, :modes_dev, :] = source[:, block * lanes:(block + 1) * lanes]
    mixer = g_ref[...]
    stored, out_blocks = where_ref.shape
    parts = []
    for row in range(owned_blocks, out_blocks):
        picked = jnp.concatenate(
            [field_ref[where_ref[c, row]].reshape(groups * PAD, lanes) for c in range(stored)], axis=1
        )
        at = (row - owned_blocks) * stored
        parts.append(mixed_row(picked, stiff_ref[:, at:at + stored], mixer))
    part = jnp.concatenate(parts, axis=1).astype(bf16)
    packed_ref[...] = dot_t(place_ref[...], part).astype(bf16)


def own_rows(rows, sizes, cols_ref, mixed_ref, stiff_ref, copies, own_ref):
    stored = cols_ref.shape[0]
    row = 0
    for size, copy in zip(sizes, copies):
        copy.wait()
        for row in range(row, row + size):
            own_ref[:, row * LANES:(row + 1) * LANES] = block_row(
                row, rows, cols_ref, mixed_ref, stiff_ref[:, row * stored:(row + 1) * stored]
            )
        row += 1


def own_fetch(sizes, stored, blocks_ref, stiff_ref, sems):
    starts = [sum(sizes[:at]) for at in range(len(sizes))]
    parts = [pl.ds(start * stored, size * stored) for start, size in zip(starts, sizes)]
    return begin(sems, *((blocks_ref.at[:, part], stiff_ref.at[:, part]) for part in parts))


def between_kernel(sizes, field_ref, g_ref, where_ref, blocks_ref, own_ref, mixed_ref, stiff_ref, sems):
    copies = own_fetch(sizes, where_ref.shape[0], blocks_ref, stiff_ref, sems)
    mix(stacked(g_ref[...]), field_ref, mixed_ref)
    own_rows(g_ref.shape[0], sizes, where_ref, mixed_ref, stiff_ref, copies, own_ref)


def second_kernel(groups, own_ref, arrived_ref, g2_ref, send_ref, recv_ref, where_ref, blocks_ref,
                  first_ref, mixed_ref, packed_ref, field_ref, r_ref, spread_ref, stiff_ref, sems):
    small = begin(sems, (last_stored(blocks_ref, stiff_ref), stiff_ref))
    me = lax.axis_index("mode")
    owned = own_ref.shape[1]
    receive_table(recv_ref, r_ref)
    arrived = arrived_ref[...].astype(f32).T.astype(bf16)
    for at in range(0, owned, WIDTH):
        total = own_ref[:, at:at + WIDTH] + dot(arrived, r_ref[:, at:at + WIDTH])
        total = total.astype(bf16)
        for part in range(0, WIDTH, LANES):
            field_ref[(at + part) // LANES] = total[:, part:part + LANES].reshape(groups, PAD, LANES)
    mix(g2_ref[...], field_ref, mixed_ref)
    spread_ref[...] = jnp.zeros_like(spread_ref)
    width = send_ref.shape[1]
    send = send_ref[...]
    lines = lax.broadcasted_iota(i32, (packed_ref.shape[0], width), 0) * QUARTERS
    place = jnp.concatenate([one_hot(send == lines + quarter) for quarter in range(QUARTERS)], axis=1)
    finish(small)
    part = interface_part(PAD, where_ref, mixed_ref, stiff_ref)
    for quarter in range(QUARTERS):
        spread_ref[quarter * PAD:(quarter + 1) * PAD, quarter * width:(quarter + 1) * width] = part
    packed_ref[...] = dot_t(place, spread_ref[...]).astype(bf16)
    for block in range(field_ref.shape[0]):
        first_ref[:, block * LANES:(block + 1) * LANES] = field_ref[block, me, :first_ref.shape[0], :]


def own_kernel(sizes, where_ref, mixed_ref, blocks_ref, own_ref, stiff_ref, sems):
    copies = own_fetch(sizes, where_ref.shape[0], blocks_ref, stiff_ref, sems)
    own_rows(PAD, sizes, where_ref, mixed_ref, stiff_ref, copies, own_ref)


def last_kernel(own_ref, arrived_ref, recv_ref, out_ref, slots_ref, r_ref):
    receive_table(recv_ref, r_ref)
    arrived = arrived_ref[...].astype(f32)
    lines = arrived.shape[0]
    for quarter in range(QUARTERS):
        turned = pltpu.roll(arrived, (QUARTERS - quarter) % QUARTERS * PAD, 1)
        slots_ref[pl.ds(quarter, lines, stride=QUARTERS), :] = turned
    by_slot = slots_ref[...].T[:PAD, :].astype(bf16)
    for at in range(0, own_ref.shape[1], WIDTH):
        total = own_ref[:, at:at + WIDTH] + dot(by_slot, r_ref[:, at:at + WIDTH])
        out_ref[:, at:at + WIDTH] = total.astype(bf16)[:out_ref.shape[0], :]


def uneven(rows):
    last, rest = rows // 8, rows - rows // 8
    third = -(-rest // 3)
    return tuple(size for size in (third, third, rest - 2 * third, last) if size)


def local(groups, peers, modes_in, blocks, block_cols, send_slot, recv_row, mix_cols, mix_coef):
    terms, all_stored, blk, _ = blocks.shape
    out_blocks, stored = block_cols.shape
    modes_dev, owned = modes_in.shape
    owned_blocks = owned // blk
    interface = send_slot.shape[0]
    slots = recv_row.shape[0]
    cap = slots // peers
    rows = groups * PAD
    lines = slots // QUARTERS
    Shape, dma = jax.ShapeDtypeStruct, pltpu.SemaphoreType.DMA

    def pin(x):
        return pltpu.with_memory_space_constraint(x, pltpu.HBM)

    others = {
        s: lax.ppermute(modes_in, "mode", [((to + s) % groups, to) for to in range(groups)])
        for s in (2, 1, 3)
    }
    blocks = pin(blocks)
    where = pin(block_cols.T)
    mix_cols, mix_coef = pin(mix_cols.transpose(0, 2, 1)), pin(mix_coef.transpose(0, 2, 1))
    send, recv = pin(send_slot.reshape(1, interface)), pin(recv_row.reshape(1, slots))
    tables = [pltpu.VMEM(mix_cols.shape, i32), pltpu.VMEM(mix_coef.shape, f32)]
    if_blocks = (terms, (out_blocks - owned_blocks) * stored, blk, blk)
    own_scratch = pltpu.VMEM((terms, owned_blocks * stored, blk, blk), bf16)
    field_shape, mixer_shape = (owned_blocks, groups, PAD, blk), (rows, terms * rows)
    field_scratch = pltpu.VMEM(field_shape, bf16)
    block_flops = 2 * terms * stored * blk * blk
    wide, narrow = (owned_blocks, terms * rows, blk), (owned_blocks, terms * PAD, blk)

    g, g2, place, send, recv, own_field, where, stiff = call(
        functools.partial(setup_kernel, groups),
        [Shape(mixer_shape, bf16), Shape((terms * PAD, rows), bf16), Shape((slots, interface), bf16), Shape(send.shape, i32),
         Shape(recv.shape, i32), Shape((modes_dev, owned), bf16), Shape(where.shape, i32), Shape(if_blocks, bf16)],
        [mix_cols, mix_coef, send, recv, pin(modes_in), where, blocks], [HBM] * 7, [VMEM] * 8, flops=10**6,
        scratch=[*tables, dma((7,))],
    )
    packed, field = call(
        functools.partial(first_kernel, groups),
        [Shape((slots, rows), bf16), Shape(field_shape, bf16)],
        [own_field, others[1], others[2], others[3], g, place, where, stiff],
        [VMEM] * 6 + [SMEM, VMEM], [VMEM] * 2, flops=block_flops * (out_blocks - owned_blocks) * rows,
    )
    arrived = lax.all_to_all(packed.reshape(peers, cap, rows), "space", split_axis=0, concat_axis=0, tiled=True)
    sizes = uneven(owned_blocks)
    own = call(
        functools.partial(between_kernel, sizes), [Shape((rows, owned), f32)],
        [field, g, where, blocks], [VMEM] * 2 + [SMEM, HBM], [VMEM], flops=block_flops * owned_blocks * rows,
        scratch=[pltpu.VMEM(wide, bf16), own_scratch, dma((len(sizes),))],
    )[0]
    first_apply, mixed2, packed2 = call(
        functools.partial(second_kernel, groups),
        [Shape((modes_dev, owned), bf16), Shape(narrow, bf16), Shape((lines, QUARTERS * PAD), bf16)],
        [own, arrived.reshape(slots, rows), g2, send, recv, where, blocks],
        [VMEM] * 5 + [SMEM, HBM], [VMEM] * 3, flops=2 * slots * rows * owned,
        scratch=[field_scratch, pltpu.VMEM((slots, owned), bf16), pltpu.VMEM((QUARTERS * PAD, QUARTERS * interface), bf16),
                 pltpu.VMEM(if_blocks, bf16), dma((1,))],
    )
    arrived2 = lax.all_to_all(
        packed2.reshape(peers, cap // QUARTERS, QUARTERS * PAD), "space", split_axis=0, concat_axis=0, tiled=True
    )
    own2 = call(
        functools.partial(own_kernel, sizes), [Shape((PAD, owned), f32)],
        [where, mixed2, blocks], [SMEM, VMEM, HBM], [VMEM], flops=block_flops * owned_blocks * PAD,
        scratch=[own_scratch, dma((len(sizes),))],
    )[0]
    second_apply = call(
        last_kernel, [Shape((modes_dev, owned), bf16)],
        [own2, arrived2.reshape(lines, QUARTERS * PAD), recv], [VMEM] * 3, [VMEM], flops=2 * slots * PAD * owned,
        scratch=[pltpu.VMEM((slots, QUARTERS * PAD), f32), pltpu.VMEM((slots, owned), bf16)],
    )[0]
    return (first_apply, second_apply)


def solution(mesh):
    in_specs = (
        P("mode", "space"),
        P(None, "space", None, None),
        P("space", None),
        P("space"),
        P("space"),
        P(),
        P(),
    )
    out_specs = (P("mode", "space"), P("mode", "space"))
    body = functools.partial(local, mesh.shape["mode"], mesh.shape["space"])
    return jax.shard_map(body, mesh=mesh, in_specs=in_specs, out_specs=out_specs, check_vma=False)
```

```python
import functools
import math

import jax
import jax.numpy as jnp
from jax import lax
from jax.experimental import pallas as pl
from jax.experimental.pallas import tpu as pltpu
from jax.sharding import PartitionSpec as P

LANES = 128
PAD = 32
QUARTERS = 4
WIDTH = 256

VMEM = pl.BlockSpec(memory_space=pltpu.VMEM)
SMEM = pl.BlockSpec(memory_space=pltpu.SMEM)
HBM = pl.BlockSpec(memory_space=pltpu.HBM)
VMEM_LIMIT = 32 * 1024 * 1024
bf16, f32, i32 = jnp.bfloat16, jnp.float32, jnp.int32


def call(kernel, outs, ins, in_specs, out_specs, flops, scratch=()):
    moved = sum(math.prod(a.shape) * jnp.dtype(a.dtype).itemsize for a in [*outs, *ins])
    return pl.pallas_call(
        kernel,
        out_shape=outs,
        in_specs=in_specs,
        out_specs=out_specs,
        scratch_shapes=scratch,
        compiler_params=pltpu.CompilerParams(vmem_limit_bytes=VMEM_LIMIT),
        cost_estimate=pl.CostEstimate(flops=flops, bytes_accessed=moved, transcendentals=0),
    )(*ins)


def begin(sems, *pairs):
    copies = [pltpu.make_async_copy(source, target, sems.at[at]) for at, (source, target) in enumerate(pairs)]
    for copy in copies:
        copy.start()
    return copies


def finish(copies):
    for copy in copies:
        copy.wait()


def one_hot(hit):
    return jnp.where(hit, 1.0, 0.0).astype(bf16)


def dot(a, b):
    return jnp.dot(a, b, preferred_element_type=f32)


def dot_t(a, b):
    return lax.dot_general(a, b, (((1,), (1,)), ((), ())), preferred_element_type=f32)


def padded_place(modes, groups, modes_dev):
    place = modes
    for group in range(1, groups):
        place += jnp.where(modes >= group * modes_dev, PAD - modes_dev, 0)
    return place


def mixer_columns(term, groups, cols_ref, coef_ref):
    modes = cols_ref.shape[2]
    cols = cols_ref[term]
    place = jnp.where(cols < modes, padded_place(cols, groups, modes // groups), -1)
    coef = coef_ref[term]
    want = lax.broadcasted_iota(i32, (groups * PAD, modes), 0)
    total = jnp.zeros(want.shape, f32)
    for slot in range(cols.shape[0]):
        total += jnp.where(place[slot:slot + 1, :] == want, coef[slot:slot + 1, :], 0.0)
    return total.astype(bf16)


def by_quarter(rows_ref, quarter):
    return rows_ref[pl.ds(quarter, rows_ref.shape[0] // QUARTERS, stride=QUARTERS), :]


def receive_table(recv_ref, r_ref, turned_ref):
    slots = recv_ref.shape[1]
    turned_ref[...] = jnp.broadcast_to(recv_ref[...].astype(f32), (LANES, slots)).T
    lanes = lax.broadcasted_iota(i32, (slots // QUARTERS, LANES), 1)
    for quarter in range(QUARTERS):
        offset = by_quarter(turned_ref, quarter).astype(i32) - lanes
        at = slice(quarter * slots // QUARTERS, (quarter + 1) * slots // QUARTERS)
        for block in range(r_ref.shape[0]):
            r_ref[block, at, :] = one_hot(offset == block * LANES)


def block_row(row, rows, cols_ref, mixed_ref, stiff):
    terms, stored = stiff.shape[:2]
    picked = jnp.concatenate(
        [
            mixed_ref[cols_ref[c, row], term * rows:(term + 1) * rows, :]
            for term in range(terms)
            for c in range(stored)
        ],
        axis=1,
    )
    return dot(picked, stiff.reshape(terms * stored * LANES, LANES))


def mix(mixer, field_ref, mixed_ref):
    blocks, groups, pad, lanes = field_ref.shape
    for block in range(0, blocks, 2):
        pair = [field_ref[block + part].reshape(groups * pad, lanes) for part in range(2)]
        mixed = dot(mixer, jnp.concatenate(pair, axis=1)).astype(bf16)
        for part in range(2):
            mixed_ref[block + part] = mixed[:, part * lanes:(part + 1) * lanes]


def stacked(wide):
    return jnp.concatenate([wide[:, at:at + LANES] for at in range(0, wide.shape[1], LANES)], axis=0)


def last_stored(blocks_ref, stiff_ref):
    count = stiff_ref.shape[1]
    return blocks_ref.at[:, pl.ds(blocks_ref.shape[1] - count, count)]


def mixed_row(picked, stiff, mixer):
    terms, stored = stiff.shape[:2]
    wide = jnp.concatenate([stiff[term].reshape(stored * LANES, LANES) for term in range(terms)], axis=1)
    product = dot(picked, wide).astype(bf16)
    return dot(mixer, jnp.concatenate([product[:, term * LANES:(term + 1) * LANES] for term in range(terms)], axis=0))


def setup_kernel(groups, cols_hbm, coef_hbm, send_hbm, recv_hbm, own_hbm, where_hbm, blocks_ref,
                 g_ref, g2_ref, place_ref, send_ref, recv_ref, own_ref, where_ref, stiff_ref, cols_ref, coef_ref, sems):
    copies = begin(
        sems, (cols_hbm, cols_ref), (coef_hbm, coef_ref), (send_hbm, send_ref), (own_hbm, own_ref),
        (where_hbm, where_ref), (recv_hbm, recv_ref), (last_stored(blocks_ref, stiff_ref), stiff_ref),
    )
    me = lax.axis_index("mode")
    modes = cols_ref.shape[2]
    rows = groups * PAD
    out_mode = lax.broadcasted_iota(i32, (rows, modes), 1)
    spread = one_hot(padded_place(out_mode, groups, modes // groups) == lax.broadcasted_iota(i32, (rows, modes), 0))
    finish(copies[:3])
    modes_dev = modes // groups
    row = lax.broadcasted_iota(i32, (PAD, modes), 0)
    mine = one_hot((lax.broadcasted_iota(i32, (PAD, modes), 1) == row + me * modes_dev) & (row < modes_dev))
    for term in range(cols_ref.shape[0]):
        columns = mixer_columns(term, groups, cols_ref, coef_ref)
        g_ref[:, term * rows:(term + 1) * rows] = dot_t(spread, columns).astype(bf16)
        g2_ref[term * PAD:(term + 1) * PAD, :] = dot_t(mine, columns).astype(bf16)
    place_ref[...] = one_hot(send_ref[...] == lax.broadcasted_iota(i32, place_ref.shape, 0))
    finish(copies[3:])


def first_kernel(groups, v0, v1, v2, v3, g_ref, place_ref, where_ref, stiff_ref,
                 packed_ref, field_hbm, g_hbm, field_ref, sems):
    copies = begin(sems, (g_ref, g_hbm))
    me = lax.axis_index("mode")
    owned_blocks, _, _, lanes = field_ref.shape
    modes_dev = v0.shape[0]
    field_ref[:, :, modes_dev:, :] = jnp.zeros_like(field_ref[:, :, modes_dev:, :])
    for slot, source in enumerate((v0, v1, v2, v3)):
        group = lax.rem(me + slot, groups)
        for block in range(owned_blocks):
            field_ref[block, group, :modes_dev, :] = source[:, block * lanes:(block + 1) * lanes]
    copies += begin(sems.at[pl.ds(1, 1)], (field_ref, field_hbm))
    mixer = g_ref[...]
    stored, out_blocks = where_ref.shape
    parts = []
    for row in range(owned_blocks, out_blocks):
        picked = jnp.concatenate(
            [field_ref[where_ref[c, row]].reshape(groups * PAD, lanes) for c in range(stored)], axis=1
        )
        at = (row - owned_blocks) * stored
        parts.append(mixed_row(picked, stiff_ref[:, at:at + stored], mixer))
    part = jnp.concatenate(parts, axis=1).astype(bf16)
    packed_ref[...] = dot_t(place_ref[...], part).astype(bf16)
    finish(copies)


def own_fetch(steps, stored, blocks_ref, stiff_ref, sems):
    count = stiff_ref.shape[1] // steps
    parts = [pl.ds(step * count, count) for step in range(steps)]
    return begin(sems, *((blocks_ref.at[:, part], stiff_ref.at[:, part]) for part in parts))


def between_kernel(steps, field_hbm, g_hbm, recv_ref, where_ref, blocks_ref,
                   own_ref, r_ref, field_ref, g_ref, mixed_ref, stiff_ref, turned_ref, sems):
    near = begin(sems, (field_hbm, field_ref), (g_hbm, g_ref))
    stored = where_ref.shape[0]
    copies = own_fetch(steps, stored, blocks_ref, stiff_ref, sems.at[pl.ds(len(near), steps)])
    receive_table(recv_ref, r_ref, turned_ref)
    finish(near)
    mix(stacked(g_ref[...]), field_ref, mixed_ref)
    per = own_ref.shape[0] // steps
    for step in range(steps):
        copies[step].wait()
        for row in range(step * per, (step + 1) * per):
            own_ref[row] = block_row(
                row, own_ref.shape[1], where_ref, mixed_ref, stiff_ref[:, row * stored:(row + 1) * stored]
            )


def second_kernel(own_ref, arrived_ref, r_ref, g2_ref, send_ref, where_ref, blocks_ref,
                  packed_ref, turned_hbm, turned_ref, lines_ref, spread_ref, stiff_ref, sems):
    near = begin(sems, (last_stored(blocks_ref, stiff_ref), stiff_ref))
    lines_ref[...] = arrived_ref[...].astype(f32)
    turned = jnp.concatenate([by_quarter(lines_ref, quarter).T.astype(bf16) for quarter in range(QUARTERS)], axis=1)
    turned_ref[...] = turned
    keeps = begin(sems.at[pl.ds(len(near), 1)], (turned_ref, turned_hbm))
    stored, out_blocks = where_ref.shape
    owned_blocks = own_ref.shape[0]
    terms = stiff_ref.shape[0]
    mixer = g2_ref[...]
    picks = []
    for row in range(owned_blocks, out_blocks):
        columns = [where_ref[c, row] for c in range(stored)]
        base = jnp.concatenate([own_ref[column] for column in columns], axis=1)
        table = jnp.concatenate([r_ref[column] for column in columns], axis=1)
        field = (base + dot(turned, table)).astype(bf16)
        mixed = dot(mixer, field).astype(bf16)
        picks.append(jnp.concatenate([mixed[term * PAD:(term + 1) * PAD, :] for term in range(terms)], axis=1))
    width = send_ref.shape[1]
    lines = lax.broadcasted_iota(i32, (packed_ref.shape[0], width), 0) * QUARTERS
    place = jnp.concatenate([one_hot(send_ref[...] == lines + quarter) for quarter in range(QUARTERS)], axis=1)
    spread_ref[...] = jnp.zeros_like(spread_ref)
    finish(near)
    depth = terms * stored * LANES
    part = jnp.concatenate(
        [dot(picked, stiff_ref[:, at * stored:(at + 1) * stored].reshape(depth, LANES)) for at, picked in enumerate(picks)],
        axis=1,
    ).astype(bf16)
    for quarter in range(QUARTERS):
        spread_ref[quarter * PAD:(quarter + 1) * PAD, quarter * width:(quarter + 1) * width] = part
    packed_ref[...] = dot_t(place, spread_ref[...]).astype(bf16)
    finish(keeps)


def own_kernel(groups, steps, where_ref, recv_ref, g2_ref, turned_hbm, own_ref, blocks_ref,
               first_ref, own2_ref, r_ref, turned_ref, field_ref, mixed_ref, stiff_ref, rows_ref, sems):
    stored = where_ref.shape[0]
    near = begin(sems, (turned_hbm, turned_ref))
    copies = own_fetch(steps, stored, blocks_ref, stiff_ref, sems.at[pl.ds(len(near), steps)])
    me = lax.axis_index("mode")
    receive_table(recv_ref, r_ref, rows_ref)
    owned_blocks, _, lanes = own_ref.shape
    finish(near)
    turned = turned_ref[...]
    for block in range(0, owned_blocks, 2):
        table = jnp.concatenate([r_ref[block], r_ref[block + 1]], axis=1)
        base = jnp.concatenate([own_ref[block], own_ref[block + 1]], axis=1)
        field = (base + dot(turned, table)).astype(bf16)
        for part in range(2):
            field_ref[block + part] = field[:, part * lanes:(part + 1) * lanes].reshape(groups, PAD, lanes)
    mix(g2_ref[...], field_ref, mixed_ref)
    for block in range(owned_blocks):
        first_ref[:, block * lanes:(block + 1) * lanes] = field_ref[block, me, :first_ref.shape[0], :]
    per = owned_blocks // steps
    for step in range(steps):
        copies[step].wait()
        for row in range(step * per, (step + 1) * per):
            own2_ref[:, row * lanes:(row + 1) * lanes] = block_row(
                row, PAD, where_ref, mixed_ref, stiff_ref[:, row * stored:(row + 1) * stored]
            )


def last_kernel(own_ref, arrived_ref, r_ref, out_ref):
    turned = arrived_ref[...].astype(f32).T.astype(bf16)
    by_slot = jnp.concatenate([turned[quarter * PAD:(quarter + 1) * PAD, :] for quarter in range(QUARTERS)], axis=1)
    for block in range(0, r_ref.shape[0], 2):
        at = slice(block * LANES, (block + 2) * LANES)
        table = jnp.concatenate([r_ref[block], r_ref[block + 1]], axis=1)
        total = own_ref[:, at] + dot(by_slot, table)
        out_ref[:, at] = total.astype(bf16)[:out_ref.shape[0], :]


def local(groups, peers, modes_in, blocks, block_cols, send_slot, recv_row, mix_cols, mix_coef):
    terms, all_stored, blk, _ = blocks.shape
    out_blocks, stored = block_cols.shape
    modes_dev, owned = modes_in.shape
    owned_blocks = owned // blk
    interface = send_slot.shape[0]
    slots = recv_row.shape[0]
    cap = slots // peers
    rows = groups * PAD
    lines = slots // QUARTERS
    Shape, dma = jax.ShapeDtypeStruct, pltpu.SemaphoreType.DMA

    def pin(x):
        return pltpu.with_memory_space_constraint(x, pltpu.HBM)

    others = {
        s: lax.ppermute(modes_in, "mode", [((to + s) % groups, to) for to in range(groups)])
        for s in (2, 1, 3)
    }
    blocks = pin(blocks)
    where = pin(block_cols.T)
    mix_cols, mix_coef = pin(mix_cols.transpose(0, 2, 1)), pin(mix_coef.transpose(0, 2, 1))
    send, recv = pin(send_slot.reshape(1, interface)), pin(recv_row.reshape(1, slots))
    tables = [pltpu.VMEM(mix_cols.shape, i32), pltpu.VMEM(mix_coef.shape, f32)]
    if_blocks = (terms, (out_blocks - owned_blocks) * stored, blk, blk)
    own_scratch = pltpu.VMEM((terms, owned_blocks * stored, blk, blk), bf16)
    field_shape, mixer_shape = (owned_blocks, groups, PAD, blk), (rows, terms * rows)
    field_scratch = pltpu.VMEM(field_shape, bf16)
    block_flops = 2 * terms * stored * blk * blk
    wide, narrow = (owned_blocks, terms * rows, blk), (owned_blocks, terms * PAD, blk)

    own_shape, table_shape = (owned_blocks, rows, blk), (owned_blocks, slots, blk)
    turned_scratch = pltpu.VMEM((slots, LANES), f32)

    g, g2, place, send, recv, own_field, where, stiff = call(
        functools.partial(setup_kernel, groups),
        [Shape(mixer_shape, bf16), Shape((terms * PAD, rows), bf16), Shape((slots, interface), bf16), Shape(send.shape, i32),
         Shape(recv.shape, i32), Shape((modes_dev, owned), bf16), Shape(where.shape, i32), Shape(if_blocks, bf16)],
        [mix_cols, mix_coef, send, recv, pin(modes_in), where, blocks], [HBM] * 7, [VMEM] * 8, flops=10**6,
        scratch=[*tables, dma((7,))],
    )
    packed, field, g_kept = call(
        functools.partial(first_kernel, groups),
        [Shape((slots, rows), bf16), pltpu.HBM(field_shape, bf16), pltpu.HBM(mixer_shape, bf16)],
        [own_field, others[1], others[2], others[3], g, place, where, stiff],
        [VMEM] * 6 + [SMEM, VMEM], [VMEM, HBM, HBM],
        flops=block_flops * (out_blocks - owned_blocks) * rows, scratch=[field_scratch, dma((2,))],
    )
    arrived = lax.all_to_all(packed.reshape(peers, cap, rows), "space", split_axis=0, concat_axis=0, tiled=True)
    steps = owned_blocks // 2
    own, r = call(
        functools.partial(between_kernel, steps), [Shape(own_shape, f32), Shape(table_shape, bf16)],
        [pin(field), pin(g_kept), recv, where, blocks], [HBM, HBM, VMEM, SMEM, HBM], [VMEM] * 2,
        flops=block_flops * owned_blocks * rows,
        scratch=[field_scratch, pltpu.VMEM(mixer_shape, bf16), pltpu.VMEM(wide, bf16), own_scratch, turned_scratch,
                 dma((2 + steps,))],
    )
    packed2, turned = call(
        second_kernel, [Shape((lines, QUARTERS * PAD), bf16), pltpu.HBM((rows, slots), bf16)],
        [own, arrived.reshape(slots, rows), r, g2, send, where, blocks], [VMEM] * 5 + [SMEM, HBM], [VMEM, HBM],
        flops=2 * slots * rows * owned,
        scratch=[pltpu.VMEM((rows, slots), bf16), turned_scratch, pltpu.VMEM((QUARTERS * PAD, QUARTERS * interface), bf16), pltpu.VMEM(if_blocks, bf16), dma((2,))],
    )
    arrived2 = lax.all_to_all(
        packed2.reshape(peers, cap // QUARTERS, QUARTERS * PAD), "space", split_axis=0, concat_axis=0, tiled=True
    )
    first_apply, own2, r2 = call(
        functools.partial(own_kernel, groups, steps),
        [Shape((modes_dev, owned), bf16), Shape((PAD, owned), f32), Shape(table_shape, bf16)],
        [where, recv, g2, pin(turned), own, blocks], [SMEM, VMEM, VMEM, HBM, VMEM, HBM], [VMEM] * 3,
        flops=block_flops * owned_blocks * PAD,
        scratch=[pltpu.VMEM((rows, slots), bf16), field_scratch, pltpu.VMEM(narrow, bf16), own_scratch, turned_scratch,
                 dma((1 + steps,))],
    )
    second_apply = call(
        last_kernel, [Shape((modes_dev, owned), bf16)],
        [own2, arrived2.reshape(lines, QUARTERS * PAD), r2], [VMEM] * 3, [VMEM], flops=2 * slots * PAD * owned,
    )[0]
    return (first_apply, second_apply)


def solution(mesh):
    in_specs = (
        P("mode", "space"),
        P(None, "space", None, None),
        P("space", None),
        P("space"),
        P("space"),
        P(),
        P(),
    )
    out_specs = (P("mode", "space"), P("mode", "space"))
    body = functools.partial(local, mesh.shape["mode"], mesh.shape["space"])
    return jax.shard_map(body, mesh=mesh, in_specs=in_specs, out_specs=out_specs, check_vma=False)
```

```python
import functools
import math

import jax
import jax.numpy as jnp
from jax import lax
from jax.experimental import pallas as pl
from jax.experimental.pallas import tpu as pltpu
from jax.sharding import PartitionSpec as P

LANES = 128
PAD = 32
QUARTERS = 4
WIDTH = 256

VMEM = pl.BlockSpec(memory_space=pltpu.VMEM)
SMEM = pl.BlockSpec(memory_space=pltpu.SMEM)
HBM = pl.BlockSpec(memory_space=pltpu.HBM)
VMEM_LIMIT = 32 * 1024 * 1024
bf16, f32, i32 = jnp.bfloat16, jnp.float32, jnp.int32


def call(kernel, outs, ins, in_specs, out_specs, flops, scratch=()):
    moved = sum(math.prod(a.shape) * jnp.dtype(a.dtype).itemsize for a in [*outs, *ins])
    return pl.pallas_call(
        kernel,
        out_shape=outs,
        in_specs=in_specs,
        out_specs=out_specs,
        scratch_shapes=scratch,
        compiler_params=pltpu.CompilerParams(vmem_limit_bytes=VMEM_LIMIT),
        cost_estimate=pl.CostEstimate(flops=flops, bytes_accessed=moved, transcendentals=0),
    )(*ins)


def begin(sems, *pairs):
    copies = [pltpu.make_async_copy(source, target, sems.at[at]) for at, (source, target) in enumerate(pairs)]
    for copy in copies:
        copy.start()
    return copies


def finish(copies):
    for copy in copies:
        copy.wait()


def one_hot(hit):
    return jnp.where(hit, 1.0, 0.0).astype(bf16)


def dot(a, b):
    return jnp.dot(a, b, preferred_element_type=f32)


def dot_t(a, b):
    return lax.dot_general(a, b, (((1,), (1,)), ((), ())), preferred_element_type=f32)


def padded_place(modes, groups, modes_dev):
    place = modes
    for group in range(1, groups):
        place += jnp.where(modes >= group * modes_dev, PAD - modes_dev, 0)
    return place


def mixer_columns(term, groups, cols_ref, coef_ref):
    modes = cols_ref.shape[2]
    cols = cols_ref[term]
    place = jnp.where(cols < modes, padded_place(cols, groups, modes // groups), -1)
    coef = coef_ref[term]
    want = lax.broadcasted_iota(i32, (groups * PAD, modes), 0)
    total = jnp.zeros(want.shape, f32)
    for slot in range(cols.shape[0]):
        total += jnp.where(place[slot:slot + 1, :] == want, coef[slot:slot + 1, :], 0.0)
    return total.astype(bf16)


def receive_table(recv_ref, r_ref):
    slots = recv_ref.shape[1]
    lanes = lax.broadcasted_iota(i32, (LANES, LANES), 1)
    for start in range(0, slots, LANES):
        at = slice(start, start + LANES)
        offset = jnp.broadcast_to(recv_ref[:, at].astype(f32), (LANES, LANES)).T.astype(i32) - lanes
        for block in range(r_ref.shape[0]):
            r_ref[block, at, :] = one_hot(offset == block * LANES)


def block_row(row, rows, cols_ref, mixed_ref, stiff):
    terms, stored = stiff.shape[:2]
    picked = jnp.concatenate(
        [
            mixed_ref[cols_ref[c, row], term * rows:(term + 1) * rows, :]
            for term in range(terms)
            for c in range(stored)
        ],
        axis=1,
    )
    return dot(picked, stiff.reshape(terms * stored * LANES, LANES))


def mix(mixer, field_ref, mixed_ref):
    blocks, groups, pad, lanes = field_ref.shape
    for block in range(0, blocks, 2):
        pair = [field_ref[block + part].reshape(groups * pad, lanes) for part in range(2)]
        mixed = dot(mixer, jnp.concatenate(pair, axis=1)).astype(bf16)
        for part in range(2):
            mixed_ref[block + part] = mixed[:, part * lanes:(part + 1) * lanes]


def stacked(wide):
    return jnp.concatenate([wide[:, at:at + LANES] for at in range(0, wide.shape[1], LANES)], axis=0)


def last_stored(blocks_ref, stiff_ref):
    count = stiff_ref.shape[1]
    return blocks_ref.at[:, pl.ds(blocks_ref.shape[1] - count, count)]


def mixed_row(picked, stiff, mixer):
    terms, stored = stiff.shape[:2]
    wide = jnp.concatenate([stiff[term].reshape(stored * LANES, LANES) for term in range(terms)], axis=1)
    product = dot(picked, wide).astype(bf16)
    return dot(mixer, jnp.concatenate([product[:, term * LANES:(term + 1) * LANES] for term in range(terms)], axis=0))


def setup_kernel(groups, cols_hbm, coef_hbm, send_hbm, recv_hbm, own_hbm, where_hbm, blocks_ref,
                 g_ref, g2_ref, place_ref, send_ref, recv_ref, own_ref, where_ref, stiff_ref, cols_ref, coef_ref, sems):
    copies = begin(
        sems, (cols_hbm, cols_ref), (coef_hbm, coef_ref), (send_hbm, send_ref), (own_hbm, own_ref),
        (where_hbm, where_ref), (recv_hbm, recv_ref), (last_stored(blocks_ref, stiff_ref), stiff_ref),
    )
    me = lax.axis_index("mode")
    modes = cols_ref.shape[2]
    rows = groups * PAD
    out_mode = lax.broadcasted_iota(i32, (rows, modes), 1)
    spread = one_hot(padded_place(out_mode, groups, modes // groups) == lax.broadcasted_iota(i32, (rows, modes), 0))
    finish(copies[:3])
    modes_dev = modes // groups
    row = lax.broadcasted_iota(i32, (PAD, modes), 0)
    mine = one_hot((lax.broadcasted_iota(i32, (PAD, modes), 1) == row + me * modes_dev) & (row < modes_dev))
    for term in range(cols_ref.shape[0]):
        columns = mixer_columns(term, groups, cols_ref, coef_ref)
        g_ref[:, term * rows:(term + 1) * rows] = dot_t(spread, columns).astype(bf16)
        g2_ref[term * PAD:(term + 1) * PAD, :] = dot_t(mine, columns).astype(bf16)
    place_ref[...] = one_hot(send_ref[...] == lax.broadcasted_iota(i32, place_ref.shape, 0))
    finish(copies[3:])


def first_kernel(groups, v0, v1, v2, v3, g_ref, place_ref, where_ref, stiff_ref,
                 packed_ref, field_hbm, g_hbm, field_ref, sems):
    copies = begin(sems, (g_ref, g_hbm))
    me = lax.axis_index("mode")
    owned_blocks, _, _, lanes = field_ref.shape
    modes_dev = v0.shape[0]
    field_ref[:, :, modes_dev:, :] = jnp.zeros_like(field_ref[:, :, modes_dev:, :])
    for slot, source in enumerate((v0, v1, v2, v3)):
        group = lax.rem(me + slot, groups)
        for block in range(owned_blocks):
            field_ref[block, group, :modes_dev, :] = source[:, block * lanes:(block + 1) * lanes]
    copies += begin(sems.at[pl.ds(1, 1)], (field_ref, field_hbm))
    mixer = g_ref[...]
    stored, out_blocks = where_ref.shape
    parts = []
    for row in range(owned_blocks, out_blocks):
        picked = jnp.concatenate(
            [field_ref[where_ref[c, row]].reshape(groups * PAD, lanes) for c in range(stored)], axis=1
        )
        at = (row - owned_blocks) * stored
        parts.append(mixed_row(picked, stiff_ref[:, at:at + stored], mixer))
    part = jnp.concatenate(parts, axis=1).astype(bf16)
    packed_ref[...] = dot_t(place_ref[...], part).astype(bf16)
    finish(copies)


def own_fetch(steps, stored, blocks_ref, stiff_ref, sems):
    count = stiff_ref.shape[1] // steps
    parts = [pl.ds(step * count, count) for step in range(steps)]
    return begin(sems, *((blocks_ref.at[:, part], stiff_ref.at[:, part]) for part in parts))


def between_kernel(steps, field_hbm, g_hbm, recv_ref, where_ref, blocks_ref,
                   own_ref, r_ref, field_ref, g_ref, mixed_ref, stiff_ref, sems):
    near = begin(sems, (field_hbm, field_ref), (g_hbm, g_ref))
    stored = where_ref.shape[0]
    copies = own_fetch(steps, stored, blocks_ref, stiff_ref, sems.at[pl.ds(len(near), steps)])
    receive_table(recv_ref, r_ref)
    finish(near)
    mix(stacked(g_ref[...]), field_ref, mixed_ref)
    per = own_ref.shape[0] // steps
    for step in range(steps):
        copies[step].wait()
        for row in range(step * per, (step + 1) * per):
            own_ref[row] = block_row(
                row, own_ref.shape[1], where_ref, mixed_ref, stiff_ref[:, row * stored:(row + 1) * stored]
            )


def second_kernel(own_ref, arrived_ref, r_ref, g2_ref, send_ref, where_ref, blocks_ref,
                  packed_ref, turned_hbm, turned_ref, spread_ref, stiff_ref, sems):
    near = begin(sems, (last_stored(blocks_ref, stiff_ref), stiff_ref))
    turned = arrived_ref[...].astype(f32).T.astype(bf16)
    turned_ref[...] = turned
    keeps = begin(sems.at[pl.ds(len(near), 1)], (turned_ref, turned_hbm))
    stored, out_blocks = where_ref.shape
    owned_blocks = own_ref.shape[0]
    terms = stiff_ref.shape[0]
    mixer = jnp.concatenate([g2_ref[term * PAD:(term + 1) * PAD, :] for term in range(terms)], axis=1)
    picks = []
    for row in range(owned_blocks, out_blocks):
        columns = [where_ref[c, row] for c in range(stored)]
        base = jnp.concatenate([own_ref[column] for column in columns], axis=1)
        table = jnp.concatenate([r_ref[column] for column in columns], axis=1)
        picks.append((base + dot(turned, table)).astype(bf16))
    width = send_ref.shape[1]
    lines = lax.broadcasted_iota(i32, (packed_ref.shape[0], width), 0) * QUARTERS
    place = jnp.concatenate([one_hot(send_ref[...] == lines + quarter) for quarter in range(QUARTERS)], axis=1)
    spread_ref[...] = jnp.zeros_like(spread_ref)
    finish(near)
    part = jnp.concatenate(
        [mixed_row(picked, stiff_ref[:, at * stored:(at + 1) * stored], mixer) for at, picked in enumerate(picks)], axis=1
    ).astype(bf16)
    for quarter in range(QUARTERS):
        spread_ref[quarter * PAD:(quarter + 1) * PAD, quarter * width:(quarter + 1) * width] = part
    packed_ref[...] = dot_t(place, spread_ref[...]).astype(bf16)
    finish(keeps)


def own_kernel(groups, steps, where_ref, recv_ref, g2_ref, turned_hbm, own_ref, blocks_ref,
               first_hbm, own2_ref, r_ref, turned_ref, first_ref, field_ref, mixed_ref, stiff_ref, sems):
    stored = where_ref.shape[0]
    near = begin(sems, (turned_hbm, turned_ref))
    copies = own_fetch(steps, stored, blocks_ref, stiff_ref, sems.at[pl.ds(len(near), steps)])
    me = lax.axis_index("mode")
    receive_table(recv_ref, r_ref)
    owned_blocks, _, lanes = own_ref.shape
    finish(near)
    turned = turned_ref[...]
    for block in range(0, owned_blocks, 2):
        table = jnp.concatenate([r_ref[block], r_ref[block + 1]], axis=1)
        base = jnp.concatenate([own_ref[block], own_ref[block + 1]], axis=1)
        field = (base + dot(turned, table)).astype(bf16)
        for part in range(2):
            field_ref[block + part] = field[:, part * lanes:(part + 1) * lanes].reshape(groups, PAD, lanes)
    mix(g2_ref[...], field_ref, mixed_ref)
    for block in range(owned_blocks):
        first_ref[:, block * lanes:(block + 1) * lanes] = field_ref[block, me, :first_ref.shape[0], :]
    keeps = begin(sems.at[pl.ds(len(near) + steps, 1)], (first_ref, first_hbm))
    per = owned_blocks // steps
    for step in range(steps):
        copies[step].wait()
        for row in range(step * per, (step + 1) * per):
            own2_ref[:, row * lanes:(row + 1) * lanes] = block_row(
                row, PAD, where_ref, mixed_ref, stiff_ref[:, row * stored:(row + 1) * stored]
            )
    finish(keeps)


def last_kernel(own_ref, arrived_ref, r_ref, out_ref, slots_ref):
    arrived = arrived_ref[...].astype(f32)
    lines = arrived.shape[0]
    for quarter in range(QUARTERS):
        turned = pltpu.roll(arrived, (QUARTERS - quarter) % QUARTERS * PAD, 1)
        slots_ref[pl.ds(quarter, lines, stride=QUARTERS), :] = turned
    by_slot = slots_ref[...].T[:PAD, :].astype(bf16)
    for block in range(0, r_ref.shape[0], 2):
        at = slice(block * LANES, (block + 2) * LANES)
        table = jnp.concatenate([r_ref[block], r_ref[block + 1]], axis=1)
        total = own_ref[:, at] + dot(by_slot, table)
        out_ref[:, at] = total.astype(bf16)[:out_ref.shape[0], :]


def local(groups, peers, modes_in, blocks, block_cols, send_slot, recv_row, mix_cols, mix_coef):
    terms, all_stored, blk, _ = blocks.shape
    out_blocks, stored = block_cols.shape
    modes_dev, owned = modes_in.shape
    owned_blocks = owned // blk
    interface = send_slot.shape[0]
    slots = recv_row.shape[0]
    cap = slots // peers
    rows = groups * PAD
    lines = slots // QUARTERS
    Shape, dma = jax.ShapeDtypeStruct, pltpu.SemaphoreType.DMA

    def pin(x):
        return pltpu.with_memory_space_constraint(x, pltpu.HBM)

    others = {
        s: lax.ppermute(modes_in, "mode", [((to + s) % groups, to) for to in range(groups)])
        for s in (2, 1, 3)
    }
    blocks = pin(blocks)
    where = pin(block_cols.T)
    mix_cols, mix_coef = pin(mix_cols.transpose(0, 2, 1)), pin(mix_coef.transpose(0, 2, 1))
    send, recv = pin(send_slot.reshape(1, interface)), pin(recv_row.reshape(1, slots))
    tables = [pltpu.VMEM(mix_cols.shape, i32), pltpu.VMEM(mix_coef.shape, f32)]
    if_blocks = (terms, (out_blocks - owned_blocks) * stored, blk, blk)
    own_scratch = pltpu.VMEM((terms, owned_blocks * stored, blk, blk), bf16)
    field_shape, mixer_shape = (owned_blocks, groups, PAD, blk), (rows, terms * rows)
    field_scratch = pltpu.VMEM(field_shape, bf16)
    block_flops = 2 * terms * stored * blk * blk
    wide, narrow = (owned_blocks, terms * rows, blk), (owned_blocks, terms * PAD, blk)

    own_shape, table_shape = (owned_blocks, rows, blk), (owned_blocks, slots, blk)

    g, g2, place, send, recv, own_field, where, stiff = call(
        functools.partial(setup_kernel, groups),
        [Shape(mixer_shape, bf16), Shape((terms * PAD, rows), bf16), Shape((slots, interface), bf16), Shape(send.shape, i32),
         Shape(recv.shape, i32), Shape((modes_dev, owned), bf16), Shape(where.shape, i32), Shape(if_blocks, bf16)],
        [mix_cols, mix_coef, send, recv, pin(modes_in), where, blocks], [HBM] * 7, [VMEM] * 8, flops=10**6,
        scratch=[*tables, dma((7,))],
    )
    packed, field, g_kept = call(
        functools.partial(first_kernel, groups),
        [Shape((slots, rows), bf16), pltpu.HBM(field_shape, bf16), pltpu.HBM(mixer_shape, bf16)],
        [own_field, others[1], others[2], others[3], g, place, where, stiff],
        [VMEM] * 6 + [SMEM, VMEM], [VMEM, HBM, HBM],
        flops=block_flops * (out_blocks - owned_blocks) * rows, scratch=[field_scratch, dma((2,))],
    )
    arrived = lax.all_to_all(packed.reshape(peers, cap, rows), "space", split_axis=0, concat_axis=0, tiled=True)
    steps = owned_blocks // 2
    own, r = call(
        functools.partial(between_kernel, steps), [Shape(own_shape, f32), Shape(table_shape, bf16)],
        [pin(field), pin(g_kept), recv, where, blocks], [HBM, HBM, VMEM, SMEM, HBM], [VMEM] * 2,
        flops=block_flops * owned_blocks * rows,
        scratch=[field_scratch, pltpu.VMEM(mixer_shape, bf16), pltpu.VMEM(wide, bf16), own_scratch, dma((2 + steps,))],
    )
    packed2, turned = call(
        second_kernel, [Shape((lines, QUARTERS * PAD), bf16), pltpu.HBM((rows, slots), bf16)],
        [own, arrived.reshape(slots, rows), r, g2, send, where, blocks], [VMEM] * 5 + [SMEM, HBM], [VMEM, HBM],
        flops=2 * slots * rows * owned,
        scratch=[pltpu.VMEM((rows, slots), bf16), pltpu.VMEM((QUARTERS * PAD, QUARTERS * interface), bf16), pltpu.VMEM(if_blocks, bf16), dma((2,))],
    )
    arrived2 = lax.all_to_all(
        packed2.reshape(peers, cap // QUARTERS, QUARTERS * PAD), "space", split_axis=0, concat_axis=0, tiled=True
    )
    first_apply, own2, r2 = call(
        functools.partial(own_kernel, groups, steps),
        [pltpu.HBM((modes_dev, owned), bf16), Shape((PAD, owned), f32), Shape(table_shape, bf16)],
        [where, recv, g2, pin(turned), own, blocks], [SMEM, VMEM, VMEM, HBM, VMEM, HBM], [HBM, VMEM, VMEM],
        flops=block_flops * owned_blocks * PAD,
        scratch=[pltpu.VMEM((rows, slots), bf16), pltpu.VMEM((modes_dev, owned), bf16), field_scratch, pltpu.VMEM(narrow, bf16),
                 own_scratch, dma((2 + steps,))],
    )
    second_apply = call(
        last_kernel, [Shape((modes_dev, owned), bf16)],
        [own2, arrived2.reshape(lines, QUARTERS * PAD), r2], [VMEM] * 3, [VMEM], flops=2 * slots * PAD * owned,
        scratch=[pltpu.VMEM((slots, QUARTERS * PAD), f32)],
    )[0]
    return (first_apply, second_apply)


def solution(mesh):
    in_specs = (
        P("mode", "space"),
        P(None, "space", None, None),
        P("space", None),
        P("space"),
        P("space"),
        P(),
        P(),
    )
    out_specs = (P("mode", "space"), P("mode", "space"))
    body = functools.partial(local, mesh.shape["mode"], mesh.shape["space"])
    return jax.shard_map(body, mesh=mesh, in_specs=in_specs, out_specs=out_specs, check_vma=False)
```

```python
import functools
import math

import jax
import jax.numpy as jnp
from jax import lax
from jax.experimental import pallas as pl
from jax.experimental.pallas import tpu as pltpu
from jax.sharding import PartitionSpec as P

LANES = 128
PAD = 32
QUARTERS = 4
WIDTH = 256

VMEM = pl.BlockSpec(memory_space=pltpu.VMEM)
HBM = pl.BlockSpec(memory_space=pltpu.HBM)
VMEM_LIMIT = 32 * 1024 * 1024
bf16, f32, i32 = jnp.bfloat16, jnp.float32, jnp.int32


def call(kernel, outs, ins, in_specs, out_specs, flops, scratch=()):
    moved = sum(math.prod(a.shape) * jnp.dtype(a.dtype).itemsize for a in [*outs, *ins])
    return pl.pallas_call(
        kernel,
        out_shape=outs,
        in_specs=in_specs,
        out_specs=out_specs,
        scratch_shapes=scratch,
        compiler_params=pltpu.CompilerParams(vmem_limit_bytes=VMEM_LIMIT),
        cost_estimate=pl.CostEstimate(flops=flops, bytes_accessed=moved, transcendentals=0),
    )(*ins)


def begin(sems, *pairs):
    copies = [pltpu.make_async_copy(source, target, sems.at[at]) for at, (source, target) in enumerate(pairs)]
    for copy in copies:
        copy.start()
    return copies


def finish(copies):
    for copy in copies:
        copy.wait()


def one_hot(hit):
    return jnp.where(hit, 1.0, 0.0).astype(bf16)


def dot(a, b):
    return jnp.dot(a, b, preferred_element_type=f32)


def dot_t(a, b):
    return lax.dot_general(a, b, (((1,), (1,)), ((), ())), preferred_element_type=f32)


def padded_place(modes, groups, modes_dev):
    place = modes
    for group in range(1, groups):
        place += jnp.where(modes >= group * modes_dev, PAD - modes_dev, 0)
    return place


def mixer_columns(term, groups, cols_ref, coef_ref):
    modes = cols_ref.shape[2]
    cols = cols_ref[term]
    place = jnp.where(cols < modes, padded_place(cols, groups, modes // groups), -1)
    coef = coef_ref[term]
    want = lax.broadcasted_iota(i32, (groups * PAD, modes), 0)
    total = jnp.zeros(want.shape, f32)
    for slot in range(cols.shape[0]):
        total += jnp.where(place[slot:slot + 1, :] == want, coef[slot:slot + 1, :], 0.0)
    return total.astype(bf16)


def receive_table(recv_ref, r_ref):
    slots = recv_ref.shape[1]
    lanes = lax.broadcasted_iota(i32, (LANES, LANES), 1)
    for start in range(0, slots, LANES):
        at = slice(start, start + LANES)
        offset = jnp.broadcast_to(recv_ref[:, at].astype(f32), (LANES, LANES)).T.astype(i32) - lanes
        for block in range(r_ref.shape[0]):
            r_ref[block, at, :] = one_hot(offset == block * LANES)


def block_row(row, rows, cols_ref, mixed_ref, stiff):
    terms, stored = stiff.shape[:2]
    picked = jnp.concatenate(
        [
            mixed_ref[cols_ref[c, row], term * rows:(term + 1) * rows, :]
            for term in range(terms)
            for c in range(stored)
        ],
        axis=1,
    )
    return dot(picked, stiff.reshape(terms * stored * LANES, LANES))


def mix(mixer, field_ref, mixed_ref):
    blocks, groups, pad, lanes = field_ref.shape
    for block in range(0, blocks, 2):
        pair = [field_ref[block + part].reshape(groups * pad, lanes) for part in range(2)]
        mixed = dot(mixer, jnp.concatenate(pair, axis=1)).astype(bf16)
        for part in range(2):
            mixed_ref[block + part] = mixed[:, part * lanes:(part + 1) * lanes]


def stacked(wide):
    return jnp.concatenate([wide[:, at:at + LANES] for at in range(0, wide.shape[1], LANES)], axis=0)


def last_stored(blocks_ref, stiff_ref):
    count = stiff_ref.shape[1]
    return blocks_ref.at[:, pl.ds(blocks_ref.shape[1] - count, count)]


def mixed_row(picked, stiff, mixer):
    terms, stored = stiff.shape[:2]
    wide = jnp.concatenate([stiff[term].reshape(stored * LANES, LANES) for term in range(terms)], axis=1)
    product = dot(picked, wide).astype(bf16)
    return dot(mixer, jnp.concatenate([product[:, term * LANES:(term + 1) * LANES] for term in range(terms)], axis=0))


def setup_kernel(groups, cols_hbm, coef_hbm, send_hbm, recv_hbm, own_hbm, where_hbm, blocks_ref,
                 g_ref, g2_ref, place_ref, send_ref, recv_ref, own_ref, where_ref, stiff_ref, cols_ref, coef_ref, sems):
    copies = begin(
        sems, (cols_hbm, cols_ref), (coef_hbm, coef_ref), (send_hbm, send_ref), (own_hbm, own_ref),
        (where_hbm, where_ref), (recv_hbm, recv_ref), (last_stored(blocks_ref, stiff_ref), stiff_ref),
    )
    me = lax.axis_index("mode")
    modes = cols_ref.shape[2]
    rows = groups * PAD
    out_mode = lax.broadcasted_iota(i32, (rows, modes), 1)
    spread = one_hot(padded_place(out_mode, groups, modes // groups) == lax.broadcasted_iota(i32, (rows, modes), 0))
    finish(copies[:3])
    modes_dev = modes // groups
    row = lax.broadcasted_iota(i32, (PAD, modes), 0)
    mine = one_hot((lax.broadcasted_iota(i32, (PAD, modes), 1) == row + me * modes_dev) & (row < modes_dev))
    for term in range(cols_ref.shape[0]):
        columns = mixer_columns(term, groups, cols_ref, coef_ref)
        g_ref[:, term * rows:(term + 1) * rows] = dot_t(spread, columns).astype(bf16)
        g2_ref[term * PAD:(term + 1) * PAD, :] = dot_t(mine, columns).astype(bf16)
    place_ref[...] = one_hot(send_ref[...] == lax.broadcasted_iota(i32, place_ref.shape, 0))
    finish(copies[3:])


def first_kernel(groups, v0, v1, v2, v3, g_ref, place_ref, where_near, stiff_ref,
                 packed_ref, field_hbm, g_hbm, field_ref, where_ref, sems):
    table = begin(sems.at[pl.ds(2, 1)], (where_near, where_ref))
    copies = begin(sems, (g_ref, g_hbm))
    me = lax.axis_index("mode")
    owned_blocks, _, _, lanes = field_ref.shape
    modes_dev = v0.shape[0]
    field_ref[:, :, modes_dev:, :] = jnp.zeros_like(field_ref[:, :, modes_dev:, :])
    for slot, source in enumerate((v0, v1, v2, v3)):
        group = lax.rem(me + slot, groups)
        for block in range(owned_blocks):
            field_ref[block, group, :modes_dev, :] = source[:, block * lanes:(block + 1) * lanes]
    copies += begin(sems.at[pl.ds(1, 1)], (field_ref, field_hbm))
    finish(table)
    mixer = g_ref[...]
    stored, out_blocks = where_ref.shape
    parts = []
    for row in range(owned_blocks, out_blocks):
        picked = jnp.concatenate(
            [field_ref[where_ref[c, row]].reshape(groups * PAD, lanes) for c in range(stored)], axis=1
        )
        at = (row - owned_blocks) * stored
        parts.append(mixed_row(picked, stiff_ref[:, at:at + stored], mixer))
    part = jnp.concatenate(parts, axis=1).astype(bf16)
    packed_ref[...] = dot_t(place_ref[...], part).astype(bf16)
    finish(copies)


def own_fetch(steps, stored, blocks_ref, stiff_ref, sems):
    count = stiff_ref.shape[1] // steps
    parts = [pl.ds(step * count, count) for step in range(steps)]
    return begin(sems, *((blocks_ref.at[:, part], stiff_ref.at[:, part]) for part in parts))


def between_kernel(steps, field_hbm, g_hbm, recv_ref, where_near, blocks_ref,
                   own_ref, r_ref, field_ref, g_ref, mixed_ref, stiff_ref, where_ref, sems):
    near = begin(sems, (field_hbm, field_ref), (g_hbm, g_ref), (where_near, where_ref))
    stored = where_ref.shape[0]
    copies = own_fetch(steps, stored, blocks_ref, stiff_ref, sems.at[pl.ds(len(near), steps)])
    receive_table(recv_ref, r_ref)
    finish(near)
    mix(stacked(g_ref[...]), field_ref, mixed_ref)
    per = own_ref.shape[0] // steps
    for step in range(steps):
        copies[step].wait()
        for row in range(step * per, (step + 1) * per):
            own_ref[row] = block_row(
                row, own_ref.shape[1], where_ref, mixed_ref, stiff_ref[:, row * stored:(row + 1) * stored]
            )


def second_kernel(own_ref, arrived_ref, r_ref, g2_ref, send_ref, where_near, blocks_ref,
                  packed_ref, turned_hbm, turned_ref, spread_ref, stiff_ref, where_ref, sems):
    table = begin(sems.at[pl.ds(2, 1)], (where_near, where_ref))
    near = begin(sems, (last_stored(blocks_ref, stiff_ref), stiff_ref))
    turned = arrived_ref[...].astype(f32).T.astype(bf16)
    turned_ref[...] = turned
    keeps = begin(sems.at[pl.ds(len(near), 1)], (turned_ref, turned_hbm))
    finish(table)
    stored, out_blocks = where_ref.shape
    owned_blocks = own_ref.shape[0]
    terms = stiff_ref.shape[0]
    mixer = jnp.concatenate([g2_ref[term * PAD:(term + 1) * PAD, :] for term in range(terms)], axis=1)
    picks = []
    for row in range(owned_blocks, out_blocks):
        columns = [where_ref[c, row] for c in range(stored)]
        base = jnp.concatenate([own_ref[column] for column in columns], axis=1)
        table = jnp.concatenate([r_ref[column] for column in columns], axis=1)
        picks.append((base + dot(turned, table)).astype(bf16))
    width = send_ref.shape[1]
    lines = lax.broadcasted_iota(i32, (packed_ref.shape[0], width), 0) * QUARTERS
    place = jnp.concatenate([one_hot(send_ref[...] == lines + quarter) for quarter in range(QUARTERS)], axis=1)
    spread_ref[...] = jnp.zeros_like(spread_ref)
    finish(near)
    part = jnp.concatenate(
        [mixed_row(picked, stiff_ref[:, at * stored:(at + 1) * stored], mixer) for at, picked in enumerate(picks)], axis=1
    ).astype(bf16)
    for quarter in range(QUARTERS):
        spread_ref[quarter * PAD:(quarter + 1) * PAD, quarter * width:(quarter + 1) * width] = part
    packed_ref[...] = dot_t(place, spread_ref[...]).astype(bf16)
    finish(keeps)


def own_kernel(groups, steps, where_near, recv_ref, g2_ref, turned_hbm, own_ref, blocks_ref,
               first_hbm, own2_ref, r_ref, turned_ref, first_ref, field_ref, mixed_ref, stiff_ref, where_ref, sems):
    stored = where_ref.shape[0]
    near = begin(sems, (turned_hbm, turned_ref), (where_near, where_ref))
    copies = own_fetch(steps, stored, blocks_ref, stiff_ref, sems.at[pl.ds(len(near), steps)])
    me = lax.axis_index("mode")
    receive_table(recv_ref, r_ref)
    owned_blocks, _, lanes = own_ref.shape
    finish(near)
    turned = turned_ref[...]
    for block in range(0, owned_blocks, 2):
        table = jnp.concatenate([r_ref[block], r_ref[block + 1]], axis=1)
        base = jnp.concatenate([own_ref[block], own_ref[block + 1]], axis=1)
        field = (base + dot(turned, table)).astype(bf16)
        for part in range(2):
            field_ref[block + part] = field[:, part * lanes:(part + 1) * lanes].reshape(groups, PAD, lanes)
    mix(g2_ref[...], field_ref, mixed_ref)
    for block in range(owned_blocks):
        first_ref[:, block * lanes:(block + 1) * lanes] = field_ref[block, me, :first_ref.shape[0], :]
    keeps = begin(sems.at[pl.ds(len(near) + steps, 1)], (first_ref, first_hbm))
    per = owned_blocks // steps
    for step in range(steps):
        copies[step].wait()
        for row in range(step * per, (step + 1) * per):
            own2_ref[:, row * lanes:(row + 1) * lanes] = block_row(
                row, PAD, where_ref, mixed_ref, stiff_ref[:, row * stored:(row + 1) * stored]
            )
    finish(keeps)


def last_kernel(own_ref, arrived_ref, r_ref, out_ref, slots_ref):
    arrived = arrived_ref[...].astype(f32)
    lines = arrived.shape[0]
    for quarter in range(QUARTERS):
        turned = pltpu.roll(arrived, (QUARTERS - quarter) % QUARTERS * PAD, 1)
        slots_ref[pl.ds(quarter, lines, stride=QUARTERS), :] = turned
    by_slot = slots_ref[...].T[:PAD, :].astype(bf16)
    for block in range(0, r_ref.shape[0], 2):
        at = slice(block * LANES, (block + 2) * LANES)
        table = jnp.concatenate([r_ref[block], r_ref[block + 1]], axis=1)
        total = own_ref[:, at] + dot(by_slot, table)
        out_ref[:, at] = total.astype(bf16)[:out_ref.shape[0], :]


def local(groups, peers, modes_in, blocks, block_cols, send_slot, recv_row, mix_cols, mix_coef):
    terms, all_stored, blk, _ = blocks.shape
    out_blocks, stored = block_cols.shape
    modes_dev, owned = modes_in.shape
    owned_blocks = owned // blk
    interface = send_slot.shape[0]
    slots = recv_row.shape[0]
    cap = slots // peers
    rows = groups * PAD
    lines = slots // QUARTERS
    Shape, dma = jax.ShapeDtypeStruct, pltpu.SemaphoreType.DMA

    def pin(x):
        return pltpu.with_memory_space_constraint(x, pltpu.HBM)

    others = {
        s: lax.ppermute(modes_in, "mode", [((to + s) % groups, to) for to in range(groups)])
        for s in (2, 1, 3)
    }
    blocks = pin(blocks)
    where = pin(block_cols.T)
    mix_cols, mix_coef = pin(mix_cols.transpose(0, 2, 1)), pin(mix_coef.transpose(0, 2, 1))
    send, recv = pin(send_slot.reshape(1, interface)), pin(recv_row.reshape(1, slots))
    tables = [pltpu.VMEM(mix_cols.shape, i32), pltpu.VMEM(mix_coef.shape, f32)]
    if_blocks = (terms, (out_blocks - owned_blocks) * stored, blk, blk)
    own_scratch = pltpu.VMEM((terms, owned_blocks * stored, blk, blk), bf16)
    field_shape, mixer_shape = (owned_blocks, groups, PAD, blk), (rows, terms * rows)
    field_scratch = pltpu.VMEM(field_shape, bf16)
    block_flops = 2 * terms * stored * blk * blk
    wide, narrow = (owned_blocks, terms * rows, blk), (owned_blocks, terms * PAD, blk)

    where_scratch = pltpu.SMEM(where.shape, i32)
    own_shape, table_shape = (owned_blocks, rows, blk), (owned_blocks, slots, blk)

    g, g2, place, send, recv, own_field, where, stiff = call(
        functools.partial(setup_kernel, groups),
        [Shape(mixer_shape, bf16), Shape((terms * PAD, rows), bf16), Shape((slots, interface), bf16), Shape(send.shape, i32),
         Shape(recv.shape, i32), Shape((modes_dev, owned), bf16), Shape(where.shape, i32), Shape(if_blocks, bf16)],
        [mix_cols, mix_coef, send, recv, pin(modes_in), where, blocks], [HBM] * 7, [VMEM] * 8, flops=10**6,
        scratch=[*tables, dma((7,))],
    )
    packed, field, g_kept = call(
        functools.partial(first_kernel, groups),
        [Shape((slots, rows), bf16), pltpu.HBM(field_shape, bf16), pltpu.HBM(mixer_shape, bf16)],
        [own_field, others[1], others[2], others[3], g, place, where, stiff],
        [VMEM] * 8, [VMEM, HBM, HBM],
        flops=block_flops * (out_blocks - owned_blocks) * rows, scratch=[field_scratch, where_scratch, dma((3,))],
    )
    arrived = lax.all_to_all(packed.reshape(peers, cap, rows), "space", split_axis=0, concat_axis=0, tiled=True)
    steps = owned_blocks // 2
    own, r = call(
        functools.partial(between_kernel, steps), [Shape(own_shape, f32), Shape(table_shape, bf16)],
        [pin(field), pin(g_kept), recv, where, blocks], [HBM, HBM, VMEM, VMEM, HBM], [VMEM] * 2,
        flops=block_flops * owned_blocks * rows,
        scratch=[field_scratch, pltpu.VMEM(mixer_shape, bf16), pltpu.VMEM(wide, bf16), own_scratch, where_scratch,
                 dma((3 + steps,))],
    )
    packed2, turned = call(
        second_kernel, [Shape((lines, QUARTERS * PAD), bf16), pltpu.HBM((rows, slots), bf16)],
        [own, arrived.reshape(slots, rows), r, g2, send, where, blocks], [VMEM] * 6 + [HBM], [VMEM, HBM],
        flops=2 * slots * rows * owned,
        scratch=[pltpu.VMEM((rows, slots), bf16), pltpu.VMEM((QUARTERS * PAD, QUARTERS * interface), bf16), pltpu.VMEM(if_blocks, bf16), where_scratch, dma((3,))],
    )
    arrived2 = lax.all_to_all(
        packed2.reshape(peers, cap // QUARTERS, QUARTERS * PAD), "space", split_axis=0, concat_axis=0, tiled=True
    )
    first_apply, own2, r2 = call(
        functools.partial(own_kernel, groups, steps),
        [pltpu.HBM((modes_dev, owned), bf16), Shape((PAD, owned), f32), Shape(table_shape, bf16)],
        [where, recv, g2, pin(turned), own, blocks], [VMEM, VMEM, VMEM, HBM, VMEM, HBM], [HBM, VMEM, VMEM],
        flops=block_flops * owned_blocks * PAD,
        scratch=[pltpu.VMEM((rows, slots), bf16), pltpu.VMEM((modes_dev, owned), bf16), field_scratch, pltpu.VMEM(narrow, bf16),
                 own_scratch, where_scratch, dma((3 + steps,))],
    )
    second_apply = call(
        last_kernel, [Shape((modes_dev, owned), bf16)],
        [own2, arrived2.reshape(lines, QUARTERS * PAD), r2], [VMEM] * 3, [VMEM], flops=2 * slots * PAD * owned,
        scratch=[pltpu.VMEM((slots, QUARTERS * PAD), f32)],
    )[0]
    return (first_apply, second_apply)


def solution(mesh):
    in_specs = (
        P("mode", "space"),
        P(None, "space", None, None),
        P("space", None),
        P("space"),
        P("space"),
        P(),
        P(),
    )
    out_specs = (P("mode", "space"), P("mode", "space"))
    body = functools.partial(local, mesh.shape["mode"], mesh.shape["space"])
    return jax.shard_map(body, mesh=mesh, in_specs=in_specs, out_specs=out_specs, check_vma=False)
```

```python
import functools
import math

import jax
import jax.numpy as jnp
from jax import lax
from jax.experimental import pallas as pl
from jax.experimental.pallas import tpu as pltpu
from jax.sharding import PartitionSpec as P

LANES = 128
PAD = 32
QUARTERS = 4
WIDTH = 256

VMEM = pl.BlockSpec(memory_space=pltpu.VMEM)
HBM = pl.BlockSpec(memory_space=pltpu.HBM)
VMEM_LIMIT = 32 * 1024 * 1024
bf16, f32, i32 = jnp.bfloat16, jnp.float32, jnp.int32


def call(kernel, outs, ins, in_specs, out_specs, flops, scratch=()):
    moved = sum(math.prod(a.shape) * jnp.dtype(a.dtype).itemsize for a in [*outs, *ins])
    return pl.pallas_call(
        kernel,
        out_shape=outs,
        in_specs=in_specs,
        out_specs=out_specs,
        scratch_shapes=scratch,
        compiler_params=pltpu.CompilerParams(vmem_limit_bytes=VMEM_LIMIT),
        cost_estimate=pl.CostEstimate(flops=flops, bytes_accessed=moved, transcendentals=0),
    )(*ins)


def begin(sems, *pairs):
    copies = [pltpu.make_async_copy(source, target, sems.at[at]) for at, (source, target) in enumerate(pairs)]
    for copy in copies:
        copy.start()
    return copies


def finish(copies):
    for copy in copies:
        copy.wait()


def one_hot(hit):
    return jnp.where(hit, 1.0, 0.0).astype(bf16)


def dot(a, b):
    return jnp.dot(a, b, preferred_element_type=f32)


def dot_t(a, b):
    return lax.dot_general(a, b, (((1,), (1,)), ((), ())), preferred_element_type=f32)


def padded_place(modes, groups, modes_dev):
    place = modes
    for group in range(1, groups):
        place += jnp.where(modes >= group * modes_dev, PAD - modes_dev, 0)
    return place


def mixer_columns(term, groups, cols_ref, coef_ref):
    modes = cols_ref.shape[2]
    cols = cols_ref[term]
    place = jnp.where(cols < modes, padded_place(cols, groups, modes // groups), -1)
    coef = coef_ref[term]
    want = lax.broadcasted_iota(i32, (groups * PAD, modes), 0)
    total = jnp.zeros(want.shape, f32)
    for slot in range(cols.shape[0]):
        total += jnp.where(place[slot:slot + 1, :] == want, coef[slot:slot + 1, :], 0.0)
    return total.astype(bf16)


def receive_table(recv_ref, r_ref, blocks):
    slots = recv_ref.shape[1]
    lanes = lax.broadcasted_iota(i32, (LANES, LANES), 1)
    for start in range(0, slots, LANES):
        at = slice(start, start + LANES)
        offset = jnp.broadcast_to(recv_ref[:, at].astype(f32), (LANES, LANES)).T.astype(i32) - lanes
        for place, block in enumerate(blocks):
            r_ref[place, at, :] = one_hot(offset == block * LANES)


def block_row(row, rows, cols_ref, mixed_ref, stiff):
    terms, stored = stiff.shape[:2]
    picked = jnp.concatenate(
        [
            mixed_ref[cols_ref[c, row], term * rows:(term + 1) * rows, :]
            for term in range(terms)
            for c in range(stored)
        ],
        axis=1,
    )
    return dot(picked, stiff.reshape(terms * stored * LANES, LANES))


def mix(mixer, field_ref, mixed_ref):
    blocks, groups, pad, lanes = field_ref.shape
    for block in range(0, blocks, 2):
        pair = [field_ref[block + part].reshape(groups * pad, lanes) for part in range(2)]
        mixed = dot(mixer, jnp.concatenate(pair, axis=1)).astype(bf16)
        for part in range(2):
            mixed_ref[block + part] = mixed[:, part * lanes:(part + 1) * lanes]


def stacked(wide):
    return jnp.concatenate([wide[:, at:at + LANES] for at in range(0, wide.shape[1], LANES)], axis=0)


def last_stored(blocks_ref, stiff_ref):
    count = stiff_ref.shape[1]
    return blocks_ref.at[:, pl.ds(blocks_ref.shape[1] - count, count)]


def mixed_row(picked, stiff, mixer):
    terms, stored = stiff.shape[:2]
    wide = jnp.concatenate([stiff[term].reshape(stored * LANES, LANES) for term in range(terms)], axis=1)
    product = dot(picked, wide).astype(bf16)
    return dot(mixer, jnp.concatenate([product[:, term * LANES:(term + 1) * LANES] for term in range(terms)], axis=0))


def setup_kernel(groups, cols_hbm, coef_hbm, send_hbm, recv_hbm, own_hbm, where_hbm, blocks_ref,
                 g_ref, g2_ref, place_ref, send_ref, recv_ref, own_ref, where_ref, stiff_ref, cols_ref, coef_ref, sems):
    copies = begin(
        sems, (cols_hbm, cols_ref), (coef_hbm, coef_ref), (send_hbm, send_ref), (own_hbm, own_ref),
        (where_hbm, where_ref), (recv_hbm, recv_ref), (last_stored(blocks_ref, stiff_ref), stiff_ref),
    )
    me = lax.axis_index("mode")
    modes = cols_ref.shape[2]
    rows = groups * PAD
    out_mode = lax.broadcasted_iota(i32, (rows, modes), 1)
    spread = one_hot(padded_place(out_mode, groups, modes // groups) == lax.broadcasted_iota(i32, (rows, modes), 0))
    finish(copies[:3])
    modes_dev = modes // groups
    row = lax.broadcasted_iota(i32, (PAD, modes), 0)
    mine = one_hot((lax.broadcasted_iota(i32, (PAD, modes), 1) == row + me * modes_dev) & (row < modes_dev))
    for term in range(cols_ref.shape[0]):
        columns = mixer_columns(term, groups, cols_ref, coef_ref)
        g_ref[:, term * rows:(term + 1) * rows] = dot_t(spread, columns).astype(bf16)
        g2_ref[term * PAD:(term + 1) * PAD, :] = dot_t(mine, columns).astype(bf16)
    place_ref[...] = one_hot(send_ref[...] == lax.broadcasted_iota(i32, place_ref.shape, 0))
    finish(copies[3:])


def first_kernel(groups, v0, v1, v2, v3, g_ref, place_ref, where_near, stiff_ref,
                 packed_ref, field_ref, where_ref, sems):
    table = begin(sems, (where_near, where_ref))
    me = lax.axis_index("mode")
    owned_blocks, _, _, lanes = field_ref.shape
    modes_dev = v0.shape[0]
    field_ref[:, :, modes_dev:, :] = jnp.zeros_like(field_ref[:, :, modes_dev:, :])
    for slot, source in enumerate((v0, v1, v2, v3)):
        group = lax.rem(me + slot, groups)
        for block in range(owned_blocks):
            field_ref[block, group, :modes_dev, :] = source[:, block * lanes:(block + 1) * lanes]
    finish(table)
    mixer = g_ref[...]
    stored, out_blocks = where_ref.shape
    parts = []
    for row in range(owned_blocks, out_blocks):
        picked = jnp.concatenate(
            [field_ref[where_ref[c, row]].reshape(groups * PAD, lanes) for c in range(stored)], axis=1
        )
        at = (row - owned_blocks) * stored
        parts.append(mixed_row(picked, stiff_ref[:, at:at + stored], mixer))
    part = jnp.concatenate(parts, axis=1).astype(bf16)
    packed_ref[...] = dot_t(place_ref[...], part).astype(bf16)


def own_fetch(steps, stored, blocks_ref, stiff_ref, sems):
    count = stiff_ref.shape[1] // steps
    parts = [pl.ds(step * count, count) for step in range(steps)]
    return begin(sems, *((blocks_ref.at[:, part], stiff_ref.at[:, part]) for part in parts))


def between_kernel(steps, field_ref, g_ref, recv_ref, where_near, blocks_ref,
                   own_ref, r_ref, mixed_ref, stiff_ref, where_ref, sems):
    near = begin(sems, (where_near, where_ref))
    stored = where_ref.shape[0]
    copies = own_fetch(steps, stored, blocks_ref, stiff_ref, sems.at[pl.ds(len(near), steps)])
    mix(stacked(g_ref[...]), field_ref, mixed_ref)
    finish(near)
    read = [(c, row) for row in range(own_ref.shape[0], where_ref.shape[1]) for c in range(stored)]
    receive_table(recv_ref, r_ref, [where_ref[c, row] for c, row in read])
    per = own_ref.shape[0] // steps
    for step in range(steps):
        copies[step].wait()
        for row in range(step * per, (step + 1) * per):
            own_ref[row] = block_row(
                row, own_ref.shape[1], where_ref, mixed_ref, stiff_ref[:, row * stored:(row + 1) * stored]
            )


def second_kernel(own_ref, arrived_ref, r_ref, g2_ref, send_ref, where_near, blocks_ref,
                  packed_ref, turned_hbm, turned_ref, spread_ref, stiff_ref, where_ref, sems):
    table = begin(sems.at[pl.ds(2, 1)], (where_near, where_ref))
    near = begin(sems, (last_stored(blocks_ref, stiff_ref), stiff_ref))
    turned = arrived_ref[...].astype(f32).T.astype(bf16)
    turned_ref[...] = turned
    keeps = begin(sems.at[pl.ds(len(near), 1)], (turned_ref, turned_hbm))
    finish(table)
    stored, out_blocks = where_ref.shape
    owned_blocks = own_ref.shape[0]
    terms = stiff_ref.shape[0]
    mixer = jnp.concatenate([g2_ref[term * PAD:(term + 1) * PAD, :] for term in range(terms)], axis=1)
    picks = []
    for row in range(owned_blocks, out_blocks):
        columns = [where_ref[c, row] for c in range(stored)]
        base = jnp.concatenate([own_ref[column] for column in columns], axis=1)
        first = (row - owned_blocks) * stored
        table = jnp.concatenate([r_ref[first + c] for c in range(stored)], axis=1)
        picks.append((base + dot(turned, table)).astype(bf16))
    width = send_ref.shape[1]
    lines = lax.broadcasted_iota(i32, (packed_ref.shape[0], width), 0) * QUARTERS
    place = jnp.concatenate([one_hot(send_ref[...] == lines + quarter) for quarter in range(QUARTERS)], axis=1)
    spread_ref[...] = jnp.zeros_like(spread_ref)
    finish(near)
    part = jnp.concatenate(
        [mixed_row(picked, stiff_ref[:, at * stored:(at + 1) * stored], mixer) for at, picked in enumerate(picks)], axis=1
    ).astype(bf16)
    for quarter in range(QUARTERS):
        spread_ref[quarter * PAD:(quarter + 1) * PAD, quarter * width:(quarter + 1) * width] = part
    packed_ref[...] = dot_t(place, spread_ref[...]).astype(bf16)
    finish(keeps)


def own_kernel(groups, steps, where_near, recv_ref, g2_ref, turned_hbm, own_ref, blocks_ref,
               first_hbm, own2_ref, r_ref, turned_ref, first_ref, field_ref, mixed_ref, stiff_ref, where_ref, sems):
    stored = where_ref.shape[0]
    near = begin(sems, (turned_hbm, turned_ref), (where_near, where_ref))
    copies = own_fetch(steps, stored, blocks_ref, stiff_ref, sems.at[pl.ds(len(near), steps)])
    me = lax.axis_index("mode")
    receive_table(recv_ref, r_ref, range(r_ref.shape[0]))
    owned_blocks, _, lanes = own_ref.shape
    finish(near)
    turned = turned_ref[...]
    for block in range(0, owned_blocks, 2):
        table = jnp.concatenate([r_ref[block], r_ref[block + 1]], axis=1)
        base = jnp.concatenate([own_ref[block], own_ref[block + 1]], axis=1)
        field = (base + dot(turned, table)).astype(bf16)
        for part in range(2):
            field_ref[block + part] = field[:, part * lanes:(part + 1) * lanes].reshape(groups, PAD, lanes)
    mix(g2_ref[...], field_ref, mixed_ref)
    for block in range(owned_blocks):
        first_ref[:, block * lanes:(block + 1) * lanes] = field_ref[block, me, :first_ref.shape[0], :]
    keeps = begin(sems.at[pl.ds(len(near) + steps, 1)], (first_ref, first_hbm))
    per = owned_blocks // steps
    for step in range(steps):
        copies[step].wait()
        for row in range(step * per, (step + 1) * per):
            own2_ref[:, row * lanes:(row + 1) * lanes] = block_row(
                row, PAD, where_ref, mixed_ref, stiff_ref[:, row * stored:(row + 1) * stored]
            )
    finish(keeps)


def last_kernel(own_ref, arrived_ref, r_ref, out_hbm, slots_ref, out_ref, sems):
    arrived = arrived_ref[...].astype(f32)
    lines = arrived.shape[0]
    for quarter in range(QUARTERS):
        turned = pltpu.roll(arrived, (QUARTERS - quarter) % QUARTERS * PAD, 1)
        slots_ref[pl.ds(quarter, lines, stride=QUARTERS), :] = turned
    by_slot = slots_ref[...].T[:PAD, :].astype(bf16)
    span = r_ref.shape[0] // sems.shape[0]
    copies = []
    for block in range(0, r_ref.shape[0], 2):
        at = slice(block * LANES, (block + 2) * LANES)
        table = jnp.concatenate([r_ref[block], r_ref[block + 1]], axis=1)
        total = own_ref[:, at] + dot(by_slot, table)
        out_ref[:, at] = total.astype(bf16)[:out_ref.shape[0], :]
        if (block + 2) % span == 0:
            part = pl.ds((block + 2 - span) * LANES, span * LANES)
            copies += begin(sems.at[pl.ds(len(copies), 1)], (out_ref.at[:, part], out_hbm.at[:, part]))
    finish(copies)


def local(groups, peers, modes_in, blocks, block_cols, send_slot, recv_row, mix_cols, mix_coef):
    terms, all_stored, blk, _ = blocks.shape
    out_blocks, stored = block_cols.shape
    modes_dev, owned = modes_in.shape
    owned_blocks = owned // blk
    interface = send_slot.shape[0]
    slots = recv_row.shape[0]
    cap = slots // peers
    rows = groups * PAD
    lines = slots // QUARTERS
    Shape, dma = jax.ShapeDtypeStruct, pltpu.SemaphoreType.DMA

    def pin(x):
        return pltpu.with_memory_space_constraint(x, pltpu.HBM)

    others = {
        s: lax.ppermute(modes_in, "mode", [((to + s) % groups, to) for to in range(groups)])
        for s in (2, 1, 3)
    }
    blocks = pin(blocks)
    where = pin(block_cols.T)
    mix_cols, mix_coef = pin(mix_cols.transpose(0, 2, 1)), pin(mix_coef.transpose(0, 2, 1))
    send, recv = pin(send_slot.reshape(1, interface)), pin(recv_row.reshape(1, slots))
    tables = [pltpu.VMEM(mix_cols.shape, i32), pltpu.VMEM(mix_coef.shape, f32)]
    if_blocks = (terms, (out_blocks - owned_blocks) * stored, blk, blk)
    own_scratch = pltpu.VMEM((terms, owned_blocks * stored, blk, blk), bf16)
    field_shape, mixer_shape = (owned_blocks, groups, PAD, blk), (rows, terms * rows)
    field_scratch = pltpu.VMEM(field_shape, bf16)
    block_flops = 2 * terms * stored * blk * blk
    wide, narrow = (owned_blocks, terms * rows, blk), (owned_blocks, terms * PAD, blk)

    where_scratch = pltpu.SMEM(where.shape, i32)
    own_shape, table_shape = (owned_blocks, rows, blk), (owned_blocks, slots, blk)

    g, g2, place, send, recv, own_field, where, stiff = call(
        functools.partial(setup_kernel, groups),
        [Shape(mixer_shape, bf16), Shape((terms * PAD, rows), bf16), Shape((slots, interface), bf16), Shape(send.shape, i32),
         Shape(recv.shape, i32), Shape((modes_dev, owned), bf16), Shape(where.shape, i32), Shape(if_blocks, bf16)],
        [mix_cols, mix_coef, send, recv, pin(modes_in), where, blocks], [HBM] * 7, [VMEM] * 8, flops=10**6,
        scratch=[*tables, dma((7,))],
    )
    packed, field = call(
        functools.partial(first_kernel, groups),
        [Shape((slots, rows), bf16), Shape(field_shape, bf16)],
        [own_field, others[1], others[2], others[3], g, place, where, stiff],
        [VMEM] * 8, [VMEM] * 2,
        flops=block_flops * (out_blocks - owned_blocks) * rows, scratch=[where_scratch, dma((1,))],
    )
    arrived = lax.all_to_all(packed.reshape(peers, cap, rows), "space", split_axis=0, concat_axis=0, tiled=True)
    steps = owned_blocks // 2
    own, r = call(
        functools.partial(between_kernel, steps), [Shape(own_shape, f32), Shape((if_blocks[1], slots, blk), bf16)],
        [field, g, recv, where, blocks], [VMEM] * 4 + [HBM], [VMEM] * 2,
        flops=block_flops * owned_blocks * rows,
        scratch=[pltpu.VMEM(wide, bf16), own_scratch, where_scratch, dma((1 + steps,))],
    )
    packed2, turned = call(
        second_kernel, [Shape((lines, QUARTERS * PAD), bf16), pltpu.HBM((rows, slots), bf16)],
        [own, arrived.reshape(slots, rows), r, g2, send, where, blocks], [VMEM] * 6 + [HBM], [VMEM, HBM],
        flops=2 * slots * rows * owned,
        scratch=[pltpu.VMEM((rows, slots), bf16), pltpu.VMEM((QUARTERS * PAD, QUARTERS * interface), bf16), pltpu.VMEM(if_blocks, bf16), where_scratch, dma((3,))],
    )
    arrived2 = lax.all_to_all(
        packed2.reshape(peers, cap // QUARTERS, QUARTERS * PAD), "space", split_axis=0, concat_axis=0, tiled=True
    )
    first_apply, own2, r2 = call(
        functools.partial(own_kernel, groups, steps),
        [pltpu.HBM((modes_dev, owned), bf16), Shape((PAD, owned), f32), Shape(table_shape, bf16)],
        [where, recv, g2, pin(turned), own, blocks], [VMEM, VMEM, VMEM, HBM, VMEM, HBM], [HBM, VMEM, VMEM],
        flops=block_flops * owned_blocks * PAD,
        scratch=[pltpu.VMEM((rows, slots), bf16), pltpu.VMEM((modes_dev, owned), bf16), field_scratch, pltpu.VMEM(narrow, bf16),
                 own_scratch, where_scratch, dma((3 + steps,))],
    )
    second_apply = call(
        last_kernel, [pltpu.HBM((modes_dev, owned), bf16)],
        [own2, arrived2.reshape(lines, QUARTERS * PAD), r2], [VMEM] * 3, [HBM], flops=2 * slots * PAD * owned,
        scratch=[pltpu.VMEM((slots, QUARTERS * PAD), f32), pltpu.VMEM((modes_dev, owned), bf16), dma((owned_blocks // 4,))],
    )[0]
    return (first_apply, second_apply)


def solution(mesh):
    in_specs = (
        P("mode", "space"),
        P(None, "space", None, None),
        P("space", None),
        P("space"),
        P("space"),
        P(),
        P(),
    )
    out_specs = (P("mode", "space"), P("mode", "space"))
    body = functools.partial(local, mesh.shape["mode"], mesh.shape["space"])
    return jax.shard_map(body, mesh=mesh, in_specs=in_specs, out_specs=out_specs, check_vma=False)
```

```python
import functools
import math

import jax
import jax.numpy as jnp
from jax import lax
from jax.experimental import pallas as pl
from jax.experimental.pallas import tpu as pltpu
from jax.sharding import PartitionSpec as P

LANES = 128
PAD = 32
QUARTERS = 4
TOGETHER = 2

VMEM = pl.BlockSpec(memory_space=pltpu.VMEM)
HBM = pl.BlockSpec(memory_space=pltpu.HBM)
VMEM_LIMIT = 32 * 1024 * 1024
bf16, f32, i32 = jnp.bfloat16, jnp.float32, jnp.int32


def call(kernel, outs, ins, in_specs, out_specs, flops, scratch=()):
    moved = sum(math.prod(a.shape) * jnp.dtype(a.dtype).itemsize for a in [*outs, *ins])
    return pl.pallas_call(
        kernel,
        out_shape=outs,
        in_specs=in_specs,
        out_specs=out_specs,
        scratch_shapes=scratch,
        compiler_params=pltpu.CompilerParams(vmem_limit_bytes=VMEM_LIMIT),
        cost_estimate=pl.CostEstimate(flops=flops, bytes_accessed=moved, transcendentals=0),
    )(*ins)


def begin(sems, *pairs):
    copies = [pltpu.make_async_copy(source, target, sems.at[at]) for at, (source, target) in enumerate(pairs)]
    for copy in copies:
        copy.start()
    return copies


def finish(copies):
    for copy in copies:
        copy.wait()


def one_hot(hit):
    return jnp.where(hit, 1.0, 0.0).astype(bf16)


def dot(a, b):
    return jnp.dot(a, b, preferred_element_type=f32)


def dot_t(a, b):
    return lax.dot_general(a, b, (((1,), (1,)), ((), ())), preferred_element_type=f32)


def padded_place(modes, groups, modes_dev):
    place = modes
    for group in range(1, groups):
        place += jnp.where(modes >= group * modes_dev, PAD - modes_dev, 0)
    return place


def mixer_columns(term, groups, cols_ref, coef_ref):
    modes = cols_ref.shape[2]
    cols = cols_ref[term]
    place = jnp.where(cols < modes, padded_place(cols, groups, modes // groups), -1)
    coef = coef_ref[term]
    want = lax.broadcasted_iota(i32, (groups * PAD, modes), 0)
    total = jnp.zeros(want.shape, f32)
    for slot in range(cols.shape[0]):
        total += jnp.where(place[slot:slot + 1, :] == want, coef[slot:slot + 1, :], 0.0)
    return total.astype(bf16)


def receive_table(recv_ref, r_ref, blocks):
    slots = recv_ref.shape[1]
    lanes = lax.broadcasted_iota(i32, (LANES, LANES), 1)
    for start in range(0, slots, LANES):
        at = slice(start, start + LANES)
        offset = jnp.broadcast_to(recv_ref[:, at].astype(f32), (LANES, LANES)).T.astype(i32) - lanes
        for place, block in enumerate(blocks):
            r_ref[place, at, :] = one_hot(offset == block * LANES)


def block_row(row, rows, cols_ref, mixed_ref, stiff):
    terms, stored = stiff.shape[:2]
    picked = jnp.concatenate(
        [
            mixed_ref[cols_ref[c, row], term * rows:(term + 1) * rows, :]
            for term in range(terms)
            for c in range(stored)
        ],
        axis=1,
    )
    return dot(picked, stiff.reshape(terms * stored * LANES, LANES))


def mix(mixer, field_ref, mixed_ref):
    blocks, groups, pad, lanes = field_ref.shape
    for block in range(0, blocks, 2):
        pair = [field_ref[block + part].reshape(groups * pad, lanes) for part in range(2)]
        mixed = dot(mixer, jnp.concatenate(pair, axis=1)).astype(bf16)
        for part in range(2):
            mixed_ref[block + part] = mixed[:, part * lanes:(part + 1) * lanes]


def stacked(wide):
    return jnp.concatenate([wide[:, at:at + LANES] for at in range(0, wide.shape[1], LANES)], axis=0)


def last_stored(blocks_ref, stiff_ref):
    count = stiff_ref.shape[1]
    return blocks_ref.at[:, pl.ds(blocks_ref.shape[1] - count, count)]


def mixed_row(picked, stiff, mixer):
    terms, stored = stiff.shape[:2]
    wide = jnp.concatenate([stiff[term].reshape(stored * LANES, LANES) for term in range(terms)], axis=1)
    product = dot(picked, wide).astype(bf16)
    return dot(mixer, jnp.concatenate([product[:, term * LANES:(term + 1) * LANES] for term in range(terms)], axis=0))


def setup_kernel(groups, cols_hbm, coef_hbm, send_hbm, recv_hbm, own_hbm, where_hbm, blocks_ref,
                 g_ref, g2_ref, place_ref, send_ref, recv_ref, own_ref, where_ref, stiff_ref, cols_ref, coef_ref, sems):
    copies = begin(
        sems, (cols_hbm, cols_ref), (coef_hbm, coef_ref), (send_hbm, send_ref), (own_hbm, own_ref),
        (where_hbm, where_ref), (recv_hbm, recv_ref), (last_stored(blocks_ref, stiff_ref), stiff_ref),
    )
    me = lax.axis_index("mode")
    modes = cols_ref.shape[2]
    rows = groups * PAD
    out_mode = lax.broadcasted_iota(i32, (rows, modes), 1)
    spread = one_hot(padded_place(out_mode, groups, modes // groups) == lax.broadcasted_iota(i32, (rows, modes), 0))
    finish(copies[:3])
    modes_dev = modes // groups
    row = lax.broadcasted_iota(i32, (PAD, modes), 0)
    mine = one_hot((lax.broadcasted_iota(i32, (PAD, modes), 1) == row + me * modes_dev) & (row < modes_dev))
    for term in range(cols_ref.shape[0]):
        columns = mixer_columns(term, groups, cols_ref, coef_ref)
        g_ref[:, term * rows:(term + 1) * rows] = dot_t(spread, columns).astype(bf16)
        g2_ref[term * PAD:(term + 1) * PAD, :] = dot_t(mine, columns).astype(bf16)
    place_ref[...] = one_hot(send_ref[...] == lax.broadcasted_iota(i32, place_ref.shape, 0))
    finish(copies[3:])


def first_kernel(groups, v0, v1, v2, v3, g_ref, place_ref, where_near, stiff_ref,
                 packed_ref, field_ref, where_ref, sems):
    table = begin(sems, (where_near, where_ref))
    me = lax.axis_index("mode")
    owned_blocks, _, _, lanes = field_ref.shape
    modes_dev = v0.shape[0]
    field_ref[:, :, modes_dev:, :] = jnp.zeros_like(field_ref[:, :, modes_dev:, :])
    for slot, source in enumerate((v0, v1, v2, v3)):
        group = lax.rem(me + slot, groups)
        for block in range(owned_blocks):
            field_ref[block, group, :modes_dev, :] = source[:, block * lanes:(block + 1) * lanes]
    finish(table)
    mixer = g_ref[...]
    stored, out_blocks = where_ref.shape
    parts = []
    for row in range(owned_blocks, out_blocks):
        picked = jnp.concatenate(
            [field_ref[where_ref[c, row]].reshape(groups * PAD, lanes) for c in range(stored)], axis=1
        )
        at = (row - owned_blocks) * stored
        parts.append(mixed_row(picked, stiff_ref[:, at:at + stored], mixer))
    part = jnp.concatenate(parts, axis=1).astype(bf16)
    packed_ref[...] = dot_t(place_ref[...], part).astype(bf16)


def own_fetch(steps, stored, blocks_ref, stiff_ref, sems):
    count = stiff_ref.shape[1] // steps
    parts = [pl.ds(step * count, count) for step in range(steps)]
    return begin(sems, *((blocks_ref.at[:, part], stiff_ref.at[:, part]) for part in parts))


def between_kernel(steps, field_ref, g_ref, recv_ref, where_near, blocks_ref,
                   own_ref, r_ref, mixed_ref, stiff_ref, where_ref, sems):
    near = begin(sems, (where_near, where_ref))
    stored = where_ref.shape[0]
    copies = own_fetch(steps, stored, blocks_ref, stiff_ref, sems.at[pl.ds(len(near), steps)])
    mix(stacked(g_ref[...]), field_ref, mixed_ref)
    finish(near)
    read = [(c, row) for row in range(own_ref.shape[0], where_ref.shape[1]) for c in range(stored)]
    receive_table(recv_ref, r_ref, [where_ref[c, row] for c, row in read])
    per = own_ref.shape[0] // steps
    for step in range(0, steps, TOGETHER):
        finish(copies[step:step + TOGETHER])
        for row in range(step * per, min(step + TOGETHER, steps) * per):
            own_ref[row] = block_row(
                row, own_ref.shape[1], where_ref, mixed_ref, stiff_ref[:, row * stored:(row + 1) * stored]
            )


def second_kernel(own_ref, arrived_ref, r_ref, g2_ref, send_ref, where_near, blocks_ref,
                  packed_ref, turned_hbm, turned_ref, spread_ref, stiff_ref, where_ref, sems):
    table = begin(sems.at[pl.ds(2, 1)], (where_near, where_ref))
    near = begin(sems, (last_stored(blocks_ref, stiff_ref), stiff_ref))
    turned = arrived_ref[...].astype(f32).T.astype(bf16)
    turned_ref[...] = turned
    keeps = begin(sems.at[pl.ds(len(near), 1)], (turned_ref, turned_hbm))
    finish(table)
    stored, out_blocks = where_ref.shape
    owned_blocks = own_ref.shape[0]
    terms = stiff_ref.shape[0]
    mixer = g2_ref[...]
    picks = []
    for row in range(owned_blocks, out_blocks):
        columns = [where_ref[c, row] for c in range(stored)]
        base = jnp.concatenate([own_ref[column] for column in columns], axis=1)
        first = (row - owned_blocks) * stored
        table = jnp.concatenate([r_ref[first + c] for c in range(stored)], axis=1)
        mixed = dot(mixer, (base + dot(turned, table)).astype(bf16)).astype(bf16)
        picks.append(jnp.concatenate([mixed[term * PAD:(term + 1) * PAD, :] for term in range(terms)], axis=1))
    width = send_ref.shape[1]
    lines = lax.broadcasted_iota(i32, (packed_ref.shape[0], width), 0) * QUARTERS
    place = jnp.concatenate([one_hot(send_ref[...] == lines + quarter) for quarter in range(QUARTERS)], axis=1)
    spread_ref[...] = jnp.zeros_like(spread_ref)
    finish(near)
    depth = terms * stored * LANES
    part = jnp.concatenate(
        [dot(picked, stiff_ref[:, at * stored:(at + 1) * stored].reshape(depth, LANES)) for at, picked in enumerate(picks)],
        axis=1,
    ).astype(bf16)
    for quarter in range(QUARTERS):
        spread_ref[quarter * PAD:(quarter + 1) * PAD, quarter * width:(quarter + 1) * width] = part
    packed_ref[...] = dot_t(place, spread_ref[...]).astype(bf16)
    finish(keeps)


def own_kernel(groups, steps, where_near, recv_ref, g2_ref, turned_hbm, own_ref, blocks_ref,
               first_hbm, own2_ref, r_ref, turned_ref, first_ref, field_ref, mixed_ref, stiff_ref, where_ref, sems):
    stored = where_ref.shape[0]
    near = begin(sems, (turned_hbm, turned_ref), (where_near, where_ref))
    copies = own_fetch(steps, stored, blocks_ref, stiff_ref, sems.at[pl.ds(len(near), steps)])
    me = lax.axis_index("mode")
    receive_table(recv_ref, r_ref, range(r_ref.shape[0]))
    owned_blocks, _, lanes = own_ref.shape
    finish(near)
    turned = turned_ref[...]
    for block in range(0, owned_blocks, 2):
        table = jnp.concatenate([r_ref[block], r_ref[block + 1]], axis=1)
        base = jnp.concatenate([own_ref[block], own_ref[block + 1]], axis=1)
        field = (base + dot(turned, table)).astype(bf16)
        for part in range(2):
            field_ref[block + part] = field[:, part * lanes:(part + 1) * lanes].reshape(groups, PAD, lanes)
    mix(g2_ref[...], field_ref, mixed_ref)
    for block in range(owned_blocks):
        first_ref[:, block * lanes:(block + 1) * lanes] = field_ref[block, me, :first_ref.shape[0], :]
    keeps = begin(sems.at[pl.ds(len(near) + steps, 1)], (first_ref, first_hbm))
    per = owned_blocks // steps
    for step in range(0, steps, TOGETHER):
        finish(copies[step:step + TOGETHER])
        for row in range(step * per, min(step + TOGETHER, steps) * per):
            own2_ref[:, row * lanes:(row + 1) * lanes] = block_row(
                row, PAD, where_ref, mixed_ref, stiff_ref[:, row * stored:(row + 1) * stored]
            )
    finish(keeps)


def last_kernel(own_ref, arrived_ref, r_ref, out_hbm, slots_ref, out_ref, sems):
    arrived = arrived_ref[...].astype(f32)
    lines = arrived.shape[0]
    for quarter in range(QUARTERS):
        turned = pltpu.roll(arrived, (QUARTERS - quarter) % QUARTERS * PAD, 1)
        slots_ref[pl.ds(quarter, lines, stride=QUARTERS), :] = turned
    by_slot = slots_ref[...].T[:PAD, :].astype(bf16)
    span = r_ref.shape[0] // sems.shape[0]
    copies = []
    for block in range(0, r_ref.shape[0], 2):
        at = slice(block * LANES, (block + 2) * LANES)
        table = jnp.concatenate([r_ref[block], r_ref[block + 1]], axis=1)
        total = own_ref[:, at] + dot(by_slot, table)
        out_ref[:, at] = total.astype(bf16)[:out_ref.shape[0], :]
        if (block + 2) % span == 0:
            part = pl.ds((block + 2 - span) * LANES, span * LANES)
            copies += begin(sems.at[pl.ds(len(copies), 1)], (out_ref.at[:, part], out_hbm.at[:, part]))
    finish(copies)


def local(groups, peers, modes_in, blocks, block_cols, send_slot, recv_row, mix_cols, mix_coef):
    terms, all_stored, blk, _ = blocks.shape
    out_blocks, stored = block_cols.shape
    modes_dev, owned = modes_in.shape
    owned_blocks = owned // blk
    interface = send_slot.shape[0]
    slots = recv_row.shape[0]
    cap = slots // peers
    rows = groups * PAD
    lines = slots // QUARTERS
    Shape, dma = jax.ShapeDtypeStruct, pltpu.SemaphoreType.DMA

    def pin(x):
        return pltpu.with_memory_space_constraint(x, pltpu.HBM)

    others = {
        s: lax.ppermute(modes_in, "mode", [((to + s) % groups, to) for to in range(groups)])
        for s in (2, 1, 3)
    }
    blocks = pin(blocks)
    where = pin(block_cols.T)
    mix_cols, mix_coef = pin(mix_cols.transpose(0, 2, 1)), pin(mix_coef.transpose(0, 2, 1))
    send, recv = pin(send_slot.reshape(1, interface)), pin(recv_row.reshape(1, slots))
    tables = [pltpu.VMEM(mix_cols.shape, i32), pltpu.VMEM(mix_coef.shape, f32)]
    if_blocks = (terms, (out_blocks - owned_blocks) * stored, blk, blk)
    own_scratch = pltpu.VMEM((terms, owned_blocks * stored, blk, blk), bf16)
    field_shape, mixer_shape = (owned_blocks, groups, PAD, blk), (rows, terms * rows)
    field_scratch = pltpu.VMEM(field_shape, bf16)
    block_flops = 2 * terms * stored * blk * blk
    wide, narrow = (owned_blocks, terms * rows, blk), (owned_blocks, terms * PAD, blk)

    where_scratch = pltpu.SMEM(where.shape, i32)
    own_shape, table_shape = (owned_blocks, rows, blk), (owned_blocks, slots, blk)

    g, g2, place, send, recv, own_field, where, stiff = call(
        functools.partial(setup_kernel, groups),
        [Shape(mixer_shape, bf16), Shape((terms * PAD, rows), bf16), Shape((slots, interface), bf16), Shape(send.shape, i32),
         Shape(recv.shape, i32), Shape((modes_dev, owned), bf16), Shape(where.shape, i32), Shape(if_blocks, bf16)],
        [mix_cols, mix_coef, send, recv, pin(modes_in), where, blocks], [HBM] * 7, [VMEM] * 8, flops=10**6,
        scratch=[*tables, dma((7,))],
    )
    packed, field = call(
        functools.partial(first_kernel, groups),
        [Shape((slots, rows), bf16), Shape(field_shape, bf16)],
        [own_field, others[1], others[2], others[3], g, place, where, stiff],
        [VMEM] * 8, [VMEM] * 2,
        flops=block_flops * (out_blocks - owned_blocks) * rows, scratch=[where_scratch, dma((1,))],
    )
    arrived = lax.all_to_all(packed.reshape(peers, cap, rows), "space", split_axis=0, concat_axis=0, tiled=True)
    steps = owned_blocks // 2
    own, r = call(
        functools.partial(between_kernel, steps), [Shape(own_shape, f32), Shape((if_blocks[1], slots, blk), bf16)],
        [field, g, recv, where, blocks], [VMEM] * 4 + [HBM], [VMEM] * 2,
        flops=block_flops * owned_blocks * rows,
        scratch=[pltpu.VMEM(wide, bf16), own_scratch, where_scratch, dma((1 + steps,))],
    )
    packed2, turned = call(
        second_kernel, [Shape((lines, QUARTERS * PAD), bf16), pltpu.HBM((rows, slots), bf16)],
        [own, arrived.reshape(slots, rows), r, g2, send, where, blocks], [VMEM] * 6 + [HBM], [VMEM, HBM],
        flops=2 * slots * rows * owned,
        scratch=[pltpu.VMEM((rows, slots), bf16), pltpu.VMEM((QUARTERS * PAD, QUARTERS * interface), bf16), pltpu.VMEM(if_blocks, bf16), where_scratch, dma((3,))],
    )
    arrived2 = lax.all_to_all(
        packed2.reshape(peers, cap // QUARTERS, QUARTERS * PAD), "space", split_axis=0, concat_axis=0, tiled=True
    )
    first_apply, own2, r2 = call(
        functools.partial(own_kernel, groups, steps),
        [pltpu.HBM((modes_dev, owned), bf16), Shape((PAD, owned), f32), Shape(table_shape, bf16)],
        [where, recv, g2, pin(turned), own, blocks], [VMEM, VMEM, VMEM, HBM, VMEM, HBM], [HBM, VMEM, VMEM],
        flops=block_flops * owned_blocks * PAD,
        scratch=[pltpu.VMEM((rows, slots), bf16), pltpu.VMEM((modes_dev, owned), bf16), field_scratch, pltpu.VMEM(narrow, bf16),
                 own_scratch, where_scratch, dma((3 + steps,))],
    )
    second_apply = call(
        last_kernel, [pltpu.HBM((modes_dev, owned), bf16)],
        [own2, arrived2.reshape(lines, QUARTERS * PAD), r2], [VMEM] * 3, [HBM], flops=2 * slots * PAD * owned,
        scratch=[pltpu.VMEM((slots, QUARTERS * PAD), f32), pltpu.VMEM((modes_dev, owned), bf16), dma((owned_blocks // 4,))],
    )[0]
    return (first_apply, second_apply)


def solution(mesh):
    in_specs = (
        P("mode", "space"),
        P(None, "space", None, None),
        P("space", None),
        P("space"),
        P("space"),
        P(),
        P(),
    )
    out_specs = (P("mode", "space"), P("mode", "space"))
    body = functools.partial(local, mesh.shape["mode"], mesh.shape["space"])
    return jax.shard_map(body, mesh=mesh, in_specs=in_specs, out_specs=out_specs, check_vma=False)
```

```python
import functools
import math

import jax
import jax.numpy as jnp
from jax import lax
from jax.experimental import pallas as pl
from jax.experimental.pallas import tpu as pltpu
from jax.sharding import PartitionSpec as P

LANES = 128
PAD = 32
QUARTERS = 4
TOGETHER = 2

VMEM = pl.BlockSpec(memory_space=pltpu.VMEM)
HBM = pl.BlockSpec(memory_space=pltpu.HBM)
VMEM_LIMIT = 32 * 1024 * 1024
bf16, f32, i32 = jnp.bfloat16, jnp.float32, jnp.int32


def call(kernel, outs, ins, in_specs, out_specs, flops, scratch=()):
    moved = sum(math.prod(a.shape) * jnp.dtype(a.dtype).itemsize for a in [*outs, *ins])
    return pl.pallas_call(
        kernel,
        out_shape=outs,
        in_specs=in_specs,
        out_specs=out_specs,
        scratch_shapes=scratch,
        compiler_params=pltpu.CompilerParams(vmem_limit_bytes=VMEM_LIMIT),
        cost_estimate=pl.CostEstimate(flops=flops, bytes_accessed=moved, transcendentals=0),
    )(*ins)


def begin(sems, *pairs):
    copies = [pltpu.make_async_copy(source, target, sems.at[at]) for at, (source, target) in enumerate(pairs)]
    for copy in copies:
        copy.start()
    return copies


def finish(copies):
    for copy in copies:
        copy.wait()


def one_hot(hit):
    return jnp.where(hit, 1.0, 0.0).astype(bf16)


def dot(a, b):
    return jnp.dot(a, b, preferred_element_type=f32)


def dot_t(a, b):
    return lax.dot_general(a, b, (((1,), (1,)), ((), ())), preferred_element_type=f32)


def padded_place(modes, groups, modes_dev):
    place = modes
    for group in range(1, groups):
        place += jnp.where(modes >= group * modes_dev, PAD - modes_dev, 0)
    return place


def mixer_columns(term, groups, cols_ref, coef_ref):
    modes = cols_ref.shape[2]
    cols = cols_ref[term]
    place = jnp.where(cols < modes, padded_place(cols, groups, modes // groups), -1)
    coef = coef_ref[term]
    want = lax.broadcasted_iota(i32, (groups * PAD, modes), 0)
    total = jnp.zeros(want.shape, f32)
    for slot in range(cols.shape[0]):
        total += jnp.where(place[slot:slot + 1, :] == want, coef[slot:slot + 1, :], 0.0)
    return total.astype(bf16)


def receive_table(recv_ref, r_ref, blocks):
    slots = recv_ref.shape[1]
    lanes = lax.broadcasted_iota(i32, (LANES, LANES), 1)
    for start in range(0, slots, LANES):
        at = slice(start, start + LANES)
        offset = jnp.broadcast_to(recv_ref[:, at].astype(f32), (LANES, LANES)).T.astype(i32) - lanes
        for place, block in enumerate(blocks):
            r_ref[place, at, :] = one_hot(offset == block * LANES)


def block_row(row, rows, cols_ref, mixed_ref, stiff):
    terms, stored = stiff.shape[:2]
    picked = jnp.concatenate(
        [
            mixed_ref[cols_ref[c, row], term * rows:(term + 1) * rows, :]
            for term in range(terms)
            for c in range(stored)
        ],
        axis=1,
    )
    return dot(picked, stiff.reshape(terms * stored * LANES, LANES))


def mix(mixer, field_ref, mixed_ref):
    blocks, groups, pad, lanes = field_ref.shape
    for block in range(0, blocks, 2):
        pair = [field_ref[block + part].reshape(groups * pad, lanes) for part in range(2)]
        mixed = dot(mixer, jnp.concatenate(pair, axis=1)).astype(bf16)
        for part in range(2):
            mixed_ref[block + part] = mixed[:, part * lanes:(part + 1) * lanes]


def stacked(wide):
    return jnp.concatenate([wide[:, at:at + LANES] for at in range(0, wide.shape[1], LANES)], axis=0)


def last_stored(blocks_ref, stiff_ref):
    count = stiff_ref.shape[1]
    return blocks_ref.at[:, pl.ds(blocks_ref.shape[1] - count, count)]


def mixed_row(picked, stiff, mixer):
    terms, stored = stiff.shape[:2]
    wide = jnp.concatenate([stiff[term].reshape(stored * LANES, LANES) for term in range(terms)], axis=1)
    product = dot(picked, wide).astype(bf16)
    return dot(mixer, jnp.concatenate([product[:, term * LANES:(term + 1) * LANES] for term in range(terms)], axis=0))


def setup_kernel(groups, cols_hbm, coef_hbm, send_hbm, recv_hbm, own_hbm, where_hbm, blocks_ref,
                 g_ref, g2_ref, place_ref, send_ref, recv_ref, own_ref, where_ref, stiff_ref, cols_ref, coef_ref, sems):
    copies = begin(
        sems, (cols_hbm, cols_ref), (coef_hbm, coef_ref), (send_hbm, send_ref), (own_hbm, own_ref),
        (where_hbm, where_ref), (recv_hbm, recv_ref), (last_stored(blocks_ref, stiff_ref), stiff_ref),
    )
    me = lax.axis_index("mode")
    modes = cols_ref.shape[2]
    rows = groups * PAD
    out_mode = lax.broadcasted_iota(i32, (rows, modes), 1)
    spread = one_hot(padded_place(out_mode, groups, modes // groups) == lax.broadcasted_iota(i32, (rows, modes), 0))
    finish(copies[:3])
    modes_dev = modes // groups
    row = lax.broadcasted_iota(i32, (PAD, modes), 0)
    mine = one_hot((lax.broadcasted_iota(i32, (PAD, modes), 1) == row + me * modes_dev) & (row < modes_dev))
    for term in range(cols_ref.shape[0]):
        columns = mixer_columns(term, groups, cols_ref, coef_ref)
        g_ref[:, term * rows:(term + 1) * rows] = dot_t(spread, columns).astype(bf16)
        g2_ref[term * PAD:(term + 1) * PAD, :] = dot_t(mine, columns).astype(bf16)
    place_ref[...] = one_hot(send_ref[...] == lax.broadcasted_iota(i32, place_ref.shape, 0))
    finish(copies[3:])


def first_kernel(groups, v0, v1, v2, v3, g_ref, place_ref, where_near, stiff_ref,
                 packed_ref, field_ref, where_ref, sems):
    table = begin(sems, (where_near, where_ref))
    me = lax.axis_index("mode")
    owned_blocks, _, _, lanes = field_ref.shape
    modes_dev = v0.shape[0]
    field_ref[:, :, modes_dev:, :] = jnp.zeros_like(field_ref[:, :, modes_dev:, :])
    for slot, source in enumerate((v0, v1, v2, v3)):
        group = lax.rem(me + slot, groups)
        for block in range(owned_blocks):
            field_ref[block, group, :modes_dev, :] = source[:, block * lanes:(block + 1) * lanes]
    finish(table)
    mixer = g_ref[...]
    stored, out_blocks = where_ref.shape
    parts = []
    for row in range(owned_blocks, out_blocks):
        picked = jnp.concatenate(
            [field_ref[where_ref[c, row]].reshape(groups * PAD, lanes) for c in range(stored)], axis=1
        )
        at = (row - owned_blocks) * stored
        parts.append(mixed_row(picked, stiff_ref[:, at:at + stored], mixer))
    part = jnp.concatenate(parts, axis=1).astype(bf16)
    packed_ref[...] = dot_t(place_ref[...], part).astype(bf16)


def own_fetch(steps, stored, blocks_ref, stiff_ref, sems):
    count = stiff_ref.shape[1] // steps
    parts = [pl.ds(step * count, count) for step in range(steps)]
    return begin(sems, *((blocks_ref.at[:, part], stiff_ref.at[:, part]) for part in parts))


def between_kernel(steps, field_ref, g_ref, recv_ref, where_near, blocks_ref,
                   own_ref, r_ref, mixed_ref, stiff_ref, where_ref, sems):
    near = begin(sems, (where_near, where_ref))
    stored = where_ref.shape[0]
    copies = own_fetch(steps, stored, blocks_ref, stiff_ref, sems.at[pl.ds(len(near), steps)])
    mix(stacked(g_ref[...]), field_ref, mixed_ref)
    finish(near)
    read = [(c, row) for row in range(own_ref.shape[0], where_ref.shape[1]) for c in range(stored)]
    receive_table(recv_ref, r_ref, [where_ref[c, row] for c, row in read])
    per = own_ref.shape[0] // steps
    for step in range(0, steps, TOGETHER):
        finish(copies[step:step + TOGETHER])
        for row in range(step * per, min(step + TOGETHER, steps) * per):
            own_ref[row] = block_row(
                row, own_ref.shape[1], where_ref, mixed_ref, stiff_ref[:, row * stored:(row + 1) * stored]
            )


def second_kernel(own_ref, arrived_ref, r_ref, g2_ref, send_ref, where_near, blocks_ref,
                  packed_ref, turned_hbm, turned_ref, spread_ref, stiff_ref, where_ref, sems):
    table = begin(sems.at[pl.ds(2, 1)], (where_near, where_ref))
    near = begin(sems, (last_stored(blocks_ref, stiff_ref), stiff_ref))
    turned = arrived_ref[...].astype(f32).T.astype(bf16)
    turned_ref[...] = turned
    keeps = begin(sems.at[pl.ds(len(near), 1)], (turned_ref, turned_hbm))
    finish(table)
    stored, out_blocks = where_ref.shape
    owned_blocks = own_ref.shape[0]
    terms = stiff_ref.shape[0]
    mixer = g2_ref[...]
    picks = []
    for row in range(owned_blocks, out_blocks):
        columns = [where_ref[c, row] for c in range(stored)]
        base = jnp.concatenate([own_ref[column] for column in columns], axis=1)
        first = (row - owned_blocks) * stored
        table = jnp.concatenate([r_ref[first + c] for c in range(stored)], axis=1)
        mixed = dot(mixer, (base + dot(turned, table)).astype(bf16)).astype(bf16)
        picks.append(jnp.concatenate([mixed[term * PAD:(term + 1) * PAD, :] for term in range(terms)], axis=1))
    width = send_ref.shape[1]
    lines = lax.broadcasted_iota(i32, (packed_ref.shape[0], width), 0) * QUARTERS
    place = jnp.concatenate([one_hot(send_ref[...] == lines + quarter) for quarter in range(QUARTERS)], axis=1)
    spread_ref[...] = jnp.zeros_like(spread_ref)
    finish(near)
    depth = terms * stored * LANES
    part = jnp.concatenate(
        [dot(picked, stiff_ref[:, at * stored:(at + 1) * stored].reshape(depth, LANES)) for at, picked in enumerate(picks)],
        axis=1,
    ).astype(bf16)
    for quarter in range(QUARTERS):
        spread_ref[quarter * PAD:(quarter + 1) * PAD, quarter * width:(quarter + 1) * width] = part
    packed_ref[...] = dot_t(place, spread_ref[...]).astype(bf16)
    finish(keeps)


def own_kernel(groups, steps, where_near, recv_ref, g2_ref, turned_hbm, own_ref, blocks_ref,
               first_hbm, own2_ref, r_ref, turned_ref, first_ref, field_ref, mixed_ref, stiff_ref, where_ref, sems):
    stored = where_ref.shape[0]
    near = begin(sems, (turned_hbm, turned_ref), (where_near, where_ref))
    copies = own_fetch(steps, stored, blocks_ref, stiff_ref, sems.at[pl.ds(len(near), steps)])
    me = lax.axis_index("mode")
    receive_table(recv_ref, r_ref, range(r_ref.shape[0]))
    owned_blocks, _, lanes = own_ref.shape
    finish(near)
    turned = turned_ref[...]
    for block in range(0, owned_blocks, 2):
        table = jnp.concatenate([r_ref[block], r_ref[block + 1]], axis=1)
        base = jnp.concatenate([own_ref[block], own_ref[block + 1]], axis=1)
        field = (base + dot(turned, table)).astype(bf16)
        for part in range(2):
            field_ref[block + part] = field[:, part * lanes:(part + 1) * lanes].reshape(groups, PAD, lanes)
    mix(g2_ref[...], field_ref, mixed_ref)
    for block in range(owned_blocks):
        first_ref[:, block * lanes:(block + 1) * lanes] = field_ref[block, me, :first_ref.shape[0], :]
    keeps = begin(sems.at[pl.ds(len(near) + steps, 1)], (first_ref, first_hbm))
    per = owned_blocks // steps
    for step in range(0, steps, TOGETHER):
        finish(copies[step:step + TOGETHER])
        for row in range(step * per, min(step + TOGETHER, steps) * per):
            own2_ref[:, row * lanes:(row + 1) * lanes] = block_row(
                row, PAD, where_ref, mixed_ref, stiff_ref[:, row * stored:(row + 1) * stored]
            )
    finish(keeps)


def last_kernel(own_ref, arrived_ref, r_ref, out_hbm, slots_ref, out_ref, sems):
    arrived = arrived_ref[...].astype(f32)
    lines = arrived.shape[0]
    for quarter in range(QUARTERS):
        turned = pltpu.roll(arrived, (QUARTERS - quarter) % QUARTERS * PAD, 1)
        slots_ref[pl.ds(quarter, lines, stride=QUARTERS), :] = turned
    by_slot = slots_ref[...].T[:PAD, :].astype(bf16)
    span = r_ref.shape[0] // sems.shape[0]
    copies = []
    for block in range(0, r_ref.shape[0], 2):
        at = slice(block * LANES, (block + 2) * LANES)
        table = jnp.concatenate([r_ref[block], r_ref[block + 1]], axis=1)
        total = own_ref[:, at] + dot(by_slot, table)
        out_ref[:, at] = total.astype(bf16)[:out_ref.shape[0], :]
        if (block + 2) % span == 0:
            part = pl.ds((block + 2 - span) * LANES, span * LANES)
            copies += begin(sems.at[pl.ds(len(copies), 1)], (out_ref.at[:, part], out_hbm.at[:, part]))
    finish(copies)


def local(groups, peers, modes_in, blocks, block_cols, send_slot, recv_row, mix_cols, mix_coef):
    terms, all_stored, blk, _ = blocks.shape
    out_blocks, stored = block_cols.shape
    modes_dev, owned = modes_in.shape
    owned_blocks = owned // blk
    interface = send_slot.shape[0]
    slots = recv_row.shape[0]
    cap = slots // peers
    rows = groups * PAD
    lines = slots // QUARTERS
    Shape, dma = jax.ShapeDtypeStruct, pltpu.SemaphoreType.DMA

    def pin(x):
        return pltpu.with_memory_space_constraint(x, pltpu.HBM)

    def from_group(field, s):
        return lax.ppermute(field, "mode", [((to + s) % groups, to) for to in range(groups)])

    others = {s: from_group(modes_in, s) for s in (3, 2)}
    blocks = pin(blocks)
    where = pin(block_cols.T)
    mix_cols, mix_coef = pin(mix_cols.transpose(0, 2, 1)), pin(mix_coef.transpose(0, 2, 1))
    send, recv = pin(send_slot.reshape(1, interface)), pin(recv_row.reshape(1, slots))
    tables = [pltpu.VMEM(mix_cols.shape, i32), pltpu.VMEM(mix_coef.shape, f32)]
    if_blocks = (terms, (out_blocks - owned_blocks) * stored, blk, blk)
    own_scratch = pltpu.VMEM((terms, owned_blocks * stored, blk, blk), bf16)
    field_shape, mixer_shape = (owned_blocks, groups, PAD, blk), (rows, terms * rows)
    field_scratch = pltpu.VMEM(field_shape, bf16)
    block_flops = 2 * terms * stored * blk * blk
    wide, narrow = (owned_blocks, terms * rows, blk), (owned_blocks, terms * PAD, blk)

    where_scratch = pltpu.SMEM(where.shape, i32)
    own_shape, table_shape = (owned_blocks, rows, blk), (owned_blocks, slots, blk)

    g, g2, place, send, recv, own_field, where, stiff = call(
        functools.partial(setup_kernel, groups),
        [Shape(mixer_shape, bf16), Shape((terms * PAD, rows), bf16), Shape((slots, interface), bf16), Shape(send.shape, i32),
         Shape(recv.shape, i32), Shape((modes_dev, owned), bf16), Shape(where.shape, i32), Shape(if_blocks, bf16)],
        [mix_cols, mix_coef, send, recv, pin(modes_in), where, blocks], [HBM] * 7, [VMEM] * 8, flops=10**6,
        scratch=[*tables, dma((7,))],
    )
    others[1] = from_group(own_field, 1)
    packed, field = call(
        functools.partial(first_kernel, groups),
        [Shape((slots, rows), bf16), Shape(field_shape, bf16)],
        [own_field, others[1], others[2], others[3], g, place, where, stiff],
        [VMEM] * 8, [VMEM] * 2,
        flops=block_flops * (out_blocks - owned_blocks) * rows, scratch=[where_scratch, dma((1,))],
    )
    arrived = lax.all_to_all(packed.reshape(peers, cap, rows), "space", split_axis=0, concat_axis=0, tiled=True)
    steps = owned_blocks // 2
    own, r = call(
        functools.partial(between_kernel, steps), [Shape(own_shape, f32), Shape((if_blocks[1], slots, blk), bf16)],
        [field, g, recv, where, blocks], [VMEM] * 4 + [HBM], [VMEM] * 2,
        flops=block_flops * owned_blocks * rows,
        scratch=[pltpu.VMEM(wide, bf16), own_scratch, where_scratch, dma((1 + steps,))],
    )
    packed2, turned = call(
        second_kernel, [Shape((lines, QUARTERS * PAD), bf16), pltpu.HBM((rows, slots), bf16)],
        [own, arrived.reshape(slots, rows), r, g2, send, where, blocks], [VMEM] * 6 + [HBM], [VMEM, HBM],
        flops=2 * slots * rows * owned,
        scratch=[pltpu.VMEM((rows, slots), bf16), pltpu.VMEM((QUARTERS * PAD, QUARTERS * interface), bf16), pltpu.VMEM(if_blocks, bf16), where_scratch, dma((3,))],
    )
    arrived2 = lax.all_to_all(
        packed2.reshape(peers, cap // QUARTERS, QUARTERS * PAD), "space", split_axis=0, concat_axis=0, tiled=True
    )
    first_apply, own2, r2 = call(
        functools.partial(own_kernel, groups, steps),
        [pltpu.HBM((modes_dev, owned), bf16), Shape((PAD, owned), f32), Shape(table_shape, bf16)],
        [where, recv, g2, pin(turned), own, blocks], [VMEM, VMEM, VMEM, HBM, VMEM, HBM], [HBM, VMEM, VMEM],
        flops=block_flops * owned_blocks * PAD,
        scratch=[pltpu.VMEM((rows, slots), bf16), pltpu.VMEM((modes_dev, owned), bf16), field_scratch, pltpu.VMEM(narrow, bf16),
                 own_scratch, where_scratch, dma((3 + steps,))],
    )
    second_apply = call(
        last_kernel, [pltpu.HBM((modes_dev, owned), bf16)],
        [own2, arrived2.reshape(lines, QUARTERS * PAD), r2], [VMEM] * 3, [HBM], flops=2 * slots * PAD * owned,
        scratch=[pltpu.VMEM((slots, QUARTERS * PAD), f32), pltpu.VMEM((modes_dev, owned), bf16), dma((owned_blocks // 4,))],
    )[0]
    return (first_apply, second_apply)


def solution(mesh):
    in_specs = (
        P("mode", "space"),
        P(None, "space", None, None),
        P("space", None),
        P("space"),
        P("space"),
        P(),
        P(),
    )
    out_specs = (P("mode", "space"), P("mode", "space"))
    body = functools.partial(local, mesh.shape["mode"], mesh.shape["space"])
    return jax.shard_map(body, mesh=mesh, in_specs=in_specs, out_specs=out_specs, check_vma=False)
```

```python
import functools
import math

import jax
import jax.numpy as jnp
from jax import lax
from jax.experimental import pallas as pl
from jax.experimental.pallas import tpu as pltpu
from jax.sharding import PartitionSpec as P

LANES = 128
PAD = 32
QUARTERS = 4
TOGETHER = 2

VMEM = pl.BlockSpec(memory_space=pltpu.VMEM)
HBM = pl.BlockSpec(memory_space=pltpu.HBM)
VMEM_LIMIT = 32 * 1024 * 1024
bf16, f32, i32 = jnp.bfloat16, jnp.float32, jnp.int32


def call(kernel, outs, ins, in_specs, out_specs, flops, scratch=()):
    moved = sum(math.prod(a.shape) * jnp.dtype(a.dtype).itemsize for a in [*outs, *ins])
    return pl.pallas_call(
        kernel,
        out_shape=outs,
        in_specs=in_specs,
        out_specs=out_specs,
        scratch_shapes=scratch,
        compiler_params=pltpu.CompilerParams(vmem_limit_bytes=VMEM_LIMIT),
        cost_estimate=pl.CostEstimate(flops=flops, bytes_accessed=moved, transcendentals=0),
    )(*ins)


def begin(sems, *pairs):
    copies = [pltpu.make_async_copy(source, target, sems.at[at]) for at, (source, target) in enumerate(pairs)]
    for copy in copies:
        copy.start()
    return copies


def finish(copies):
    for copy in copies:
        copy.wait()


def one_hot(hit):
    return jnp.where(hit, 1.0, 0.0).astype(bf16)


def dot(a, b):
    return jnp.dot(a, b, preferred_element_type=f32)


def dot_t(a, b):
    return lax.dot_general(a, b, (((1,), (1,)), ((), ())), preferred_element_type=f32)


def padded_place(modes, groups, modes_dev):
    place = modes
    for group in range(1, groups):
        place += jnp.where(modes >= group * modes_dev, PAD - modes_dev, 0)
    return place


def mixer_columns(term, groups, cols_ref, coef_ref):
    modes = cols_ref.shape[2]
    cols = cols_ref[term]
    place = jnp.where(cols < modes, padded_place(cols, groups, modes // groups), -1)
    coef = coef_ref[term]
    want = lax.broadcasted_iota(i32, (groups * PAD, modes), 0)
    total = jnp.zeros(want.shape, f32)
    for slot in range(cols.shape[0]):
        total += jnp.where(place[slot:slot + 1, :] == want, coef[slot:slot + 1, :], 0.0)
    return total.astype(bf16)


def receive_table(recv_ref, r_ref, blocks):
    slots = recv_ref.shape[1]
    lanes = lax.broadcasted_iota(i32, (LANES, LANES), 1)
    for start in range(0, slots, LANES):
        at = slice(start, start + LANES)
        offset = jnp.broadcast_to(recv_ref[:, at].astype(f32), (LANES, LANES)).T.astype(i32) - lanes
        for place, block in enumerate(blocks):
            r_ref[place, at, :] = one_hot(offset == block * LANES)


def block_row(row, rows, cols_ref, mixed_ref, stiff):
    terms, stored = stiff.shape[:2]
    picked = jnp.concatenate(
        [
            mixed_ref[cols_ref[c, row], term * rows:(term + 1) * rows, :]
            for term in range(terms)
            for c in range(stored)
        ],
        axis=1,
    )
    return dot(picked, stiff.reshape(terms * stored * LANES, LANES))


def mix(mixer, field_ref, mixed_ref):
    blocks, groups, pad, lanes = field_ref.shape
    for block in range(0, blocks, 2):
        pair = [field_ref[block + part].reshape(groups * pad, lanes) for part in range(2)]
        mixed = dot(mixer, jnp.concatenate(pair, axis=1)).astype(bf16)
        for part in range(2):
            mixed_ref[block + part] = mixed[:, part * lanes:(part + 1) * lanes]


def stacked(wide):
    return jnp.concatenate([wide[:, at:at + LANES] for at in range(0, wide.shape[1], LANES)], axis=0)


def last_stored(blocks_ref, stiff_ref):
    count = stiff_ref.shape[1]
    return blocks_ref.at[:, pl.ds(blocks_ref.shape[1] - count, count)]


def mixed_row(picked, stiff, mixer):
    terms, stored = stiff.shape[:2]
    wide = jnp.concatenate([stiff[term].reshape(stored * LANES, LANES) for term in range(terms)], axis=1)
    product = dot(picked, wide).astype(bf16)
    return dot(mixer, jnp.concatenate([product[:, term * LANES:(term + 1) * LANES] for term in range(terms)], axis=0))


def setup_kernel(groups, cols_hbm, coef_hbm, send_hbm, recv_hbm, own_hbm, where_hbm, blocks_ref,
                 g_ref, g2_ref, place_ref, send_ref, recv_ref, own_ref, where_ref, stiff_ref, cols_ref, coef_ref, sems):
    copies = begin(
        sems, (cols_hbm, cols_ref), (coef_hbm, coef_ref), (send_hbm, send_ref),
        (last_stored(blocks_ref, stiff_ref), stiff_ref), (own_hbm, own_ref), (where_hbm, where_ref), (recv_hbm, recv_ref),
    )
    me = lax.axis_index("mode")
    modes = cols_ref.shape[2]
    rows = groups * PAD
    out_mode = lax.broadcasted_iota(i32, (rows, modes), 1)
    spread = one_hot(padded_place(out_mode, groups, modes // groups) == lax.broadcasted_iota(i32, (rows, modes), 0))
    finish(copies[:3])
    modes_dev = modes // groups
    row = lax.broadcasted_iota(i32, (PAD, modes), 0)
    mine = one_hot((lax.broadcasted_iota(i32, (PAD, modes), 1) == row + me * modes_dev) & (row < modes_dev))
    for term in range(cols_ref.shape[0]):
        columns = mixer_columns(term, groups, cols_ref, coef_ref)
        g_ref[:, term * rows:(term + 1) * rows] = dot_t(spread, columns).astype(bf16)
        g2_ref[term * PAD:(term + 1) * PAD, :] = dot_t(mine, columns).astype(bf16)
    place_ref[...] = one_hot(send_ref[...] == lax.broadcasted_iota(i32, place_ref.shape, 0))
    finish(copies[3:])


def first_kernel(groups, v0, v1, v2, v3, g_ref, place_ref, where_near, stiff_ref,
                 packed_ref, field_ref, where_ref, sems):
    table = begin(sems, (where_near, where_ref))
    me = lax.axis_index("mode")
    owned_blocks, _, _, lanes = field_ref.shape
    modes_dev = v0.shape[0]
    field_ref[:, :, modes_dev:, :] = jnp.zeros_like(field_ref[:, :, modes_dev:, :])
    for slot, source in enumerate((v0, v1, v2, v3)):
        group = lax.rem(me + slot, groups)
        for block in range(owned_blocks):
            field_ref[block, group, :modes_dev, :] = source[:, block * lanes:(block + 1) * lanes]
    finish(table)
    mixer = g_ref[...]
    stored, out_blocks = where_ref.shape
    parts = []
    for row in range(owned_blocks, out_blocks):
        picked = jnp.concatenate(
            [field_ref[where_ref[c, row]].reshape(groups * PAD, lanes) for c in range(stored)], axis=1
        )
        at = (row - owned_blocks) * stored
        parts.append(mixed_row(picked, stiff_ref[:, at:at + stored], mixer))
    part = jnp.concatenate(parts, axis=1).astype(bf16)
    packed_ref[...] = dot_t(place_ref[...], part).astype(bf16)


def own_fetch(steps, stored, blocks_ref, stiff_ref, sems):
    count = stiff_ref.shape[1] // steps
    parts = [pl.ds(step * count, count) for step in range(steps)]
    return begin(sems, *((blocks_ref.at[:, part], stiff_ref.at[:, part]) for part in parts))


def between_kernel(steps, field_ref, g_ref, recv_ref, where_near, blocks_ref,
                   own_ref, r_ref, mixed_ref, stiff_ref, where_ref, sems):
    near = begin(sems, (where_near, where_ref))
    stored = where_ref.shape[0]
    copies = own_fetch(steps, stored, blocks_ref, stiff_ref, sems.at[pl.ds(len(near), steps)])
    mix(stacked(g_ref[...]), field_ref, mixed_ref)
    finish(near)
    read = [(c, row) for row in range(own_ref.shape[0], where_ref.shape[1]) for c in range(stored)]
    receive_table(recv_ref, r_ref, [where_ref[c, row] for c, row in read])
    per = own_ref.shape[0] // steps
    for step in range(0, steps, TOGETHER):
        finish(copies[step:step + TOGETHER])
        for row in range(step * per, min(step + TOGETHER, steps) * per):
            own_ref[row] = block_row(
                row, own_ref.shape[1], where_ref, mixed_ref, stiff_ref[:, row * stored:(row + 1) * stored]
            )


def second_kernel(own_ref, arrived_ref, r_ref, g2_ref, send_ref, where_near, blocks_ref,
                  packed_ref, turned_hbm, turned_ref, spread_ref, stiff_ref, where_ref, sems):
    table = begin(sems.at[pl.ds(2, 1)], (where_near, where_ref))
    near = begin(sems, (last_stored(blocks_ref, stiff_ref), stiff_ref))
    turned = arrived_ref[...].astype(f32).T.astype(bf16)
    turned_ref[...] = turned
    keeps = begin(sems.at[pl.ds(len(near), 1)], (turned_ref, turned_hbm))
    finish(table)
    stored, out_blocks = where_ref.shape
    owned_blocks = own_ref.shape[0]
    terms = stiff_ref.shape[0]
    mixer = g2_ref[...]
    picks = []
    for row in range(owned_blocks, out_blocks):
        columns = [where_ref[c, row] for c in range(stored)]
        base = jnp.concatenate([own_ref[column] for column in columns], axis=1)
        first = (row - owned_blocks) * stored
        table = jnp.concatenate([r_ref[first + c] for c in range(stored)], axis=1)
        mixed = dot(mixer, (base + dot(turned, table)).astype(bf16)).astype(bf16)
        picks.append(jnp.concatenate([mixed[term * PAD:(term + 1) * PAD, :] for term in range(terms)], axis=1))
    width = send_ref.shape[1]
    lines = lax.broadcasted_iota(i32, (packed_ref.shape[0], width), 0) * QUARTERS
    place = jnp.concatenate([one_hot(send_ref[...] == lines + quarter) for quarter in range(QUARTERS)], axis=1)
    spread_ref[...] = jnp.zeros_like(spread_ref)
    finish(near)
    depth = terms * stored * LANES
    part = jnp.concatenate(
        [dot(picked, stiff_ref[:, at * stored:(at + 1) * stored].reshape(depth, LANES)) for at, picked in enumerate(picks)],
        axis=1,
    ).astype(bf16)
    for quarter in range(QUARTERS):
        spread_ref[quarter * PAD:(quarter + 1) * PAD, quarter * width:(quarter + 1) * width] = part
    packed_ref[...] = dot_t(place, spread_ref[...]).astype(bf16)
    finish(keeps)


def own_kernel(groups, steps, where_near, recv_ref, g2_ref, turned_hbm, own_ref, blocks_ref,
               first_hbm, own2_ref, r_ref, turned_ref, first_ref, field_ref, mixed_ref, stiff_ref, where_ref, sems):
    stored = where_ref.shape[0]
    near = begin(sems, (turned_hbm, turned_ref), (where_near, where_ref))
    copies = own_fetch(steps, stored, blocks_ref, stiff_ref, sems.at[pl.ds(len(near), steps)])
    me = lax.axis_index("mode")
    receive_table(recv_ref, r_ref, range(r_ref.shape[0]))
    owned_blocks, _, lanes = own_ref.shape
    finish(near)
    turned = turned_ref[...]
    for block in range(0, owned_blocks, 2):
        table = jnp.concatenate([r_ref[block], r_ref[block + 1]], axis=1)
        base = jnp.concatenate([own_ref[block], own_ref[block + 1]], axis=1)
        field = (base + dot(turned, table)).astype(bf16)
        for part in range(2):
            field_ref[block + part] = field[:, part * lanes:(part + 1) * lanes].reshape(groups, PAD, lanes)
    mix(g2_ref[...], field_ref, mixed_ref)
    for block in range(owned_blocks):
        first_ref[:, block * lanes:(block + 1) * lanes] = field_ref[block, me, :first_ref.shape[0], :]
    keeps = begin(sems.at[pl.ds(len(near) + steps, 1)], (first_ref, first_hbm))
    per = owned_blocks // steps
    for step in range(steps):
        copies[step].wait()
        for row in range(step * per, (step + 1) * per):
            own2_ref[:, row * lanes:(row + 1) * lanes] = block_row(
                row, PAD, where_ref, mixed_ref, stiff_ref[:, row * stored:(row + 1) * stored]
            )
    finish(keeps)


def last_kernel(own_ref, arrived_ref, r_ref, out_hbm, slots_ref, out_ref, sems):
    arrived = arrived_ref[...].astype(f32)
    lines = arrived.shape[0]
    for quarter in range(QUARTERS):
        turned = pltpu.roll(arrived, (QUARTERS - quarter) % QUARTERS * PAD, 1)
        slots_ref[pl.ds(quarter, lines, stride=QUARTERS), :] = turned
    by_slot = slots_ref[...].T[:PAD, :].astype(bf16)
    span = r_ref.shape[0] // sems.shape[0]
    copies = []
    for block in range(0, r_ref.shape[0], 2):
        at = slice(block * LANES, (block + 2) * LANES)
        table = jnp.concatenate([r_ref[block], r_ref[block + 1]], axis=1)
        total = own_ref[:, at] + dot(by_slot, table)
        out_ref[:, at] = total.astype(bf16)[:out_ref.shape[0], :]
        if (block + 2) % span == 0:
            part = pl.ds((block + 2 - span) * LANES, span * LANES)
            copies += begin(sems.at[pl.ds(len(copies), 1)], (out_ref.at[:, part], out_hbm.at[:, part]))
    finish(copies)


def local(groups, peers, modes_in, blocks, block_cols, send_slot, recv_row, mix_cols, mix_coef):
    terms, all_stored, blk, _ = blocks.shape
    out_blocks, stored = block_cols.shape
    modes_dev, owned = modes_in.shape
    owned_blocks = owned // blk
    interface = send_slot.shape[0]
    slots = recv_row.shape[0]
    cap = slots // peers
    rows = groups * PAD
    lines = slots // QUARTERS
    Shape, dma = jax.ShapeDtypeStruct, pltpu.SemaphoreType.DMA

    def pin(x):
        return pltpu.with_memory_space_constraint(x, pltpu.HBM)

    def from_group(field, s):
        return lax.ppermute(field, "mode", [((to + s) % groups, to) for to in range(groups)])

    others = {s: from_group(modes_in, s) for s in (3, 2)}
    blocks = pin(blocks)
    where = pin(block_cols.T)
    mix_cols, mix_coef = pin(mix_cols.transpose(0, 2, 1)), pin(mix_coef.transpose(0, 2, 1))
    send, recv = pin(send_slot.reshape(1, interface)), pin(recv_row.reshape(1, slots))
    tables = [pltpu.VMEM(mix_cols.shape, i32), pltpu.VMEM(mix_coef.shape, f32)]
    if_blocks = (terms, (out_blocks - owned_blocks) * stored, blk, blk)
    own_scratch = pltpu.VMEM((terms, owned_blocks * stored, blk, blk), bf16)
    field_shape, mixer_shape = (owned_blocks, groups, PAD, blk), (rows, terms * rows)
    field_scratch = pltpu.VMEM(field_shape, bf16)
    block_flops = 2 * terms * stored * blk * blk
    wide, narrow = (owned_blocks, terms * rows, blk), (owned_blocks, terms * PAD, blk)

    where_scratch = pltpu.SMEM(where.shape, i32)
    own_shape, table_shape = (owned_blocks, rows, blk), (owned_blocks, slots, blk)

    g, g2, place, send, recv, own_field, where, stiff = call(
        functools.partial(setup_kernel, groups),
        [Shape(mixer_shape, bf16), Shape((terms * PAD, rows), bf16), Shape((slots, interface), bf16), Shape(send.shape, i32),
         Shape(recv.shape, i32), Shape((modes_dev, owned), bf16), Shape(where.shape, i32), Shape(if_blocks, bf16)],
        [mix_cols, mix_coef, send, recv, pin(modes_in), where, blocks], [HBM] * 7, [VMEM] * 8, flops=10**6,
        scratch=[*tables, dma((7,))],
    )
    others[1] = from_group(own_field, 1)
    packed, field = call(
        functools.partial(first_kernel, groups),
        [Shape((slots, rows), bf16), Shape(field_shape, bf16)],
        [own_field, others[1], others[2], others[3], g, place, where, stiff],
        [VMEM] * 8, [VMEM] * 2,
        flops=block_flops * (out_blocks - owned_blocks) * rows, scratch=[where_scratch, dma((1,))],
    )
    arrived = lax.all_to_all(packed.reshape(peers, cap, rows), "space", split_axis=0, concat_axis=0, tiled=True)
    steps = owned_blocks // 2
    own, r = call(
        functools.partial(between_kernel, steps), [Shape(own_shape, f32), Shape((if_blocks[1], slots, blk), bf16)],
        [field, g, recv, where, blocks], [VMEM] * 4 + [HBM], [VMEM] * 2,
        flops=block_flops * owned_blocks * rows,
        scratch=[pltpu.VMEM(wide, bf16), own_scratch, where_scratch, dma((1 + steps,))],
    )
    packed2, turned = call(
        second_kernel, [Shape((lines, QUARTERS * PAD), bf16), pltpu.HBM((rows, slots), bf16)],
        [own, arrived.reshape(slots, rows), r, g2, send, where, blocks], [VMEM] * 6 + [HBM], [VMEM, HBM],
        flops=2 * slots * rows * owned,
        scratch=[pltpu.VMEM((rows, slots), bf16), pltpu.VMEM((QUARTERS * PAD, QUARTERS * interface), bf16), pltpu.VMEM(if_blocks, bf16), where_scratch, dma((3,))],
    )
    arrived2 = lax.all_to_all(
        packed2.reshape(peers, cap // QUARTERS, QUARTERS * PAD), "space", split_axis=0, concat_axis=0, tiled=True
    )
    first_apply, own2, r2 = call(
        functools.partial(own_kernel, groups, steps),
        [pltpu.HBM((modes_dev, owned), bf16), Shape((PAD, owned), f32), Shape(table_shape, bf16)],
        [where, recv, g2, pin(turned), own, blocks], [VMEM, VMEM, VMEM, HBM, VMEM, HBM], [HBM, VMEM, VMEM],
        flops=block_flops * owned_blocks * PAD,
        scratch=[pltpu.VMEM((rows, slots), bf16), pltpu.VMEM((modes_dev, owned), bf16), field_scratch, pltpu.VMEM(narrow, bf16),
                 own_scratch, where_scratch, dma((3 + steps,))],
    )
    second_apply = call(
        last_kernel, [pltpu.HBM((modes_dev, owned), bf16)],
        [own2, arrived2.reshape(lines, QUARTERS * PAD), r2], [VMEM] * 3, [HBM], flops=2 * slots * PAD * owned,
        scratch=[pltpu.VMEM((slots, QUARTERS * PAD), f32), pltpu.VMEM((modes_dev, owned), bf16), dma((owned_blocks // 4,))],
    )[0]
    return (first_apply, second_apply)


def solution(mesh):
    in_specs = (
        P("mode", "space"),
        P(None, "space", None, None),
        P("space", None),
        P("space"),
        P("space"),
        P(),
        P(),
    )
    out_specs = (P("mode", "space"), P("mode", "space"))
    body = functools.partial(local, mesh.shape["mode"], mesh.shape["space"])
    return jax.shard_map(body, mesh=mesh, in_specs=in_specs, out_specs=out_specs, check_vma=False)
```
